32 devices in a mesh: spot: 8 (over z, y), gene: 4 (over x, core).
Axes of the slice: x: 2, y: 2, z: 4, core: 2. Of those that a mesh axis runs over, the one named last changes fastest.
Arguments:
- logits: float32 [2048, 16384], P(None, 'spot'), may hold values from -9 to 9
- centroid_expr: float32 [2048, 2048], P('spot', 'gene'), may hold values from -6 to 6
- spatial: float32 [16384, 2048], P('spot', 'gene'), may hold values from -6 to 6
- cluster_cells: int32 [2048], replicated, may hold values from 1 to 176, 45056 in all
- density: float32 [16384], P('spot'), may hold values from 0.2 to 5
- gene_order: int32 [2048], P('gene'), may hold values from 0 to 2047, as said below
Outputs:
- loss_terms: float32 [3], replicated
- gene_pred: float32 [16384, 2048], P('spot', 'gene')
- grad_logits: float32 [2048, 16384], P('gene', 'spot')
The draws below stay inside these ranges and needn't reach their ends.
Inputs may be any that keep to these rules, and one draw needn't show every extreme that they name: cluster_cells sum to 45056. gene_order is a permutation of the genes that maps each aligned block of 512 positions onto the same block of genes.
All inputs are finite; a program needn't handle non-finite values.
Results may differ from the reference program's by a relative error of at most 0.00021.
Values sent between devices are 32-bit elements; how exact they have to be, the bound alone decides.
No kernel may reach another device: no remote copies, remote signals or barrier semaphores. Data moves between devices by JAX's collectives and lax.ppermute only.
A program may use at most 192 MiB of HBM per device.

```python
import math
import jax
import jax.numpy as jnp
import numpy as np
from jax import lax

C = 2048
G = 2048
GB = 512
MOST_CELLS = 176
CELLS = 45056
SPOTS = 16384
NB = 4
GENE_DEV = 512
GB_DEV = 128
N_GENE = 4


def draw_gene_order(key, part):
    blocks = G // GENE_DEV
    keys = jax.random.split(jax.random.fold_in(key, 11), blocks)
    perms = jax.vmap(lambda k: jax.random.permutation(k, GENE_DEV))(keys)
    offsets = (jnp.arange(blocks, dtype=jnp.int32) * GENE_DEV)[:, None]
    return (perms.astype(jnp.int32) + offsets).reshape(-1).astype(jnp.int32)


def shard_levels(stream_key, shape, pieces, smallest, largest):
    def one(dim, parts):
        draws = jax.random.uniform(jax.random.fold_in(jax.random.fold_in(stream_key, 6), dim), (parts,), jnp.float32, smallest / len(pieces), largest / len(pieces))
        return jnp.repeat(jnp.exp(draws), shape[dim] // parts).reshape((-1,) + (1,) * (len(shape) - dim - 1))

    factor_of = one(*pieces[0])
    for cut in pieces[1:]:
        factor_of = factor_of * one(*cut)
    return factor_of


def length_profile(count, total, limit, skew):
    loads = [(1 << 20) // math.isqrt(standing ** skew) + 1 for standing in range(2, count + 1)]
    rest, counts = total - limit - (count - 1), [1] * (count - 1)
    while rest > 0:
        candidates = [i for i in range(count - 1) if counts[i] < limit]
        pool, remaining = sum([loads[i] for i in candidates]), rest
        for i in candidates:
            addition = min(limit - counts[i], max(1, remaining * loads[i] // pool), rest)
            counts[i] = counts[i] + addition
            rest = rest - addition
    return np.array([limit] + counts)


def ragged_sizes(rng, number_of, total, most, skew):
    if number_of == 2:
        one = jax.random.randint(rng, (), max(1, total - most), min(most, total - 1) + 1)
        return jnp.stack([one, total - one])
    sizes = jnp.asarray(length_profile(number_of, total, most, skew), jnp.int32)
    twos = (number_of - 1) // 2
    giver, receiver = sizes[1:1 + 2 * twos:2], sizes[2:2 + 2 * twos:2]
    room = jnp.minimum(giver - 1, most - receiver)
    shifted = jax.random.randint(jax.random.fold_in(rng, 1), (twos,), 0, 1 << 20) % (room + 1)
    sizes = sizes.at[1:1 + 2 * twos:2].set(giver - shifted).at[2:2 + 2 * twos:2].set(receiver + shifted)
    return sizes[jax.random.permutation(jax.random.fold_in(rng, 2), number_of)]


def scatter_about(rng, dims, spread, bound, cuts=(), kind=jnp.bfloat16):
    loudness = shard_levels(rng, dims, cuts, -0.22, 0.18) if cuts else 1.0
    result = jax.random.normal(rng, dims, jnp.float32) * spread * loudness
    return jnp.minimum(jnp.maximum(result, -bound), bound).astype(kind)


def setup_inputs(seed: int = 0) -> dict:
    seeds = jax.random.split(jax.random.key(seed), 7)
    return {
        "logits": scatter_about(seeds[0], (C, SPOTS), 1.5, 9.0, ((1, 8),), jnp.float32),
        "centroid_expr": scatter_about(seeds[1], (C, G), 1.0, 6.0, ((0, 8), (1, 4)), jnp.float32),
        "spatial": scatter_about(seeds[2], (SPOTS, G), 1.0, 6.0, ((0, 8), (1, 4)), jnp.float32),
        "cluster_cells": ragged_sizes(seeds[3], C, CELLS, MOST_CELLS, 2).astype(jnp.int32),
        "density": jnp.clip(jnp.exp(math.log(5.0) - 3.218876 * jax.random.uniform(seeds[4], (SPOTS,), jnp.float32) ** shard_levels(seeds[4], (SPOTS,), ((0, 8),), -0.2, 0.2)), 0.2, 5.0),
        "gene_order": draw_gene_order(jax.random.fold_in(seeds[6], 71), 0),
    }


EPS = 1e-06
HI = lax.Precision.HIGHEST

def forward(logits, centroid_expr, spatial, cluster_cells, density, gene_order):
    probs = jax.nn.softmax(logits, axis=0)
    sorted_expr = centroid_expr[:, gene_order].reshape(C, N_GENE, NB, GB_DEV)
    sorted_spat = spatial[:, gene_order].reshape(SPOTS, N_GENE, NB, GB_DEV)
    preds = []
    gene_total = jnp.float32(0.0)
    spot_total = jnp.float32(0.0)
    for batch in range(NB):
        block = sorted_expr[:, :, batch, :].reshape(C, GB)
        target = sorted_spat[:, :, batch, :].reshape(SPOTS, GB)
        pred = jnp.dot(probs.T, block, precision=HI, preferred_element_type=jnp.float32)
        preds.append(pred)
        inner = lax.optimization_barrier(jnp.sum(pred * target, axis=0))
        upper = lax.optimization_barrier(jnp.sum(pred * pred, axis=0)) + EPS
        vnorm = lax.optimization_barrier(jnp.sum(target * target, axis=0)) + EPS
        gene_total = gene_total + jnp.sum(inner * lax.rsqrt(upper) * lax.rsqrt(vnorm))
        sinner = lax.optimization_barrier(jnp.sum(pred * target, axis=1))
        supper = lax.optimization_barrier(jnp.sum(pred * pred, axis=1)) + EPS
        svnorm = lax.optimization_barrier(jnp.sum(target * target, axis=1)) + EPS
        spot_total = spot_total + jnp.sum(sinner * lax.rsqrt(supper) * lax.rsqrt(svnorm))
    weights = cluster_cells.astype(logits.dtype)
    weights = weights / jnp.sum(weights)
    raw = jnp.dot(weights, probs, precision=HI, preferred_element_type=jnp.float32)
    total_raw = jnp.sum(raw)
    dens_norm = density / jnp.sum(density)
    diverge = jnp.sum(dens_norm * (jnp.log(dens_norm) - jnp.log(raw / total_raw)))
    terms = jnp.stack([-gene_total / G, -spot_total / (NB * SPOTS), diverge])
    stacked = jnp.stack(preds, 0).reshape(NB, SPOTS, N_GENE, GB_DEV)
    reordered = jnp.transpose(stacked, (1, 2, 0, 3)).reshape(SPOTS, G)
    gene_pred = jnp.zeros((SPOTS, G), logits.dtype).at[:, gene_order].set(reordered)
    return (jnp.sum(terms), (terms, gene_pred))

def reference(logits, centroid_expr, spatial, cluster_cells, density, gene_order):

    def wrapped(values):
        return forward(values, centroid_expr, spatial, cluster_cells, density, gene_order)
    total, pullback, extras = jax.vjp(wrapped, logits, has_aux=True)
    grad_logits, = pullback(jnp.ones_like(total) * (SPOTS * C))
    return (extras[0], extras[1], grad_logits)
```

```python
import functools
import jax
import jax.numpy as jnp
from jax import lax
from jax.experimental import pallas as pl
from jax.experimental.pallas import tpu as pltpu
from jax.sharding import PartitionSpec as P

NB = 4
EPS = 1e-06
BF = jnp.bfloat16
F32 = jnp.float32
KC = 256
NT = (((1,), (1,)), ((), ()))
TN = (((0,), (0,)), ((), ()))
VMEM_LIMIT = 60 << 20


def split(value):
    high = value.astype(BF)
    return high, (value - high.astype(F32)).astype(BF)


def store_left(ref, rows, start, value):
    high, low = split(value)
    width = value.shape[1]
    ref[rows, start : start + width] = high
    ref[rows, start + width : start + 2 * width] = high
    ref[rows, start + 2 * width : start + 3 * width] = low


def store_right(ref, start, value):
    high, low = split(value)
    depth = value.shape[0]
    ref[start : start + depth] = high
    ref[start + depth : start + 2 * depth] = low
    ref[start + 2 * depth : start + 3 * depth] = high


def params():
    return pltpu.CompilerParams(dimension_semantics=("arbitrary",), vmem_limit_bytes=VMEM_LIMIT)


def turn_kernel(order_ref, x_ref, out_ref):
    high, low = split(x_ref[...])
    pick = order_ref[...]
    out_ref[...] = lax.dot_general(pick, high, NT, preferred_element_type=F32) + lax.dot_general(
        pick, low, NT, preferred_element_type=F32
    )


def turn(pick, x, tile=256):
    spots, genes = x.shape
    return pl.pallas_call(
        turn_kernel,
        out_shape=jax.ShapeDtypeStruct((genes, spots), F32),
        grid=(spots // tile,),
        in_specs=[
            pl.BlockSpec((genes, genes), lambda i: (0, 0)),
            pl.BlockSpec((tile, genes), lambda i: (i, 0)),
        ],
        out_specs=pl.BlockSpec((genes, tile), lambda i: (0, i)),
        compiler_params=params(),
        cost_estimate=pl.CostEstimate(
            flops=4 * genes * genes * spots, bytes_accessed=8 * genes * spots, transcendentals=0
        ),
        name="turn",
    )(pick, x)


def products(ah, bh, l_refs, first_sum=None, w_refs=None):
    total = weighted = None
    at = 0
    for number, l_ref in enumerate(l_refs):
        for part in range(l_ref.shape[0] // KC):
            rows = slice(part * KC, part * KC + KC)
            value = jnp.exp(l_ref[rows, :])
            store_right(bh, at, value)
            at += 3 * KC
            if w_refs is not None:
                one = jnp.sum(value, axis=0, keepdims=True)
                two = jnp.sum(value * w_refs[number][rows, :], axis=0, keepdims=True)
                total = one if total is None else total + one
                weighted = two if weighted is None else weighted + two
    return jnp.dot(ah[...], bh[...], preferred_element_type=F32), total, weighted


def load_left(ah, s_refs):
    at = 0
    for s_ref in s_refs:
        for part in range(s_ref.shape[1] // KC):
            store_left(ah, slice(None), at, s_ref[:, part * KC : part * KC + KC])
            at += 3 * KC


def own_kernel(count, cents, *refs):
    refs = refs[1:]
    s_refs, l_refs, w_refs = refs[:count], refs[count : 2 * count], refs[2 * count : 3 * count]
    x_ref, d_ref, pick_ref, pred_ref, out_ref, info_ref, ah, bh, sums, scal = refs[3 * count :]
    step = pl.program_id(0)
    tile = x_ref.shape[1]
    genes = x_ref.shape[0]
    width = genes // NB

    @pl.when(step == 0)
    def _():
        load_left(ah, s_refs)
        sums[...] = jnp.zeros_like(sums)
        scal[...] = jnp.zeros_like(scal)
        info_ref[...] = jnp.zeros_like(info_ref)

    value, total, weighted = products(ah, bh, l_refs, w_refs=w_refs)
    inv = 1.0 / total
    pred = value * inv
    pred_ref[...] = pred
    high, low = split(pred)
    pick = pick_ref[...]
    out_ref[...] = lax.dot_general(high, pick, TN, preferred_element_type=F32) + lax.dot_general(
        low, pick, TN, preferred_element_type=F32
    )
    x = x_ref[...]
    rows = []
    for number, product in enumerate((pred * x, pred * pred, x * x)):
        for batch in range(NB):
            rows.append(
                jnp.sum(product[batch * width : (batch + 1) * width], axis=0, keepdims=True)
            )
        lanes = product[:, :128]
        for group in range(1, tile // 128):
            lanes = lanes + product[:, group * 128 : group * 128 + 128]
        sums[number] += lanes
    raw = weighted * inv
    dens = d_ref[...]
    at = pl.ds(pl.multiple_of(step * tile, 128), tile)
    info_ref[0 : 3 * NB, at] = jnp.concatenate(rows, axis=0)
    info_ref[13:14, at] = inv
    info_ref[14:15, at] = raw
    scal[0:1] += dens
    scal[1:2] += raw
    scal[2:3] += dens * (jnp.log(dens) - jnp.log(raw * cents))

    @pl.when(step == pl.num_programs(0) - 1)
    def _():
        for number in range(3):
            info_ref[12:13, number * genes : (number + 1) * genes] = jnp.sum(
                sums[number].T, axis=0, keepdims=True
            )
        for number in range(3):
            info_ref[15:16, number * 128 : number * 128 + 128] = jnp.broadcast_to(
                jnp.sum(scal[number : number + 1], axis=1, keepdims=True), (1, 128)
            )


def own_part(blocks, index, logits, weights, x_own, density, pick, tile=256):
    cents, spots = logits.shape
    genes, deep = blocks[0].shape
    count = len(blocks)
    whole = lambda i, ix: (0, 0)
    specs = [pl.BlockSpec((genes, deep), whole, pipeline_mode=pl.Buffered(1)) for _ in blocks]
    specs += [
        pl.BlockSpec((deep, tile), functools.partial(lambda b, i, ix: (ix[b], i), b))
        for b in range(count)
    ]
    specs += [
        pl.BlockSpec((deep, 1), functools.partial(lambda b, i, ix: (ix[b], 0), b))
        for b in range(count)
    ]
    specs += [
        pl.BlockSpec((genes, tile), lambda i, ix: (0, i)),
        pl.BlockSpec((1, tile), lambda i, ix: (0, i)),
        pl.BlockSpec((genes, genes), whole),
    ]
    return pl.pallas_call(
        functools.partial(own_kernel, count, float(cents)),
        out_shape=(
            jax.ShapeDtypeStruct((genes, spots), F32),
            jax.ShapeDtypeStruct((spots, genes), F32),
            jax.ShapeDtypeStruct((16, spots), F32),
        ),
        grid_spec=pltpu.PrefetchScalarGridSpec(
            num_scalar_prefetch=1,
            grid=(spots // tile,),
            in_specs=specs,
            out_specs=(
                pl.BlockSpec((genes, tile), lambda i, ix: (0, i)),
                pl.BlockSpec((tile, genes), lambda i, ix: (i, 0)),
                pl.BlockSpec((16, spots), whole),
            ),
            scratch_shapes=[
                pltpu.VMEM((genes, 3 * cents), BF),
                pltpu.VMEM((3 * cents, tile), BF),
                pltpu.VMEM((3, genes, 128), F32),
                pltpu.VMEM((8, tile), F32),
            ],
        ),
        compiler_params=params(),
        cost_estimate=pl.CostEstimate(
            flops=6 * genes * cents * spots, bytes_accessed=4 * cents * spots, transcendentals=0
        ),
        name="own_part",
    )(index, *blocks, *([logits] * count), *([weights] * count), x_own, density, pick)


def other_kernel(count, first, last, *refs):
    refs = refs[1:]
    s_refs, l_refs = refs[:count], refs[count : 2 * count]
    refs = refs[2 * count :]
    if not first:
        acc_ref, refs = refs[0], refs[1:]
    if last:
        info_ref, refs = refs[0], refs[1:]
    out_ref, ah, bh = refs

    @pl.when(pl.program_id(0) == 0)
    def _():
        load_left(ah, s_refs)

    value, _, _ = products(ah, bh, l_refs)
    if not first:
        value = value + acc_ref[...]
    if last:
        value = value * info_ref[5:6, :]
    out_ref[...] = value


def other_part(blocks, index, logits, acc, info, tile=256):
    cents, spots = logits.shape
    genes, deep = blocks[0].shape
    count = len(blocks)
    first, last = acc is None, info is not None
    whole = lambda i, ix: (0, 0)
    specs = [pl.BlockSpec((genes, deep), whole, pipeline_mode=pl.Buffered(1)) for _ in blocks]
    specs += [
        pl.BlockSpec((deep, tile), functools.partial(lambda b, i, ix: (ix[b], i), b))
        for b in range(count)
    ]
    args = [index, *blocks, *([logits] * count)]
    alias = {}
    if not first:
        alias = {len(args): 0}
        specs.append(pl.BlockSpec((genes, tile), lambda i, ix: (0, i)))
        args.append(acc)
    if last:
        specs.append(pl.BlockSpec((8, tile), lambda i, ix: (1, i)))
        args.append(info)
    return pl.pallas_call(
        functools.partial(other_kernel, count, first, last),
        out_shape=jax.ShapeDtypeStruct((genes, spots), F32),
        grid_spec=pltpu.PrefetchScalarGridSpec(
            num_scalar_prefetch=1,
            grid=(spots // tile,),
            in_specs=specs,
            out_specs=pl.BlockSpec((genes, tile), lambda i, ix: (0, i)),
            scratch_shapes=[
                pltpu.VMEM((genes, 3 * deep * count), BF),
                pltpu.VMEM((3 * deep * count, tile), BF),
            ],
        ),
        input_output_aliases=alias,
        compiler_params=params(),
        cost_estimate=pl.CostEstimate(
            flops=6 * genes * deep * count * spots,
            bytes_accessed=4 * deep * count * spots + 8 * genes * spots,
            transcendentals=0,
        ),
        name="other_part",
    )(*args)


def cosine(inner, left, right):
    left = left + EPS
    inv = lax.rsqrt(left) * lax.rsqrt(right + EPS)
    cos = inner * inv
    return cos, inv, cos / left


def pack_kernel(spots_ref, mine_ref, theirs_ref, out_ref):
    genes = out_ref.shape[1] // 2
    totals = spots_ref[...]
    cos, _, _ = cosine(totals[0:NB], totals[NB : 2 * NB], totals[2 * NB : 3 * NB])
    out_ref[...] = jnp.zeros_like(out_ref)
    for number in range(3):
        at = slice(number * genes, (number + 1) * genes)
        out_ref[number : number + 1, 0:genes] = mine_ref[12:13, at]
        out_ref[number : number + 1, genes : 2 * genes] = theirs_ref[12:13, at]
        out_ref[3 + number : 4 + number, 0:128] = mine_ref[15:16, number * 128 : number * 128 + 128]
    out_ref[6:7, 0:128] = jnp.broadcast_to(
        jnp.sum(jnp.sum(cos, axis=0, keepdims=True), axis=1, keepdims=True), (1, 128)
    )


def pack(spot_totals, mine, theirs, genes):
    return pl.pallas_call(
        pack_kernel,
        out_shape=jax.ShapeDtypeStruct((8, 2 * genes), F32),
        compiler_params=pltpu.CompilerParams(vmem_limit_bytes=VMEM_LIMIT),
        name="pack",
    )(spot_totals, mine, theirs)


def rows_left(ah, buffer, sem, which, refs, of_part, rows):
    genes, deep = refs[0][0].shape
    for part in range(2):
        for piece in range(rows // KC):
            at = slice(piece * KC, piece * KC + KC)
            block, offset = of_part(which, piece)
            if len(refs[part]) == 1:
                src = refs[part][0].at[:, pl.ds(pl.multiple_of(offset, KC), KC)]
                pltpu.make_async_copy(src, buffer, sem).start()
            else:
                for number, ref in enumerate(refs[part]):

                    @pl.when(block == number)
                    def _(ref=ref):
                        pltpu.make_async_copy(ref, buffer, sem).start()

            pltpu.make_async_copy(refs[part][0].at[:, 0:KC], buffer, sem).wait()
            high, low = split(buffer[...].T)
            width = 2 * genes
            start = part * genes
            ah[at, start : start + genes] = high
            ah[at, width + start : width + start + genes] = high
            ah[at, 2 * width + start : 2 * width + start + genes] = low


def back_kernel(count, final, sizes, *refs):
    batches_scale, gene_scale, scale, loss_scale, of_part = sizes
    where = refs[0]
    refs = refs[1:]
    parts = (refs[:count], refs[count : 2 * count])
    refs = refs[2 * count :]
    pred_refs, x_refs = refs[0:2], refs[2:4]
    totals_ref, spot_ref, info_ref, dens_ref = refs[4:8]
    refs = refs[8:]
    if final:
        sent_ref, got_ref, logit_ref, w_ref, out_ref, loss_ref, ah, bh, coef, buffer, sem = refs
    else:
        out_ref, ah, bh, coef, buffer, sem = refs
    genes, tile = pred_refs[0].shape
    rows = ah.shape[0]
    width = genes // NB

    gene_cos, inv_gene, over_gene = cosine(
        totals_ref[0:1, :], totals_ref[1:2, :], totals_ref[2:3, :]
    )

    @pl.when(pl.program_id(0) == 0)
    def _():
        coef[0] = jnp.broadcast_to(-gene_scale * inv_gene, (128, 2 * genes)).T
        coef[1] = jnp.broadcast_to(gene_scale * over_gene, (128, 2 * genes)).T
        rows_left(ah, buffer, sem, where, parts, of_part, rows)

    spot = spot_ref[...]
    _, inv_spot, over_spot = cosine(spot[0:NB], spot[NB : 2 * NB], spot[2 * NB : 3 * NB])
    column = jnp.zeros((1, tile), F32)
    for part in range(2):
        for batch in range(NB):
            at = slice(batch * width, (batch + 1) * width)
            here = slice(part * genes + batch * width, part * genes + (batch + 1) * width)
            x_by = jnp.concatenate([coef[0, here]] * (tile // 128), axis=1) - (
                batches_scale * inv_spot[batch : batch + 1]
            )
            p_by = jnp.concatenate([coef[1, here]] * (tile // 128), axis=1) + (
                batches_scale * over_spot[batch : batch + 1]
            )
            pred = pred_refs[part][at, :]
            grad = x_refs[part][at, :] * x_by + pred * p_by
            high, low = split(grad)
            bh[here] = high
            bh[2 * genes + here.start : 2 * genes + here.stop] = low
            bh[4 * genes + here.start : 4 * genes + here.stop] = high
            if not final:
                column = column + jnp.sum(pred * grad, axis=0, keepdims=True)
    value = jnp.dot(ah[...], bh[...], preferred_element_type=F32)
    if not final:
        out_ref[0:rows] = value
        out_ref[rows : rows + 1] = column
        out_ref[rows + 1 : rows + 2] = jnp.broadcast_to(
            jnp.sum(gene_cos, axis=1, keepdims=True), (1, tile)
        )
        out_ref[rows + 2 : rows + 8] = jnp.zeros((6, tile), F32)
        return
    raw = info_ref[6:7, :]
    dens = totals_ref[3:4, 0:1]
    mass = totals_ref[4:5, 0:1]
    grad_raw = scale * (1.0 / mass - dens_ref[...] / (dens * raw))
    column = sent_ref[0:1, :] + got_ref[rows : rows + 1, :] + raw * grad_raw
    value = value + got_ref[0:rows, :] + w_ref[...] * grad_raw
    out_ref[...] = jnp.exp(logit_ref[...]) * info_ref[5:6, :] * (value - column)

    @pl.when(pl.program_id(0) == 0)
    def _():
        gene_scale_loss, spot_scale_loss, per_cent, spots_all = loss_scale
        gene = (sent_ref[1:2, 0:128] + got_ref[rows + 1 : rows + 2, 0:128]) * gene_scale_loss
        cos = totals_ref[6:7, 0:128] * spot_scale_loss
        kl = (
            totals_ref[5:6, 0:128] / totals_ref[3:4, 0:128]
            + jnp.log(totals_ref[4:5, 0:128] * (per_cent / spots_all))
            - jnp.log(totals_ref[3:4, 0:128] * (1.0 / spots_all))
        )
        loss_ref[...] = jnp.concatenate([gene, cos, kl, jnp.zeros((5, 128), F32)], axis=0)


def back(
    which, own, other, preds, xs, totals, spot, info, density, consts, of_part, rows, final, tile=256
):
    genes, spots = preds[0].shape
    count = len(own)
    by_tile = lambda height: pl.BlockSpec((height, tile), lambda i, ix: (0, i))
    specs = [pl.BlockSpec(memory_space=pl.ANY)] * (2 * count)
    specs += [by_tile(genes)] * 4
    specs += [
        pl.BlockSpec((8, 2 * genes), lambda i, ix: (0, 0)),
        by_tile(16),
        pl.BlockSpec((8, tile), lambda i, ix: (1, i)),
        by_tile(1),
    ]
    args = [which, *own, *other, *preds, *xs, totals, spot, info, density]
    if final is None:
        shapes = jax.ShapeDtypeStruct((rows + 8, spots), F32)
        outs = by_tile(rows + 8)
    else:
        sent, got, logits, weights = final
        args += [sent, got, logits, weights]
        specs += [
            pl.BlockSpec((8, tile), lambda i, ix: (rows // 8, i)),
            by_tile(rows + 8),
            pl.BlockSpec((rows, tile), lambda i, ix: (ix[0], i)),
            pl.BlockSpec((rows, 1), lambda i, ix: (ix[0], 0)),
        ]
        shapes = (
            jax.ShapeDtypeStruct((rows, spots), F32),
            jax.ShapeDtypeStruct((8, 128), F32),
        )
        outs = (by_tile(rows), pl.BlockSpec((8, 128), lambda i, ix: (0, 0)))
    return pl.pallas_call(
        functools.partial(back_kernel, count, final is not None, (*consts, of_part)),
        out_shape=shapes,
        grid_spec=pltpu.PrefetchScalarGridSpec(
            num_scalar_prefetch=1,
            grid=(spots // tile,),
            in_specs=specs,
            out_specs=outs,
            scratch_shapes=[
                pltpu.VMEM((rows, 6 * genes), BF),
                pltpu.VMEM((6 * genes, tile), BF),
                pltpu.VMEM((2, 2 * genes, 128), F32),
                pltpu.VMEM((genes, KC), F32),
                pltpu.SemaphoreType.DMA,
            ],
        ),
        compiler_params=params(),
        cost_estimate=pl.CostEstimate(
            flops=12 * genes * rows * spots, bytes_accessed=24 * genes * spots, transcendentals=0
        ),
        name="back_sum" if final is None else "back_end",
    )(*args)


def swap(value, axis, bit):
    return lax.ppermute(value, axis, [(i, i ^ bit) for i in range(lax.axis_size(axis))])


def local(logits, centroid_expr, spatial, cluster_cells, density, gene_order):
    n_spot = lax.axis_size("spot")
    n_gene = lax.axis_size("gene")
    me = lax.axis_index("spot")
    col = lax.axis_index("gene")
    cents, spots = logits.shape
    genes = spatial.shape[1]
    genes_all = genes * n_gene
    spots_all = spots * n_spot
    rows = cents // n_gene
    scale = float(spots_all * cents)
    consts = (
        scale / (NB * spots_all),
        scale / genes_all,
        scale,
        (-1.0 / genes_all, -1.0 / (NB * spots_all), float(cents), float(spots_all)),
    )
    ring = n_spot == 8 and cents // n_spot == KC

    order = (gene_order - col * genes).reshape(genes, 1)
    lanes = lax.broadcasted_iota(jnp.int32, (genes, genes), 1)
    pick = order == lanes
    mine = lax.dot_general(
        pick.astype(F32), centroid_expr, NT, precision=lax.Precision.HIGHEST, preferred_element_type=F32
    )
    pick = pick.astype(BF)
    theirs = swap(mine, "gene", 2)
    order_other = swap(gene_order, "gene", 2) - (col ^ 2) * genes
    pick_other = (order_other.reshape(genes, 1) == lanes).astype(BF)
    cut = spots * 3 // 4
    x_other = [swap(spatial[:cut], "gene", 2), swap(spatial[cut:], "gene", 2)]

    if ring:
        def gather(block):
            got = [block] + [swap(block, "spot", bit) for bit in (2, 4, 6)]
            out = []
            for one in got:
                out += [one, swap(one, "spot", 1)]
            return out

        own = gather(mine)
        other = gather(theirs)
        index = me ^ jnp.arange(n_spot, dtype=jnp.int32)
        of_part = lambda where, piece: ((where[0] * (rows // KC) + piece) ^ where[1], 0)
        early = 6
    else:
        own = [lax.all_gather(mine, "spot", axis=1, tiled=True)]
        other = [lax.all_gather(theirs, "spot", axis=1, tiled=True)]
        index = jnp.zeros((1,), jnp.int32)
        of_part = lambda where, piece: (0, where[0] * rows + piece * KC)
        early = 0

    weights = cluster_cells.astype(F32)
    weights = (weights / jnp.sum(weights)).reshape(cents, 1)
    dens_row = density.reshape(1, spots)
    x_own = turn(pick, spatial)
    pred_own, predicted, info = own_part(own, index, logits, weights, x_own, dens_row, pick)

    info_x = swap(info, "gene", 2)
    half = info + info_x
    spot = half + swap(half, "gene", 1)
    totals = pack(spot, info, info_x, genes)
    if ring:
        for bit in (1, 2, 4):
            totals = totals + swap(totals, "spot", bit)
    else:
        totals = lax.psum(totals, "spot")

    acc = None
    if early:
        acc = other_part(other[:early], index[:early], logits, None, None)
    pred_other = other_part(other[early:], index[early:], logits, acc, info)
    x_turned = jnp.concatenate([turn(pick_other, one) for one in x_other], axis=1)

    partner = jnp.stack([col ^ 1, me]).astype(jnp.int32)
    self_at = jnp.stack([col, me]).astype(jnp.int32)
    common = (own, other, (pred_own, pred_other), (x_own, x_turned), totals, spot, info, dens_row, consts, of_part, rows)
    sent = back(partner, *common, None)
    got = swap(sent, "gene", 1)
    grad_logits, loss = back(self_at, *common, (sent, got, logits, weights))
    return loss[0:3, 0], predicted, grad_logits


def solution(mesh):
    return jax.shard_map(
        local,
        mesh=mesh,
        in_specs=(P(None, "spot"), P("spot", "gene"), P("spot", "gene"), P(), P("spot"), P("gene")),
        out_specs=(P(), P("spot", "gene"), P("gene", "spot")),
        check_vma=False,
    )
```

```python
import functools
import jax
import jax.numpy as jnp
from jax import lax
from jax.experimental import pallas as pl
from jax.experimental.pallas import tpu as pltpu
from jax.sharding import PartitionSpec as P

NB = 4
XS = 2
EPS = 1e-06
BF = jnp.bfloat16
F32 = jnp.float32
KC = 256
NT = (((1,), (1,)), ((), ()))
TN = (((0,), (0,)), ((), ()))
VMEM_LIMIT = 67043328
CHEAP = pl.CostEstimate(flops=1000, bytes_accessed=1000, transcendentals=0)


def split(value):
    high = value.astype(BF)
    return high, (value - high.astype(F32)).astype(BF)


def dot(left, right, dims=(((1,), (0,)), ((), ()))):
    return lax.dot_general(left, right, dims, preferred_element_type=F32)


def call(kernel, name, where, args, specs, out_shape, out_specs, grid, scratch=(), alias=None):
    return pl.pallas_call(
        kernel,
        out_shape=out_shape,
        grid_spec=pltpu.PrefetchScalarGridSpec(
            num_scalar_prefetch=1,
            grid=grid,
            in_specs=specs,
            out_specs=out_specs,
            scratch_shapes=list(scratch),
        ),
        input_output_aliases=alias or {},
        compiler_params=pltpu.CompilerParams(
            dimension_semantics=("arbitrary",), vmem_limit_bytes=VMEM_LIMIT
        ),
        cost_estimate=CHEAP,
        name=name,
    )(where, *args)


def fixed(shape):
    return pl.BlockSpec(shape, lambda i, ix: (0,) * len(shape), pipeline_mode=pl.Buffered(1))


def by_tile(height, tile, row=0, start=0):
    return pl.BlockSpec((height, tile), lambda i, ix: (row, i + start))


def exp_kernel(cents, where, l_ref, w_ref, d_ref, high_ref, low_ref, info_ref, scal):
    step = pl.program_id(0)
    tile = l_ref.shape[1]

    @pl.when(step == 0)
    def _():
        scal[...] = jnp.zeros_like(scal)

    total = weighted = jnp.zeros((1, tile), F32)
    for part in range(l_ref.shape[0] // KC):
        rows = slice(part * KC, part * KC + KC)
        value = jnp.exp(l_ref[rows, :])
        high, low = split(value)
        high_ref[rows, :] = high
        low_ref[rows, :] = low
        total = total + jnp.sum(value, axis=0, keepdims=True)
        weighted = weighted + jnp.sum(value * w_ref[rows, :], axis=0, keepdims=True)
    inv = 1.0 / total
    raw = weighted * inv
    dens = d_ref[...]
    scal[0:1] += dens
    scal[1:2] += raw
    scal[2:3] += dens * (jnp.log(dens) - jnp.log(raw * cents))
    sums = jnp.broadcast_to(jnp.sum(scal[...], axis=1, keepdims=True), (8, tile))
    info_ref[0:1, :] = inv
    info_ref[1:2, :] = raw
    info_ref[2:8, :] = sums[0:6]


def exp_parts(where, logits, weights, density, tile):
    cents, spots = logits.shape
    return call(
        functools.partial(exp_kernel, float(cents)),
        "exp_parts",
        where,
        [logits, weights, density],
        [by_tile(cents, tile), fixed((cents, 1)), by_tile(1, tile)],
        (
            jax.ShapeDtypeStruct((cents, spots), BF),
            jax.ShapeDtypeStruct((cents, spots), BF),
            jax.ShapeDtypeStruct((8, spots), F32),
        ),
        (by_tile(cents, tile), by_tile(cents, tile), by_tile(8, tile)),
        (spots // tile,),
        [pltpu.VMEM((8, tile), F32)],
    )


def turn_kernel(where, pick_ref, x_ref, *out_refs):
    high, low = split(x_ref[...])
    pick = pick_ref[...]
    value = dot(pick, high, NT) + dot(pick, low, NT)
    width = out_refs[0].shape[0]
    for batch, out_ref in enumerate(out_refs):
        out_ref[...] = value[batch * width : (batch + 1) * width]


def turn(where, pick, x, tile):
    spots, genes = x.shape
    width = genes // XS
    return call(
        turn_kernel,
        "turn",
        where,
        [pick, x],
        [fixed((genes, genes)), pl.BlockSpec((tile, genes), lambda i, ix: (i, 0))],
        (jax.ShapeDtypeStruct((width, spots), F32),) * XS,
        (by_tile(width, tile),) * XS,
        (spots // tile,),
    )


def of_batch(refs, batch, width):
    each = NB // XS
    start = batch % each * width
    return refs[batch // each][start : start + width, :]


def load_left(groups, high, low):
    at = 0
    for group in groups:
        value = group[0][...]
        for ref in group[1:]:
            value = value + ref[...]
        wide = value.shape[1]
        high[:, at : at + wide], low[:, at : at + wide] = split(value)
        at += wide


def flat(blocks):
    sizes = [len(block) if isinstance(block, tuple) else 1 for block in blocks]
    arrays = [one for block in blocks for one in (block if isinstance(block, tuple) else (block,))]
    return sizes, arrays


def grouped(sizes, refs):
    out, at = [], 0
    for size in sizes:
        out.append(refs[at : at + size])
        at += size
    return out


def product(high, low, e_high, e_low):
    right = jnp.concatenate([ref[...] for ref in e_high], axis=0)
    value = dot(high[...], right) + dot(low[...], right)
    return value + dot(high[...], jnp.concatenate([ref[...] for ref in e_low], axis=0))


def pred_kernel(sizes, first, last, stats, where, *refs):
    count = len(sizes)
    s_refs, refs = grouped(sizes, refs), refs[sum(sizes) :]
    h_refs, l_refs = refs[:count], refs[count : 2 * count]
    refs = refs[2 * count :]
    if not first:
        acc_ref, refs = refs[0], refs[1:]
    if last:
        zinfo_ref, refs = refs[0], refs[1:]
    if stats:
        x_refs, (out_ref, info_ref, high, low, sums) = refs[:XS], refs[XS:]
    else:
        out_ref, high, low = refs
    step = pl.program_id(0)
    genes, tile = out_ref.shape
    width = genes // NB

    @pl.when(step == 0)
    def _():
        load_left(s_refs, high, low)
        if stats:
            sums[...] = jnp.zeros_like(sums)
            info_ref[...] = jnp.zeros_like(info_ref)

    value = product(high, low, h_refs, l_refs)
    if not first:
        value = value + acc_ref[...]
    if last:
        value = value * zinfo_ref[0:1, :]
    out_ref[...] = value
    if not stats:
        return
    rows = [[], [], []]
    for batch in range(NB):
        at = slice(batch * width, (batch + 1) * width)
        pred, x = value[at], of_batch(x_refs, batch, width)
        for number, term in enumerate((pred * x, pred * pred, x * x)):
            rows[number].append(jnp.sum(term, axis=0, keepdims=True))
            lanes = term[:, :128]
            for group in range(1, tile // 128):
                lanes = lanes + term[:, group * 128 : group * 128 + 128]
            sums[number, at] += lanes
    info_ref[0 : 3 * NB, pl.ds(pl.multiple_of(step * tile, 128), tile)] = jnp.concatenate(
        rows[0] + rows[1] + rows[2], axis=0
    )

    @pl.when(step == pl.num_programs(0) - 1)
    def _():
        for number in range(3):
            info_ref[12:13, number * genes : (number + 1) * genes] = jnp.sum(
                sums[number].T, axis=0, keepdims=True
            )


def pred_part(where, keys, blocks, e_high, e_low, acc, zinfo, x, tile, name):
    cents, spots = e_high.shape
    sizes, blocks = flat(blocks)
    genes, deep = blocks[0].shape
    count = len(sizes)
    first, last, stats = acc is None, zinfo is not None, x is not None
    rows = [
        pl.BlockSpec((deep, tile), functools.partial(lambda key, i, ix: (key(ix), i), key))
        for key in keys
    ]
    specs = [fixed((genes, deep)) for _ in blocks] + rows + rows
    args = [*blocks, *([e_high] * count), *([e_low] * count)]
    alias = {}
    if not first:
        alias = {len(args) + 1: 0}
        specs.append(by_tile(genes, tile))
        args.append(acc)
    if last:
        specs.append(by_tile(8, tile))
        args.append(zinfo)
    shapes = jax.ShapeDtypeStruct((genes, spots), F32)
    outs = by_tile(genes, tile)
    scratch = [pltpu.VMEM((genes, deep * count), BF)] * 2
    if stats:
        specs += [by_tile(genes // XS, tile)] * XS
        args += x
        shapes = (shapes, jax.ShapeDtypeStruct((16, spots), F32))
        outs = (outs, fixed_out((16, spots)))
        scratch.append(pltpu.VMEM((3, genes, 128), F32))
    return call(
        functools.partial(pred_kernel, sizes, first, last, stats),
        name,
        where,
        args,
        specs,
        shapes,
        outs,
        (spots // tile,),
        scratch,
        alias,
    )


def fixed_out(shape):
    return pl.BlockSpec(shape, lambda i, ix: (0,) * len(shape))


def emit_kernel(where, pred_ref, pick_ref, out_ref):
    high, low = split(pred_ref[...].T)
    pick = pick_ref[...]
    out_ref[...] = dot(high, pick) + dot(low, pick)


def emit(where, pred, pick, tile):
    genes, spots = pred.shape
    return call(
        emit_kernel,
        "emit",
        where,
        [pred, pick],
        [by_tile(genes, tile), fixed((genes, genes))],
        jax.ShapeDtypeStruct((spots, genes), F32),
        pl.BlockSpec((tile, genes), lambda i, ix: (i, 0)),
        (spots // tile,),
    )


def cosine(inner, left, right):
    left = left + EPS
    inv = lax.rsqrt(left) * lax.rsqrt(right + EPS)
    cos = inner * inv
    return cos, inv, cos / left


def pack_kernel(half_ref, core_ref, mine_ref, theirs_ref, z_ref, out_ref, spot_ref):
    genes = out_ref.shape[1] // 2
    totals = half_ref[...] + core_ref[...]
    spot_ref[...] = totals
    cos, _, _ = cosine(totals[0:NB], totals[NB : 2 * NB], totals[2 * NB : 3 * NB])
    out_ref[...] = jnp.zeros_like(out_ref)
    spots = z_ref.shape[1]
    for number in range(3):
        at = slice(number * genes, (number + 1) * genes)
        out_ref[number : number + 1, 0:genes] = mine_ref[12:13, at]
        out_ref[number : number + 1, genes : 2 * genes] = theirs_ref[12:13, at]
        out_ref[3 + number : 4 + number, 0:128] = z_ref[2 + number : 3 + number, spots - 128 :]
    out_ref[6:7, 0:128] = jnp.broadcast_to(
        jnp.sum(jnp.sum(cos, axis=0, keepdims=True), axis=1, keepdims=True), (1, 128)
    )


def pack(half, core, mine, theirs, zinfo, genes):
    return pl.pallas_call(
        pack_kernel,
        out_shape=(
            jax.ShapeDtypeStruct((8, 2 * genes), F32),
            jax.ShapeDtypeStruct(half.shape, F32),
        ),
        compiler_params=pltpu.CompilerParams(vmem_limit_bytes=VMEM_LIMIT),
        cost_estimate=CHEAP,
        name="pack",
    )(half, core, mine, theirs, zinfo)


def rows_kernel(sizes, chosen, where, *refs):
    s_refs = grouped(sizes, refs)
    high_ref, low_ref, buffer, sem = refs[sum(sizes) :]
    rows = high_ref.shape[0] // 2
    pieces = rows // KC
    deepest = max(sizes)
    for slot in range(2 * pieces):
        which = where[1 - slot // pieces]
        piece = slot % pieces
        if chosen is not None:
            hits = chosen(where, which * pieces + piece)
            for hit, group in zip(hits, s_refs):

                @pl.when(hit)
                def _(group=group):
                    for number in range(deepest):
                        ref = group[min(number, len(group) - 1)]
                        pltpu.make_async_copy(ref, buffer.at[slot, number], sem.at[slot, number]).start()

        else:
            at = pl.ds(pl.multiple_of(which * rows + piece * KC, KC), KC)
            pltpu.make_async_copy(s_refs[0][0].at[:, at], buffer.at[slot, 0], sem.at[slot, 0]).start()
    for slot in range(2 * pieces):
        for number in range(deepest):
            pltpu.make_async_copy(s_refs[0][0].at[:, 0:KC], buffer.at[slot, number], sem.at[slot, number]).wait()
        at = slice(slot * KC, slot * KC + KC)
        value = buffer[slot, 0]
        if deepest > 1:
            value = jnp.where(value == 0.0, buffer[slot, 1], value)
        high_ref[at, :], low_ref[at, :] = split(value.T)


def rows_left(where, blocks, rows, chosen):
    sizes, blocks = flat(blocks)
    genes = blocks[0].shape[0]
    shape = jax.ShapeDtypeStruct((2 * rows, genes), BF)
    slots = (2 * rows // KC, max(sizes))
    return call(
        functools.partial(rows_kernel, sizes, chosen),
        "rows_left",
        where,
        list(blocks),
        [pl.BlockSpec(memory_space=pl.ANY)] * len(blocks),
        (shape, shape),
        (fixed_out((2 * rows, genes)), fixed_out((2 * rows, genes))),
        (1,),
        [pltpu.VMEM((*slots, genes, KC), F32), pltpu.SemaphoreType.DMA(slots)],
    )


def back_kernel(final, sizes, where, *refs):
    batch_scale, gene_scale, scale, loss_scale = sizes
    pred_refs, x_refs, refs = refs[0:2], refs[2 : 2 + 2 * XS], refs[2 + 2 * XS :]
    high_refs, low_refs = refs[0:2], refs[2:4]
    totals_ref, spot_ref, z_ref, dens_ref = refs[4:8]
    refs = refs[8:]
    if final:
        sent_ref, got_ref, logit_ref, w_ref, out_ref, loss_ref, bhigh, blow, coef = refs
    else:
        out_ref, bhigh, blow, coef = refs
    genes, tile = pred_refs[0].shape
    rows = high_refs[0].shape[0]
    width = genes // NB
    gene_cos, inv_gene, over_gene = cosine(
        totals_ref[0:1, :], totals_ref[1:2, :], totals_ref[2:3, :]
    )

    @pl.when(pl.program_id(0) == 0)
    def _():
        coef[0] = jnp.broadcast_to(-gene_scale * inv_gene, (128, 2 * genes)).T
        coef[1] = jnp.broadcast_to(gene_scale * over_gene, (128, 2 * genes)).T

    spot = spot_ref[...]
    _, inv_spot, over_spot = cosine(spot[0:NB], spot[NB : 2 * NB], spot[2 * NB : 3 * NB])
    column = jnp.zeros((1, tile), F32)
    value = None
    for part in range(2):
        for batch in range(NB):
            at = slice(batch * width, (batch + 1) * width)
            here = slice(part * genes + batch * width, part * genes + (batch + 1) * width)
            x_by = jnp.concatenate([coef[0, here]] * (tile // 128), axis=1) - (
                batch_scale * inv_spot[batch : batch + 1]
            )
            p_by = jnp.concatenate([coef[1, here]] * (tile // 128), axis=1) + (
                batch_scale * over_spot[batch : batch + 1]
            )
            pred = pred_refs[part][at, :]
            grad = of_batch(x_refs[part * XS :], batch, width) * x_by + pred * p_by
            bhigh[here], blow[here] = split(grad)
            if not final:
                column = column + jnp.sum(pred * grad, axis=0, keepdims=True)
        at = slice(part * genes, (part + 1) * genes)
        one = dot(high_refs[part][...], bhigh[at]) + dot(low_refs[part][...], bhigh[at])
        one = one + dot(high_refs[part][...], blow[at])
        value = one if value is None else value + one
    if not final:
        out_ref[0:rows] = value
        out_ref[rows : rows + 1] = column
        out_ref[rows + 1 : rows + 2] = jnp.broadcast_to(
            jnp.sum(gene_cos, axis=1, keepdims=True), (1, tile)
        )
        out_ref[rows + 2 : rows + 8] = jnp.zeros((6, tile), F32)
        return
    inv, raw = z_ref[0:1, :], z_ref[1:2, :]
    dens = totals_ref[3:4, 0:1]
    mass = totals_ref[4:5, 0:1]
    grad_raw = scale * (1.0 / mass - dens_ref[...] / (dens * raw))
    column = sent_ref[0:1, :] + got_ref[rows : rows + 1, :] + raw * grad_raw
    value = value + got_ref[0:rows, :] + w_ref[...] * grad_raw
    out_ref[...] = jnp.exp(logit_ref[...]) * inv * (value - column)

    @pl.when(pl.program_id(0) == 0)
    def _():
        gene_loss, spot_loss, cents, spots_all = loss_scale
        gene = (sent_ref[1:2, 0:128] + got_ref[rows + 1 : rows + 2, 0:128]) * gene_loss
        cos = totals_ref[6:7, 0:128] * spot_loss
        kl = (
            totals_ref[5:6, 0:128] / totals_ref[3:4, 0:128]
            + jnp.log(totals_ref[4:5, 0:128] * (cents / spots_all))
            - jnp.log(totals_ref[3:4, 0:128] * (1.0 / spots_all))
        )
        lane = lax.broadcasted_iota(jnp.int32, (1, 128), 1)
        loss_ref[...] = jnp.where(lane == 0, gene, jnp.where(lane == 1, cos, kl))


def back(where, preds, xs, lefts, totals, spot, zinfo, density, consts, rows, final, tile):
    genes, spots = preds[0].shape
    left = pl.BlockSpec(
        (rows, genes), lambda i, ix: (0 if final is None else 1, 0), pipeline_mode=pl.Buffered(1)
    )
    specs = [by_tile(genes, tile)] * 2 + [by_tile(genes // XS, tile)] * (2 * XS) + [left] * 4
    specs += [fixed((8, 2 * genes)), by_tile(16, tile), by_tile(8, tile), by_tile(1, tile)]
    args = [*preds, *xs, lefts[0][0], lefts[1][0], lefts[0][1], lefts[1][1]]
    args += [totals, spot, zinfo, density]
    if final is None:
        shapes = jax.ShapeDtypeStruct((rows + 8, spots), F32)
        outs = by_tile(rows + 8, tile)
    else:
        args += final
        specs += [
            by_tile(8, tile, rows // 8),
            by_tile(rows + 8, tile),
            pl.BlockSpec((rows, tile), lambda i, ix: (ix[0], i)),
            pl.BlockSpec((rows, 1), lambda i, ix: (ix[0], 0)),
        ]
        shapes = (
            jax.ShapeDtypeStruct((rows, spots), F32),
            jax.ShapeDtypeStruct((1, 128), F32),
        )
        outs = (by_tile(rows, tile), fixed_out((1, 128)))
    return call(
        functools.partial(back_kernel, final is not None, consts),
        "back_sum" if final is None else "back_end",
        where,
        args,
        specs,
        shapes,
        outs,
        (spots // tile,),
        [
            pltpu.VMEM((2 * genes, tile), BF),
            pltpu.VMEM((2 * genes, tile), BF),
            pltpu.VMEM((2, 2 * genes, 128), F32),
        ],
    )


def swap(value, axis, bit):
    return lax.ppermute(value, axis, [(i, i ^ bit) for i in range(lax.axis_size(axis))])


def after(value, *others):
    return lax.optimization_barrier((value, *others))[0]


def tie(*values):
    return lax.optimization_barrier(values)


def local(logits, centroid_expr, spatial, cluster_cells, density, gene_order):
    n_spot = lax.axis_size("spot")
    n_gene = lax.axis_size("gene")
    me = lax.axis_index("spot")
    col = lax.axis_index("gene")
    cents, spots = logits.shape
    genes = spatial.shape[1]
    genes_all = genes * n_gene
    spots_all = spots * n_spot
    rows = cents // n_gene
    scale = float(spots_all * cents)
    consts = (
        scale / (NB * spots_all),
        scale / genes_all,
        scale,
        (-1.0 / genes_all, -1.0 / (NB * spots_all), float(cents), float(spots_all)),
    )
    ring = n_spot == 8 and cents // n_spot == KC
    where = jnp.stack([col, col ^ 1, me]).astype(jnp.int32)
    tile = 512

    order = (gene_order - col * genes).reshape(genes, 1)
    pick = order == lax.broadcasted_iota(jnp.int32, (genes, genes), 1)
    mine = lax.dot_general(
        pick.astype(F32), centroid_expr, NT, precision=lax.Precision.HIGHEST, preferred_element_type=F32
    )
    pick = pick.astype(BF)
    theirs = swap(mine, "gene", 2)
    weights = cluster_cells.astype(F32)
    weights = (weights / jnp.sum(weights)).reshape(cents, 1)
    dens_row = density.reshape(1, spots)
    fwd = lambda name, keys, blocks, acc, scale_by, x: pred_part(
        where, keys, blocks, e_high, e_low, acc, scale_by, x, tile, name
    )
    if ring:
        hop = lambda block, bit: swap(block, "spot", bit)
        keys = [functools.partial(lambda k, ix: ix[2] ^ k, k) for k in range(n_spot)]
        o1, o2, o3, oy = hop(mine, 2), hop(mine, 4), hop(mine, 6), hop(mine, 1)
        x_own = turn(where, pick, spatial, tile)
        o1, oy, theirs, logits, *x_own = tie(o1, oy, theirs, logits, *x_own)
        o1y, ty = hop(o1, 1), hop(theirs, 1)
        x_got = [swap(x_own[0], "gene", 2)]
        e_high, e_low, zinfo = exp_parts(where, logits, weights, dens_row, tile)
        mine, o1y, e_high = tie(mine, o1y, e_high)
        acc = fwd("own_early", keys[:4], [mine, oy, o1, o1y], None, None, None)
        acc, o2, ty, theirs = tie(acc, o2, ty, theirs)
        o2y, t1, t2 = hop(o2, 1), hop(theirs, 2), hop(theirs, 4)
        theirs, ty, acc, o3 = tie(theirs, ty, acc, o3)
        o3y = hop(o3, 1)
        acc_other = fwd("other_early", keys[:2], [theirs, ty], None, None, None)
        acc, acc_other, o2y, o3y, x_got[0], t1, theirs = tie(acc, acc_other, o2y, o3y, x_got[0], t1, theirs)
        t1y, t3 = hop(t1, 1), hop(theirs, 6)
        pred_own, info = fwd("own_late", keys[4:], [o2, o2y, o3, o3y], acc, zinfo, x_own)
        own = [mine, oy, o1, o1y, o2, o2y, o3, o3y]
        own_pick = lambda ix, block: [(block ^ ix[2]) == key for key in range(n_spot)]
    else:
        x_own = turn(where, pick, spatial, tile)
        x_got = [swap(x_own[0], "gene", 2)]
        e_high, e_low, zinfo = exp_parts(where, logits, weights, dens_row, tile)
        own = [lax.all_gather(mine, "spot", axis=1, tiled=True)]
        other = [lax.all_gather(theirs, "spot", axis=1, tiled=True)]
        first = [lambda ix: 0]
        pred_own, info = fwd("own_late", first, own, None, zinfo, x_own)
        own_pick = None

    info_x = swap(info, "gene", 2)
    left_own = rows_left(where, own, rows, own_pick)
    if ring:
        t2, t3, info_x, left_own = tie(t2, t3, info_x, left_own)
    else:
        info_x, left_own = tie(info_x, left_own)
    half = info + info_x
    totals, spot = pack(half, swap(half, "gene", 1), info, info_x, zinfo, genes)
    x_got += [swap(after(one, info_x), "gene", 2) for one in x_own[1:]]
    if ring:
        t2, t1y, totals, acc_other = tie(t2, t1y, totals, acc_other)
        t2y = hop(t2, 1)
        got = swap(totals, "spot", 1)
        acc_other = fwd("other_mid", [keys[2], keys[3], keys[4]], [t1, t1y, t2], acc_other, None, None)
        t3, acc_other, got = tie(t3, acc_other, got)
        totals = totals + got
        t3y = hop(t3, 1)
        for bit in (2, 4):
            totals = totals + swap(totals, "spot", bit)
        acc_other, totals, t2y = tie(acc_other, totals, t2y)
        pred_other = fwd("other_late", keys[5:], [t2y, t3, t3y], acc_other, zinfo, None)
        other = [theirs, ty, t1, t1y, t2, t2y, t3, t3y]
    else:
        totals = lax.psum(totals, "spot")
        pred_other = fwd("other_late", first, other, None, zinfo, None)
    left_other = rows_left(where, other, rows, own_pick)

    common = (
        (pred_own, pred_other), (*x_own, *x_got), (left_own, left_other), totals, spot, zinfo, dens_row, consts, rows,
    )
    sent = back(where, *common, None, tile)
    got = swap(sent, "gene", 1)
    predicted = emit(where, after(pred_own, sent), pick, tile)
    predicted, got = tie(predicted, got)
    grad, loss = back(where, *common, [sent, got, logits, weights], tile)
    return loss[0, 0:3], predicted, grad


def solution(mesh):
    return jax.shard_map(
        local,
        mesh=mesh,
        in_specs=(P(None, "spot"), P("spot", "gene"), P("spot", "gene"), P(), P("spot"), P("gene")),
        out_specs=(P(), P("spot", "gene"), P("gene", "spot")),
        check_vma=False,
    )
```

```python
import functools
import jax
import jax.numpy as jnp
from jax import lax
from jax.experimental import pallas as pl
from jax.experimental.pallas import tpu as pltpu
from jax.sharding import PartitionSpec as P

NB = 4
XS = 2
EPS = 1e-06
BF = jnp.bfloat16
F32 = jnp.float32
KC = 256
NT = (((1,), (1,)), ((), ()))
TN = (((0,), (0,)), ((), ()))
VMEM_LIMIT = 67043328
CHEAP = pl.CostEstimate(flops=1000, bytes_accessed=1000, transcendentals=0)


def split(value):
    high = value.astype(BF)
    return high, (value - high.astype(F32)).astype(BF)


def dot(left, right, dims=(((1,), (0,)), ((), ()))):
    return lax.dot_general(left, right, dims, preferred_element_type=F32)


def call(kernel, name, where, args, specs, out_shape, out_specs, grid, scratch=(), alias=None):
    return pl.pallas_call(
        kernel,
        out_shape=out_shape,
        grid_spec=pltpu.PrefetchScalarGridSpec(
            num_scalar_prefetch=1,
            grid=grid,
            in_specs=specs,
            out_specs=out_specs,
            scratch_shapes=list(scratch),
        ),
        input_output_aliases=alias or {},
        compiler_params=pltpu.CompilerParams(
            dimension_semantics=("arbitrary",), vmem_limit_bytes=VMEM_LIMIT
        ),
        cost_estimate=CHEAP,
        name=name,
    )(where, *args)


def fixed(shape):
    return pl.BlockSpec(shape, lambda i, ix: (0,) * len(shape), pipeline_mode=pl.Buffered(1))


def by_tile(height, tile, row=0, start=0):
    return pl.BlockSpec((height, tile), lambda i, ix: (row, i + start))


def exp_kernel(cents, where, l_ref, w_ref, d_ref, high_ref, low_ref, info_ref, scal):
    step = pl.program_id(0)
    tile = l_ref.shape[1]

    @pl.when(step == 0)
    def _():
        scal[...] = jnp.zeros_like(scal)

    total = weighted = jnp.zeros((1, tile), F32)
    for part in range(l_ref.shape[0] // KC):
        rows = slice(part * KC, part * KC + KC)
        value = jnp.exp(l_ref[rows, :])
        high, low = split(value)
        high_ref[rows, :] = high
        low_ref[rows, :] = low
        total = total + jnp.sum(value, axis=0, keepdims=True)
        weighted = weighted + jnp.sum(value * w_ref[rows, :], axis=0, keepdims=True)
    inv = 1.0 / total
    raw = weighted * inv
    dens = d_ref[...]
    scal[0:1] += dens
    scal[1:2] += raw
    scal[2:3] += dens * (jnp.log(dens) - jnp.log(raw * cents))
    sums = jnp.broadcast_to(jnp.sum(scal[...], axis=1, keepdims=True), (8, tile))
    info_ref[0:1, :] = inv
    info_ref[1:2, :] = raw
    info_ref[2:8, :] = sums[0:6]


def exp_parts(where, logits, weights, density, tile):
    cents, spots = logits.shape
    return call(
        functools.partial(exp_kernel, float(cents)),
        "exp_parts",
        where,
        [logits, weights, density],
        [by_tile(cents, tile), fixed((cents, 1)), by_tile(1, tile)],
        (
            jax.ShapeDtypeStruct((cents, spots), BF),
            jax.ShapeDtypeStruct((cents, spots), BF),
            jax.ShapeDtypeStruct((8, spots), F32),
        ),
        (by_tile(cents, tile), by_tile(cents, tile), by_tile(8, tile)),
        (spots // tile,),
        [pltpu.VMEM((8, tile), F32)],
    )


def turn_kernel(where, pick_ref, x_ref, *out_refs):
    high, low = split(x_ref[...])
    pick = pick_ref[...]
    value = dot(pick, high, NT) + dot(pick, low, NT)
    width = out_refs[0].shape[0]
    for batch, out_ref in enumerate(out_refs):
        out_ref[...] = value[batch * width : (batch + 1) * width]


def turn(where, pick, x, tile):
    spots, genes = x.shape
    width = genes // XS
    return call(
        turn_kernel,
        "turn",
        where,
        [pick, x],
        [fixed((genes, genes)), pl.BlockSpec((tile, genes), lambda i, ix: (i, 0))],
        (jax.ShapeDtypeStruct((width, spots), F32),) * XS,
        (by_tile(width, tile),) * XS,
        (spots // tile,),
    )


def of_batch(refs, batch, width):
    each = NB // XS
    start = batch % each * width
    return refs[batch // each][start : start + width, :]


def load_left(groups, high, low):
    at = 0
    for group in groups:
        value = group[0][...]
        for ref in group[1:]:
            value = value + ref[...]
        wide = value.shape[1]
        high[:, at : at + wide], low[:, at : at + wide] = split(value)
        at += wide


def flat(blocks):
    sizes = [len(block) if isinstance(block, tuple) else 1 for block in blocks]
    arrays = [one for block in blocks for one in (block if isinstance(block, tuple) else (block,))]
    return sizes, arrays


def grouped(sizes, refs):
    out, at = [], 0
    for size in sizes:
        out.append(refs[at : at + size])
        at += size
    return out


def product(high, low, e_high, e_low):
    right = jnp.concatenate([ref[...] for ref in e_high], axis=0)
    value = dot(high[...], right) + dot(low[...], right)
    return value + dot(high[...], jnp.concatenate([ref[...] for ref in e_low], axis=0))


def pred_kernel(sizes, first, last, stats, where, *refs):
    count = len(sizes)
    s_refs, refs = grouped(sizes, refs), refs[sum(sizes) :]
    h_refs, l_refs = refs[:count], refs[count : 2 * count]
    refs = refs[2 * count :]
    if not first:
        acc_ref, refs = refs[0], refs[1:]
    if last:
        zinfo_ref, refs = refs[0], refs[1:]
    if stats:
        x_refs, (out_ref, info_ref, high, low, sums) = refs[:XS], refs[XS:]
    else:
        out_ref, high, low = refs
    step = pl.program_id(0)
    genes, tile = out_ref.shape
    width = genes // NB

    @pl.when(step == 0)
    def _():
        load_left(s_refs, high, low)
        if stats:
            sums[...] = jnp.zeros_like(sums)
            info_ref[...] = jnp.zeros_like(info_ref)

    value = product(high, low, h_refs, l_refs)
    if not first:
        value = value + acc_ref[...]
    if last:
        value = value * zinfo_ref[0:1, :]
    out_ref[...] = value
    if not stats:
        return
    rows = [[], [], []]
    for batch in range(NB):
        at = slice(batch * width, (batch + 1) * width)
        pred, x = value[at], of_batch(x_refs, batch, width)
        for number, term in enumerate((pred * x, pred * pred, x * x)):
            rows[number].append(jnp.sum(term, axis=0, keepdims=True))
            lanes = term[:, :128]
            for group in range(1, tile // 128):
                lanes = lanes + term[:, group * 128 : group * 128 + 128]
            sums[number, at] += lanes
    info_ref[0 : 3 * NB, pl.ds(pl.multiple_of(step * tile, 128), tile)] = jnp.concatenate(
        rows[0] + rows[1] + rows[2], axis=0
    )

    @pl.when(step == pl.num_programs(0) - 1)
    def _():
        for number in range(3):
            info_ref[12:13, number * genes : (number + 1) * genes] = jnp.sum(
                sums[number].T, axis=0, keepdims=True
            )


def pred_part(where, keys, blocks, e_high, e_low, acc, zinfo, x, tile, name):
    cents, spots = e_high.shape
    sizes, blocks = flat(blocks)
    genes, deep = blocks[0].shape
    count = len(sizes)
    first, last, stats = acc is None, zinfo is not None, x is not None
    rows = [
        pl.BlockSpec((deep, tile), functools.partial(lambda key, i, ix: (key(ix), i), key))
        for key in keys
    ]
    specs = [fixed((genes, deep)) for _ in blocks] + rows + rows
    args = [*blocks, *([e_high] * count), *([e_low] * count)]
    alias = {}
    if not first:
        alias = {len(args) + 1: 0}
        specs.append(by_tile(genes, tile))
        args.append(acc)
    if last:
        specs.append(by_tile(8, tile))
        args.append(zinfo)
    shapes = jax.ShapeDtypeStruct((genes, spots), F32)
    outs = by_tile(genes, tile)
    scratch = [pltpu.VMEM((genes, deep * count), BF)] * 2
    if stats:
        specs += [by_tile(genes // XS, tile)] * XS
        args += x
        shapes = (shapes, jax.ShapeDtypeStruct((16, spots), F32))
        outs = (outs, fixed_out((16, spots)))
        scratch.append(pltpu.VMEM((3, genes, 128), F32))
    return call(
        functools.partial(pred_kernel, sizes, first, last, stats),
        name,
        where,
        args,
        specs,
        shapes,
        outs,
        (spots // tile,),
        scratch,
        alias,
    )


def fixed_out(shape):
    return pl.BlockSpec(shape, lambda i, ix: (0,) * len(shape))


def emit_kernel(where, pred_ref, pick_ref, out_ref):
    high, low = split(pred_ref[...].T)
    pick = pick_ref[...]
    out_ref[...] = dot(high, pick) + dot(low, pick)


def emit(where, pred, pick, tile):
    genes, spots = pred.shape
    return call(
        emit_kernel,
        "emit",
        where,
        [pred, pick],
        [by_tile(genes, tile), fixed((genes, genes))],
        jax.ShapeDtypeStruct((spots, genes), F32),
        pl.BlockSpec((tile, genes), lambda i, ix: (i, 0)),
        (spots // tile,),
    )


def cosine(inner, left, right):
    left = left + EPS
    inv = lax.rsqrt(left) * lax.rsqrt(right + EPS)
    cos = inner * inv
    return cos, inv, cos / left


def pack_kernel(half_ref, core_ref, mine_ref, theirs_ref, z_ref, out_ref, spot_ref):
    genes = out_ref.shape[1] // 2
    totals = half_ref[...] + core_ref[...]
    spot_ref[...] = totals
    cos, _, _ = cosine(totals[0:NB], totals[NB : 2 * NB], totals[2 * NB : 3 * NB])
    out_ref[...] = jnp.zeros_like(out_ref)
    spots = z_ref.shape[1]
    for number in range(3):
        at = slice(number * genes, (number + 1) * genes)
        out_ref[number : number + 1, 0:genes] = mine_ref[12:13, at]
        out_ref[number : number + 1, genes : 2 * genes] = theirs_ref[12:13, at]
        out_ref[3 + number : 4 + number, 0:128] = z_ref[2 + number : 3 + number, spots - 128 :]
    out_ref[6:7, 0:128] = jnp.broadcast_to(
        jnp.sum(jnp.sum(cos, axis=0, keepdims=True), axis=1, keepdims=True), (1, 128)
    )


def pack(half, core, mine, theirs, zinfo, genes):
    return pl.pallas_call(
        pack_kernel,
        out_shape=(
            jax.ShapeDtypeStruct((8, 2 * genes), F32),
            jax.ShapeDtypeStruct(half.shape, F32),
        ),
        compiler_params=pltpu.CompilerParams(vmem_limit_bytes=VMEM_LIMIT),
        cost_estimate=CHEAP,
        name="pack",
    )(half, core, mine, theirs, zinfo)


def rows_kernel(sizes, chosen, where, *refs):
    s_refs = grouped(sizes, refs)
    high_ref, low_ref, buffer, sem = refs[sum(sizes) :]
    rows = high_ref.shape[0] // 2
    pieces = rows // KC
    deepest = max(sizes)
    for slot in range(2 * pieces):
        which = where[1 - slot // pieces]
        piece = slot % pieces
        if chosen is not None:
            hits = chosen(where, which * pieces + piece)
            for hit, group in zip(hits, s_refs):

                @pl.when(hit)
                def _(group=group):
                    for number in range(deepest):
                        ref = group[min(number, len(group) - 1)]
                        pltpu.make_async_copy(ref, buffer.at[slot, number], sem.at[slot, number]).start()

        else:
            at = pl.ds(pl.multiple_of(which * rows + piece * KC, KC), KC)
            pltpu.make_async_copy(s_refs[0][0].at[:, at], buffer.at[slot, 0], sem.at[slot, 0]).start()
    for slot in range(2 * pieces):
        for number in range(deepest):
            pltpu.make_async_copy(s_refs[0][0].at[:, 0:KC], buffer.at[slot, number], sem.at[slot, number]).wait()
        at = slice(slot * KC, slot * KC + KC)
        value = buffer[slot, 0]
        if deepest > 1:
            value = jnp.where(value == 0.0, buffer[slot, 1], value)
        high_ref[at, :], low_ref[at, :] = split(value.T)


def rows_left(where, blocks, rows, chosen):
    sizes, blocks = flat(blocks)
    genes = blocks[0].shape[0]
    shape = jax.ShapeDtypeStruct((2 * rows, genes), BF)
    slots = (2 * rows // KC, max(sizes))
    return call(
        functools.partial(rows_kernel, sizes, chosen),
        "rows_left",
        where,
        list(blocks),
        [pl.BlockSpec(memory_space=pl.ANY)] * len(blocks),
        (shape, shape),
        (fixed_out((2 * rows, genes)), fixed_out((2 * rows, genes))),
        (1,),
        [pltpu.VMEM((*slots, genes, KC), F32), pltpu.SemaphoreType.DMA(slots)],
    )


def back_dots(high_refs, low_refs, bhigh, blow, genes):
    value = None
    for part in range(2):
        at = slice(part * genes, (part + 1) * genes)
        one = dot(high_refs[part][...], bhigh[at]) + dot(low_refs[part][...], bhigh[at])
        one = one + dot(high_refs[part][...], blow[at])
        value = one if value is None else value + one
    return value


def back_sum_kernel(sizes, where, *refs):
    batch_scale, gene_scale = sizes
    pred_refs, x_refs, refs = refs[0:2], refs[2 : 2 + 2 * XS], refs[2 + 2 * XS :]
    high_refs, low_refs = refs[0:2], refs[2:4]
    totals_ref, more_ref, spot_ref, out_ref, bhigh, blow, sum_ref, coef = refs[4:]
    genes, tile = pred_refs[0].shape
    rows = high_refs[0].shape[0]
    width = genes // NB

    @pl.when(pl.program_id(0) == 0)
    def _():
        totals = totals_ref[...] + more_ref[...]
        gene_cos, inv_gene, over_gene = cosine(totals[0:1], totals[1:2], totals[2:3])
        coef[0] = jnp.broadcast_to(-gene_scale * inv_gene, (128, 2 * genes)).T
        coef[1] = jnp.broadcast_to(gene_scale * over_gene, (128, 2 * genes)).T
        cos = jnp.broadcast_to(jnp.sum(gene_cos, axis=1, keepdims=True), (1, 128))
        sum_ref[...] = jnp.concatenate([totals[3:7, 0:128], cos, jnp.zeros((3, 128), F32)], axis=0)

    spot = spot_ref[...]
    _, inv_spot, over_spot = cosine(spot[0:NB], spot[NB : 2 * NB], spot[2 * NB : 3 * NB])
    column = jnp.zeros((1, tile), F32)
    for part in range(2):
        for batch in range(NB):
            at = slice(batch * width, (batch + 1) * width)
            here = slice(part * genes + batch * width, part * genes + (batch + 1) * width)
            x_by = jnp.concatenate([coef[0, here]] * (tile // 128), axis=1) - (
                batch_scale * inv_spot[batch : batch + 1]
            )
            p_by = jnp.concatenate([coef[1, here]] * (tile // 128), axis=1) + (
                batch_scale * over_spot[batch : batch + 1]
            )
            pred = pred_refs[part][at, :]
            grad = of_batch(x_refs[part * XS :], batch, width) * x_by + pred * p_by
            bhigh[here], blow[here] = split(grad)
            column = column + jnp.sum(pred * grad, axis=0, keepdims=True)
    out_ref[0:rows] = back_dots(high_refs, low_refs, bhigh, blow, genes)
    out_ref[rows : rows + 1] = column
    out_ref[rows + 1 : rows + 2] = jnp.concatenate([sum_ref[4:5]] * (tile // 128), axis=1)
    out_ref[rows + 2 : rows + 8] = jnp.zeros((6, tile), F32)


def back_sum(where, preds, xs, lefts, totals, more, spot, consts, rows, tile):
    genes, spots = preds[0].shape
    left = pl.BlockSpec((rows, genes), lambda i, ix: (0, 0), pipeline_mode=pl.Buffered(1))
    specs = [by_tile(genes, tile)] * 2 + [by_tile(genes // XS, tile)] * (2 * XS) + [left] * 4
    specs += [fixed((8, 2 * genes))] * 2 + [by_tile(16, tile)]
    args = [*preds, *xs, lefts[0][0], lefts[1][0], lefts[0][1], lefts[1][1], totals, more, spot]
    return call(
        functools.partial(back_sum_kernel, consts[:2]),
        "back_sum",
        where,
        args,
        specs,
        (
            jax.ShapeDtypeStruct((rows + 8, spots), F32),
            jax.ShapeDtypeStruct((2 * genes, spots), BF),
            jax.ShapeDtypeStruct((2 * genes, spots), BF),
            jax.ShapeDtypeStruct((8, 128), F32),
        ),
        (by_tile(rows + 8, tile), by_tile(2 * genes, tile), by_tile(2 * genes, tile), fixed_out((8, 128))),
        (spots // tile,),
        [pltpu.VMEM((2, 2 * genes, 128), F32)],
    )


def back_end_kernel(sizes, where, *refs):
    scale, (gene_loss, spot_loss, cents, spots_all) = sizes
    high_refs, low_refs = refs[0:2], refs[2:4]
    bhigh, blow, sum_ref, z_ref, dens_ref, sent_ref, got_ref, logit_ref, w_ref, out_ref, loss_ref = refs[4:]
    rows, genes = high_refs[0].shape
    value = back_dots(high_refs, low_refs, bhigh, blow, genes)
    inv, raw = z_ref[0:1, :], z_ref[1:2, :]
    dens, mass = sum_ref[0:1, 0:1], sum_ref[1:2, 0:1]
    grad_raw = scale * (1.0 / mass - dens_ref[...] / (dens * raw))
    column = sent_ref[0:1, :] + got_ref[rows : rows + 1, :] + raw * grad_raw
    value = value + got_ref[0:rows, :] + w_ref[...] * grad_raw
    out_ref[...] = jnp.exp(logit_ref[...]) * inv * (value - column)

    @pl.when(pl.program_id(0) == 0)
    def _():
        dens, mass, log_sum, cos = (sum_ref[k : k + 1] for k in range(4))
        gene = (sum_ref[4:5] + got_ref[rows + 1 : rows + 2, 0:128]) * gene_loss
        kl = log_sum / dens + jnp.log(mass * (cents / spots_all)) - jnp.log(dens * (1.0 / spots_all))
        for number, term in enumerate((gene, cos * spot_loss, kl)):
            loss_ref[number] = term[0, 0]


def back_end(where, highs, lefts, sums, zinfo, density, sent, got, logits, weights, consts, rows, tile):
    twice, spots = highs[0].shape
    left = pl.BlockSpec((rows, twice // 2), lambda i, ix: (1, 0), pipeline_mode=pl.Buffered(1))
    specs = [left] * 4 + [by_tile(twice, tile)] * 2
    specs += [fixed((8, 128)), by_tile(8, tile), by_tile(1, tile), by_tile(8, tile, rows // 8), by_tile(rows + 8, tile)]
    specs += [
        pl.BlockSpec((rows, tile), lambda i, ix: (ix[0], i)),
        pl.BlockSpec((rows, 1), lambda i, ix: (ix[0], 0)),
    ]
    args = [lefts[0][0], lefts[1][0], lefts[0][1], lefts[1][1], *highs]
    args += [sums, zinfo, density, sent, got, logits, weights]
    return call(
        functools.partial(back_end_kernel, consts[2:]),
        "back_end",
        where,
        args,
        specs,
        (jax.ShapeDtypeStruct((rows, spots), F32), jax.ShapeDtypeStruct((3,), F32)),
        (by_tile(rows, tile), pl.BlockSpec(memory_space=pltpu.SMEM)),
        (spots // tile,),
    )


def swap(value, axis, bit):
    return lax.ppermute(value, axis, [(i, i ^ bit) for i in range(lax.axis_size(axis))])


def after(value, *others):
    return lax.optimization_barrier((value, *others))[0]


def tie(*values):
    return lax.optimization_barrier(values)


def local(logits, centroid_expr, spatial, cluster_cells, density, gene_order):
    n_spot = lax.axis_size("spot")
    n_gene = lax.axis_size("gene")
    me = lax.axis_index("spot")
    col = lax.axis_index("gene")
    cents, spots = logits.shape
    genes = spatial.shape[1]
    genes_all = genes * n_gene
    spots_all = spots * n_spot
    rows = cents // n_gene
    scale = float(spots_all * cents)
    consts = (
        scale / (NB * spots_all),
        scale / genes_all,
        scale,
        (-1.0 / genes_all, -1.0 / (NB * spots_all), float(cents), float(spots_all)),
    )
    ring = n_spot == 8 and cents // n_spot == KC
    where = jnp.stack([col, col ^ 1, me]).astype(jnp.int32)
    tile = 512

    order = (gene_order - col * genes).reshape(genes, 1)
    pick = order == lax.broadcasted_iota(jnp.int32, (genes, genes), 1)
    mine = lax.dot_general(
        pick.astype(F32), centroid_expr, NT, precision=lax.Precision.HIGHEST, preferred_element_type=F32
    )
    pick = pick.astype(BF)
    theirs = swap(mine, "gene", 2)
    weights = cluster_cells.astype(F32)
    weights = (weights / jnp.sum(weights)).reshape(cents, 1)
    dens_row = density.reshape(1, spots)
    fwd = lambda name, keys, blocks, acc, scale_by, x: pred_part(
        where, keys, blocks, e_high, e_low, acc, scale_by, x, tile, name
    )
    if ring:
        hop = lambda block, bit: swap(block, "spot", bit)
        send = lambda one, *others: swap(after(one, *others), "gene", 2)
        keys = [functools.partial(lambda k, ix: ix[2] ^ k, k) for k in range(n_spot)]
        o1, o2, oy = [hop(mine, bit) for bit in (2, 4, 1)]
        x_own = turn(where, pick, spatial, tile)
        logits, *x_own = tie(logits, *x_own)
        e_high, e_low, zinfo = exp_parts(where, logits, weights, dens_row, tile)
        o1, oy, o2, theirs, e_high, *x_own = tie(o1, oy, o2, theirs, e_high, *x_own)
        o2y, o3, o1y = hop(o2, 1), hop(o2, 2), hop(oy, 2)
        x0, t2 = send(x_own[0]), hop(theirs, 4)
        acc = fwd("own_early", keys[:3] + keys[4:5], [mine, oy, o1, o2], None, None, None)
        acc, o2y, o3, theirs = tie(acc, o2y, o3, theirs)
        o3y, ty = hop(o3, 1), hop(theirs, 1)
        acc, o3y, o1y, theirs = tie(acc, o3y, o1y, theirs)
        t1 = hop(theirs, 2)
        pred_own, info = fwd("own_late", keys[3:4] + keys[5:], [o1y, o2y, o3, o3y], acc, zinfo, x_own)
        own = [mine, oy, o1, o1y, o2, o2y, o3, o3y]
        own_pick = lambda ix, block: [(block ^ ix[2]) == key for key in range(n_spot)]
    else:
        x_own = turn(where, pick, spatial, tile)
        x_got = [swap(one, "gene", 2) for one in x_own]
        e_high, e_low, zinfo = exp_parts(where, logits, weights, dens_row, tile)
        own = [lax.all_gather(mine, "spot", axis=1, tiled=True)]
        other = [lax.all_gather(theirs, "spot", axis=1, tiled=True)]
        first = [lambda ix: 0]
        pred_own, info = fwd("own_late", first, own, None, zinfo, x_own)
        own_pick = None

    info_x = swap(info, "gene", 2)
    if ring:
        pred_own, t2, x0, ty, mine = tie(pred_own, t2, x0, ty, mine)
        own[0] = mine
        t3, t2y = hop(t2, 2), hop(t2, 1)
    left_own = rows_left(where, own, rows, own_pick)
    if ring:
        info_x, left_own, t1, held = tie(info_x, left_own, t1, x_own[1])
        x1 = send(held)
    half = info + info_x
    totals, spot = pack(half, swap(half, "gene", 1), info, info_x, zinfo, genes)
    if ring:
        totals, t1, t2y = tie(totals, t1, t2y)
        t1y, t3y = hop(t1, 1), hop(t2y, 2)
        got = swap(totals, "spot", 1)
        acc_other = fwd(
            "other_mid", [keys[k] for k in (0, 1, 2, 4, 5)], [theirs, ty, t1, t2, t2y], None, None, None
        )
        acc_other, got, t1y, t3, t3y = tie(acc_other, got, t1y, t3, t3y)
        totals = totals + got
        got = swap(totals, "spot", 2)
        other = [theirs, ty, t1, t1y, t2, t2y, t3, t3y]
        left_other = rows_left(where, other, rows, own_pick)
        left_other, got = tie(left_other, got)
        totals = totals + got
        got = swap(totals, "spot", 4)
        acc_other, _ = tie(acc_other, left_other)
        pred_other = fwd("other_late", [keys[k] for k in (3, 6, 7)], [t1y, t3, t3y], acc_other, zinfo, None)
        pred_other, got = tie(pred_other, got)
        more = got
        x_got = [x0, x1]
    else:
        totals = lax.psum(totals, "spot")
        more = jnp.zeros_like(totals)
        pred_other = fwd("other_late", first, other, None, zinfo, None)
        left_other = rows_left(where, other, rows, own_pick)

    lefts = (left_own, left_other)
    sent, *highs, sums = back_sum(
        where, (pred_own, pred_other), (*x_own, *x_got), lefts, totals, more, spot, consts, rows, tile
    )
    got = swap(sent, "gene", 1)
    predicted = emit(where, after(pred_own, sent), pick, tile)
    predicted, got = tie(predicted, got)
    grad, loss = back_end(
        where, highs, lefts, sums, zinfo, dens_row, sent, got, logits, weights, consts, rows, tile
    )
    return loss, predicted, grad


def solution(mesh):
    return jax.shard_map(
        local,
        mesh=mesh,
        in_specs=(P(None, "spot"), P("spot", "gene"), P("spot", "gene"), P(), P("spot"), P("gene")),
        out_specs=(P(), P("spot", "gene"), P("gene", "spot")),
        check_vma=False,
    )
```

```python
import functools
import jax
import jax.numpy as jnp
from jax import lax
from jax.experimental import pallas as pl
from jax.experimental.pallas import tpu as pltpu
from jax.sharding import PartitionSpec as P

NB = 4
XS = 2
EPS = 1e-06
BF = jnp.bfloat16
F32 = jnp.float32
KC = 256
NT = (((1,), (1,)), ((), ()))
TN = (((0,), (0,)), ((), ()))
VMEM_LIMIT = 67043328
CHEAP = pl.CostEstimate(flops=1000, bytes_accessed=1000, transcendentals=0)


def split(value):
    high = value.astype(BF)
    return high, (value - high.astype(F32)).astype(BF)


def dot(left, right, dims=(((1,), (0,)), ((), ()))):
    return lax.dot_general(left, right, dims, preferred_element_type=F32)


def call(kernel, name, where, args, specs, out_shape, out_specs, grid, scratch=(), alias=None):
    return pl.pallas_call(
        kernel,
        out_shape=out_shape,
        grid_spec=pltpu.PrefetchScalarGridSpec(
            num_scalar_prefetch=1,
            grid=grid,
            in_specs=specs,
            out_specs=out_specs,
            scratch_shapes=list(scratch),
        ),
        input_output_aliases=alias or {},
        compiler_params=pltpu.CompilerParams(
            dimension_semantics=("arbitrary",), vmem_limit_bytes=VMEM_LIMIT
        ),
        cost_estimate=CHEAP,
        name=name,
    )(where, *args)


def fixed(shape):
    return pl.BlockSpec(shape, lambda i, ix: (0,) * len(shape), pipeline_mode=pl.Buffered(1))


def by_tile(height, tile, row=0, start=0):
    return pl.BlockSpec((height, tile), lambda i, ix: (row, i + start))


def exp_kernel(cents, count, first, last, where, *refs):
    l_refs, w_refs, d_ref, refs = refs[:count], refs[count : 2 * count], refs[2 * count], refs[2 * count + 1 :]
    if not first:
        before_ref, refs = refs[0], refs[1:]
    high_ref, low_ref, info_ref, scal = refs
    step = pl.program_id(0)
    tile = d_ref.shape[1]

    @pl.when(step == 0)
    def _():
        scal[...] = jnp.zeros_like(scal)

    if first:
        total = weighted = jnp.zeros((1, tile), F32)
    else:
        total, weighted = before_ref[0:1, :], before_ref[1:2, :]
    start = 0
    for l_ref, w_ref in zip(l_refs, w_refs):
        for part in range(l_ref.shape[0] // KC):
            rows = slice(part * KC, part * KC + KC)
            value = jnp.exp(l_ref[rows, :])
            high, low = split(value)
            high_ref[start : start + KC, :] = high
            low_ref[start : start + KC, :] = low
            start += KC
            total = total + jnp.sum(value, axis=0, keepdims=True)
            weighted = weighted + jnp.sum(value * w_ref[rows, :], axis=0, keepdims=True)
    if not last:
        info_ref[...] = jnp.concatenate([total, weighted, jnp.zeros((6, tile), F32)], axis=0)
        return
    inv = 1.0 / total
    raw = weighted * inv
    dens = d_ref[...]
    scal[0:1] += dens
    scal[1:2] += raw
    scal[2:3] += dens * (jnp.log(dens) - jnp.log(raw * cents))
    sums = jnp.broadcast_to(jnp.sum(scal[...], axis=1, keepdims=True), (8, tile))
    info_ref[0:1, :] = inv
    info_ref[1:2, :] = raw
    info_ref[2:8, :] = sums[0:6]


def exp_parts(where, keys, deep, logits, weights, density, before, last, tile):
    cents, spots = logits.shape
    count = len(keys)
    specs = [
        pl.BlockSpec((deep, tile), functools.partial(lambda key, i, ix: (key(ix), i), key)) for key in keys
    ]
    specs += [pl.BlockSpec((deep, 1), functools.partial(lambda key, i, ix: (key(ix), 0), key)) for key in keys]
    specs.append(by_tile(1, tile))
    args = [*([logits] * count), *([weights] * count), density]
    if before is not None:
        specs.append(by_tile(8, tile))
        args.append(before)
    rows = deep * count
    return call(
        functools.partial(exp_kernel, float(cents), count, before is None, last),
        "exp_parts",
        where,
        args,
        specs,
        (
            jax.ShapeDtypeStruct((rows, spots), BF),
            jax.ShapeDtypeStruct((rows, spots), BF),
            jax.ShapeDtypeStruct((8, spots), F32),
        ),
        (by_tile(rows, tile), by_tile(rows, tile), by_tile(8, tile)),
        (spots // tile,),
        [pltpu.VMEM((8, tile), F32)],
    )


def turn_kernel(where, pick_ref, x_ref, *out_refs):
    high, low = split(x_ref[...])
    pick = pick_ref[...]
    value = dot(pick, high, NT) + dot(pick, low, NT)
    width = out_refs[0].shape[0]
    for batch, out_ref in enumerate(out_refs):
        out_ref[...] = value[batch * width : (batch + 1) * width]


def turn(where, pick, x, tile):
    spots, genes = x.shape
    width = genes // XS
    return call(
        turn_kernel,
        "turn",
        where,
        [pick, x],
        [fixed((genes, genes)), pl.BlockSpec((tile, genes), lambda i, ix: (i, 0))],
        (jax.ShapeDtypeStruct((width, spots), F32),) * XS,
        (by_tile(width, tile),) * XS,
        (spots // tile,),
    )


def of_batch(refs, batch, width):
    each = NB // XS
    start = batch % each * width
    return refs[batch // each][start : start + width, :]


def load_left(refs, high, low):
    at = 0
    for ref in refs:
        wide = ref.shape[1]
        high[:, at : at + wide], low[:, at : at + wide] = split(ref[...])
        at += wide


def product(high, low, e_high, e_low):
    right = jnp.concatenate([ref[...] for ref in e_high], axis=0)
    value = dot(high[...], right) + dot(low[...], right)
    return value + dot(high[...], jnp.concatenate([ref[...] for ref in e_low], axis=0))


def pred_kernel(blocks, count, first, last, stats, where, *refs):
    s_refs, refs = refs[:blocks], refs[blocks:]
    h_refs, l_refs = refs[:count], refs[count : 2 * count]
    refs = refs[2 * count :]
    if not first:
        acc_ref, refs = refs[0], refs[1:]
    if last:
        zinfo_ref, refs = refs[0], refs[1:]
    if stats:
        x_refs, (out_ref, info_ref, high, low, sums) = refs[:XS], refs[XS:]
    else:
        out_ref, high, low = refs
    step = pl.program_id(0)
    genes, tile = out_ref.shape
    width = genes // NB

    @pl.when(step == 0)
    def _():
        load_left(s_refs, high, low)
        if stats:
            sums[...] = jnp.zeros_like(sums)
            info_ref[...] = jnp.zeros_like(info_ref)

    value = product(high, low, h_refs, l_refs)
    if not first:
        value = value + acc_ref[...]
    if last:
        value = value * zinfo_ref[0:1, :]
    out_ref[...] = value
    if not stats:
        return
    rows = [[], [], []]
    for batch in range(NB):
        at = slice(batch * width, (batch + 1) * width)
        pred, x = value[at], of_batch(x_refs, batch, width)
        for number, term in enumerate((pred * x, pred * pred, x * x)):
            rows[number].append(jnp.sum(term, axis=0, keepdims=True))
            lanes = term[:, :128]
            for group in range(1, tile // 128):
                lanes = lanes + term[:, group * 128 : group * 128 + 128]
            sums[number, at] += lanes
    info_ref[0 : 3 * NB, pl.ds(pl.multiple_of(step * tile, 128), tile)] = jnp.concatenate(
        rows[0] + rows[1] + rows[2], axis=0
    )

    @pl.when(step == pl.num_programs(0) - 1)
    def _():
        for number in range(3):
            info_ref[12:13, number * genes : (number + 1) * genes] = jnp.sum(
                sums[number].T, axis=0, keepdims=True
            )


def pred_part(where, blocks, terms, acc, zinfo, x, tile, name):
    spots = terms[0][0].shape[1]
    genes, deep = blocks[0].shape
    first, last, stats = acc is None, zinfo is not None, x is not None
    specs = [fixed((genes, deep)) for _ in blocks]
    specs += [by_tile(rows, tile, place) for _, _, rows, place in terms] * 2
    args = [*blocks, *(term[0] for term in terms), *(term[1] for term in terms)]
    alias = {}
    if not first:
        alias = {len(args) + 1: 0}
        specs.append(by_tile(genes, tile))
        args.append(acc)
    if last:
        specs.append(by_tile(8, tile))
        args.append(zinfo)
    shapes = jax.ShapeDtypeStruct((genes, spots), F32)
    outs = by_tile(genes, tile)
    scratch = [pltpu.VMEM((genes, deep * len(blocks)), BF)] * 2
    if stats:
        specs += [by_tile(genes // XS, tile)] * XS
        args += x
        shapes = (shapes, jax.ShapeDtypeStruct((16, spots), F32))
        outs = (outs, fixed_out((16, spots)))
        scratch.append(pltpu.VMEM((3, genes, 128), F32))
    return call(
        functools.partial(pred_kernel, len(blocks), len(terms), first, last, stats),
        name,
        where,
        args,
        specs,
        shapes,
        outs,
        (spots // tile,),
        scratch,
        alias,
    )


def fixed_out(shape):
    return pl.BlockSpec(shape, lambda i, ix: (0,) * len(shape))


def emit_kernel(where, pred_ref, pick_ref, out_ref):
    high, low = split(pred_ref[...].T)
    pick = pick_ref[...]
    out_ref[...] = dot(high, pick) + dot(low, pick)


def emit(where, pred, pick, tile):
    genes, spots = pred.shape
    return call(
        emit_kernel,
        "emit",
        where,
        [pred, pick],
        [by_tile(genes, tile), fixed((genes, genes))],
        jax.ShapeDtypeStruct((spots, genes), F32),
        pl.BlockSpec((tile, genes), lambda i, ix: (i, 0)),
        (spots // tile,),
    )


def cosine(inner, left, right):
    left = left + EPS
    inv = lax.rsqrt(left) * lax.rsqrt(right + EPS)
    cos = inner * inv
    return cos, inv, cos / left


def pack_kernel(mine_ref, theirs_ref, core_ref, far_ref, z_ref, out_ref, spot_ref):
    genes = out_ref.shape[1] // 2
    totals = (mine_ref[...] + theirs_ref[...]) + (core_ref[...] + far_ref[...])
    spot_ref[...] = totals
    cos, _, _ = cosine(totals[0:NB], totals[NB : 2 * NB], totals[2 * NB : 3 * NB])
    out_ref[...] = jnp.zeros_like(out_ref)
    spots = z_ref.shape[1]
    for number in range(3):
        at = slice(number * genes, (number + 1) * genes)
        out_ref[number : number + 1, 0:genes] = mine_ref[12:13, at]
        out_ref[number : number + 1, genes : 2 * genes] = theirs_ref[12:13, at]
        out_ref[3 + number : 4 + number, 0:128] = z_ref[2 + number : 3 + number, spots - 128 :]
    out_ref[6:7, 0:128] = jnp.broadcast_to(
        jnp.sum(jnp.sum(cos, axis=0, keepdims=True), axis=1, keepdims=True), (1, 128)
    )


def pack(mine, theirs, core, far, zinfo, genes):
    return pl.pallas_call(
        pack_kernel,
        out_shape=(
            jax.ShapeDtypeStruct((8, 2 * genes), F32),
            jax.ShapeDtypeStruct(mine.shape, F32),
        ),
        compiler_params=pltpu.CompilerParams(vmem_limit_bytes=VMEM_LIMIT),
        cost_estimate=CHEAP,
        name="pack",
    )(mine, theirs, core, far, zinfo)


def rows_kernel(count, chosen, where, *refs):
    s_refs, (high_ref, low_ref, buffer, sem) = refs[:count], refs[count:]
    rows = high_ref.shape[0] // 2
    pieces = rows // KC
    for slot in range(2 * pieces):
        which = where[1 - slot // pieces]
        piece = slot % pieces
        if chosen is not None:
            for hit, ref in zip(chosen(where, which * pieces + piece), s_refs):

                @pl.when(hit)
                def _(ref=ref):
                    pltpu.make_async_copy(ref, buffer.at[slot], sem.at[slot]).start()

        else:
            at = pl.ds(pl.multiple_of(which * rows + piece * KC, KC), KC)
            pltpu.make_async_copy(s_refs[0].at[:, at], buffer.at[slot], sem.at[slot]).start()
    for slot in range(2 * pieces):
        pltpu.make_async_copy(s_refs[0].at[:, 0:KC], buffer.at[slot], sem.at[slot]).wait()
        at = slice(slot * KC, slot * KC + KC)
        high_ref[at, :], low_ref[at, :] = split(buffer[slot].T)


def rows_left(where, blocks, rows, chosen):
    genes = blocks[0].shape[0]
    shape = jax.ShapeDtypeStruct((2 * rows, genes), BF)
    slots = 2 * rows // KC
    return call(
        functools.partial(rows_kernel, len(blocks), chosen),
        "rows_left",
        where,
        list(blocks),
        [pl.BlockSpec(memory_space=pl.ANY)] * len(blocks),
        (shape, shape),
        (fixed_out((2 * rows, genes)), fixed_out((2 * rows, genes))),
        (1,),
        [pltpu.VMEM((slots, genes, KC), F32), pltpu.SemaphoreType.DMA((slots,))],
    )


def back_dots(high_refs, low_refs, bhigh, blow, genes):
    value = None
    for part in range(2):
        at = slice(part * genes, (part + 1) * genes)
        one = dot(high_refs[part][...], bhigh[at]) + dot(low_refs[part][...], bhigh[at])
        one = one + dot(high_refs[part][...], blow[at])
        value = one if value is None else value + one
    return value


def back_sum_kernel(sizes, where, *refs):
    batch_scale, gene_scale = sizes
    pred_refs, x_refs, refs = refs[0:2], refs[2 : 2 + 2 * XS], refs[2 + 2 * XS :]
    high_refs, low_refs = refs[0:2], refs[2:4]
    totals_ref, more_ref, spot_ref, out_ref, bhigh, blow, sum_ref, coef = refs[4:]
    genes, tile = pred_refs[0].shape
    rows = high_refs[0].shape[0]
    width = genes // NB

    @pl.when(pl.program_id(0) == 0)
    def _():
        totals = totals_ref[...] + more_ref[...]
        gene_cos, inv_gene, over_gene = cosine(totals[0:1], totals[1:2], totals[2:3])
        coef[0] = jnp.broadcast_to(-gene_scale * inv_gene, (128, 2 * genes)).T
        coef[1] = jnp.broadcast_to(gene_scale * over_gene, (128, 2 * genes)).T
        cos = jnp.broadcast_to(jnp.sum(gene_cos, axis=1, keepdims=True), (1, 128))
        sum_ref[...] = jnp.concatenate([totals[3:7, 0:128], cos, jnp.zeros((3, 128), F32)], axis=0)

    spot = spot_ref[...]
    _, inv_spot, over_spot = cosine(spot[0:NB], spot[NB : 2 * NB], spot[2 * NB : 3 * NB])
    column = jnp.zeros((1, tile), F32)
    for part in range(2):
        for batch in range(NB):
            at = slice(batch * width, (batch + 1) * width)
            here = slice(part * genes + batch * width, part * genes + (batch + 1) * width)
            x_by = jnp.concatenate([coef[0, here]] * (tile // 128), axis=1) - (
                batch_scale * inv_spot[batch : batch + 1]
            )
            p_by = jnp.concatenate([coef[1, here]] * (tile // 128), axis=1) + (
                batch_scale * over_spot[batch : batch + 1]
            )
            pred = pred_refs[part][at, :]
            grad = of_batch(x_refs[part * XS :], batch, width) * x_by + pred * p_by
            bhigh[here], blow[here] = split(grad)
            column = column + jnp.sum(pred * grad, axis=0, keepdims=True)
    out_ref[0:rows] = back_dots(high_refs, low_refs, bhigh, blow, genes)
    out_ref[rows : rows + 1] = column
    out_ref[rows + 1 : rows + 2] = jnp.concatenate([sum_ref[4:5]] * (tile // 128), axis=1)
    out_ref[rows + 2 : rows + 8] = jnp.zeros((6, tile), F32)


def back_sum(where, preds, xs, lefts, totals, more, spot, consts, rows, tile):
    genes, spots = preds[0].shape
    left = pl.BlockSpec((rows, genes), lambda i, ix: (0, 0), pipeline_mode=pl.Buffered(1))
    specs = [by_tile(genes, tile)] * 2 + [by_tile(genes // XS, tile)] * (2 * XS) + [left] * 4
    specs += [fixed((8, 2 * genes))] * 2 + [by_tile(16, tile)]
    args = [*preds, *xs, lefts[0][0], lefts[1][0], lefts[0][1], lefts[1][1], totals, more, spot]
    return call(
        functools.partial(back_sum_kernel, consts[:2]),
        "back_sum",
        where,
        args,
        specs,
        (
            jax.ShapeDtypeStruct((rows + 8, spots), F32),
            jax.ShapeDtypeStruct((2 * genes, spots), BF),
            jax.ShapeDtypeStruct((2 * genes, spots), BF),
            jax.ShapeDtypeStruct((8, 128), F32),
        ),
        (by_tile(rows + 8, tile), by_tile(2 * genes, tile), by_tile(2 * genes, tile), fixed_out((8, 128))),
        (spots // tile,),
        [pltpu.VMEM((2, 2 * genes, 128), F32)],
    )


def back_end_kernel(sizes, where, *refs):
    scale, (gene_loss, spot_loss, cents, spots_all) = sizes
    high_refs, low_refs = refs[0:2], refs[2:4]
    bhigh, blow, sum_ref, z_ref, dens_ref, sent_ref, got_ref, logit_ref, w_ref, out_ref, loss_ref = refs[4:]
    rows, genes = high_refs[0].shape
    value = back_dots(high_refs, low_refs, bhigh, blow, genes)
    inv, raw = z_ref[0:1, :], z_ref[1:2, :]
    dens, mass = sum_ref[0:1, 0:1], sum_ref[1:2, 0:1]
    grad_raw = scale * (1.0 / mass - dens_ref[...] / (dens * raw))
    column = sent_ref[0:1, :] + got_ref[rows : rows + 1, :] + raw * grad_raw
    value = value + got_ref[0:rows, :] + w_ref[...] * grad_raw
    out_ref[...] = jnp.exp(logit_ref[...]) * inv * (value - column)

    @pl.when(pl.program_id(0) == 0)
    def _():
        dens, mass, log_sum, cos = (sum_ref[k : k + 1] for k in range(4))
        gene = (sum_ref[4:5] + got_ref[rows + 1 : rows + 2, 0:128]) * gene_loss
        kl = log_sum / dens + jnp.log(mass * (cents / spots_all)) - jnp.log(dens * (1.0 / spots_all))
        for number, term in enumerate((gene, cos * spot_loss, kl)):
            loss_ref[number] = term[0, 0]


def back_end(where, highs, lefts, sums, zinfo, density, sent, got, logits, weights, consts, rows, tile):
    twice, spots = highs[0].shape
    left = pl.BlockSpec((rows, twice // 2), lambda i, ix: (1, 0), pipeline_mode=pl.Buffered(1))
    specs = [left] * 4 + [by_tile(twice, tile)] * 2
    specs += [fixed((8, 128)), by_tile(8, tile), by_tile(1, tile), by_tile(8, tile, rows // 8), by_tile(rows + 8, tile)]
    specs += [
        pl.BlockSpec((rows, tile), lambda i, ix: (ix[0], i)),
        pl.BlockSpec((rows, 1), lambda i, ix: (ix[0], 0)),
    ]
    args = [lefts[0][0], lefts[1][0], lefts[0][1], lefts[1][1], *highs]
    args += [sums, zinfo, density, sent, got, logits, weights]
    return call(
        functools.partial(back_end_kernel, consts[2:]),
        "back_end",
        where,
        args,
        specs,
        (jax.ShapeDtypeStruct((rows, spots), F32), jax.ShapeDtypeStruct((3,), F32)),
        (by_tile(rows, tile), pl.BlockSpec(memory_space=pltpu.SMEM)),
        (spots // tile,),
    )


def swap(value, axis, bit):
    return lax.ppermute(value, axis, [(i, i ^ bit) for i in range(lax.axis_size(axis))])


def after(value, *others):
    return lax.optimization_barrier((value, *others))[0]


def tie(*values):
    return lax.optimization_barrier(values)


def local(logits, centroid_expr, spatial, cluster_cells, density, gene_order):
    n_spot = lax.axis_size("spot")
    n_gene = lax.axis_size("gene")
    me = lax.axis_index("spot")
    col = lax.axis_index("gene")
    cents, spots = logits.shape
    genes = spatial.shape[1]
    genes_all = genes * n_gene
    spots_all = spots * n_spot
    rows = cents // n_gene
    scale = float(spots_all * cents)
    consts = (
        scale / (NB * spots_all),
        scale / genes_all,
        scale,
        (-1.0 / genes_all, -1.0 / (NB * spots_all), float(cents), float(spots_all)),
    )
    ring = n_spot == 8 and cents // n_spot == KC
    where = jnp.stack([col, col ^ 1, me]).astype(jnp.int32)
    tile = 512

    order = (gene_order - col * genes).reshape(genes, 1)
    pick = order == lax.broadcasted_iota(jnp.int32, (genes, genes), 1)
    mine = lax.dot_general(
        pick.astype(F32), centroid_expr, NT, precision=lax.Precision.HIGHEST, preferred_element_type=F32
    )
    pick = pick.astype(BF)
    theirs = swap(mine, "gene", 2)
    weights = cluster_cells.astype(F32)
    weights = (weights / jnp.sum(weights)).reshape(cents, 1)
    dens_row = density.reshape(1, spots)
    fwd = lambda name, blocks, terms, acc, scale_by, x: pred_part(
        where, blocks, terms, acc, scale_by, x, tile, name
    )
    if ring:
        hop = lambda block, bit: swap(block, "spot", bit)
        send = lambda one, *others: swap(after(one, *others), "gene", 2)
        keys = lambda *order: [functools.partial(lambda k, ix: ix[2] ^ k, k) for k in order]
        o1, o2, oy = [hop(mine, bit) for bit in (2, 4, 1)]
        x_own = turn(where, pick, spatial, 2 * tile)
        logits, *x_own = tie(logits, *x_own)
        *e_one, z_one = exp_parts(where, keys(0, 1, 2, 4), KC, logits, weights, dens_row, None, False, 2 * tile)
        o1, oy, o2, theirs, z_one, *x_own = tie(o1, oy, o2, theirs, z_one, *x_own)
        o2y, o3 = hop(o2, 1), hop(o2, 2)
        x0 = send(x_own[0])
        acc = fwd("own_early", [mine, oy, o1, o2], [(*e_one, 4 * KC, 0)], None, None, None)
        acc, o2y, o3, oy, theirs, z_one, logits = tie(acc, o2y, o3, oy, theirs, z_one, logits)
        o3y, o1y, ty = hop(o3, 1), hop(oy, 2), hop(theirs, 1)
        *e_two, zinfo = exp_parts(where, keys(3, 5, 6, 7), KC, logits, weights, dens_row, z_one, True, 2 * tile)
        acc, o3y, o1y, theirs, zinfo = tie(acc, o3y, o1y, theirs, zinfo)
        t1, t2 = hop(theirs, 2), hop(theirs, 4)
        pred_own, info = fwd("own_late", [o1y, o2y, o3, o3y], [(*e_two, 4 * KC, 0)], acc, zinfo, x_own)
        own = [mine, oy, o1, o1y, o2, o2y, o3, o3y]
        own_pick = lambda ix, block: [(block ^ ix[2]) == key for key in range(n_spot)]
    else:
        x_own = turn(where, pick, spatial, 2 * tile)
        x_got = [swap(one, "gene", 2) for one in x_own]
        *e_all, zinfo = exp_parts(where, [lambda ix: 0], cents, logits, weights, dens_row, None, True, tile)
        own = [lax.all_gather(mine, "spot", axis=1, tiled=True)]
        other = [lax.all_gather(theirs, "spot", axis=1, tiled=True)]
        whole = [(*e_all, cents, 0)]
        pred_own, info = fwd("own_late", own, whole, None, zinfo, x_own)
        own_pick = None

    infos = [swap(info, "gene", bit) for bit in (2, 1, 3)]
    if ring:
        pred_own, t1, ty, x0, mine = tie(pred_own, t1, ty, x0, mine)
        t1y = hop(t1, 1)
        own[0] = mine
    left_own = rows_left(where, own, rows, own_pick)
    if ring:
        t2, left_own, held, *infos = tie(t2, left_own, x_own[1], *infos)
        t3, t2y, x1 = hop(t2, 2), hop(t2, 1), send(held)
    totals, spot = pack(info, *infos, zinfo, genes)
    if ring:
        got = swap(totals, "spot", 1)
        theirs, totals = tie(theirs, totals)
        acc_other = fwd("other_mid", [theirs, ty, t1, t2], [(*e_one, 4 * KC, 0)], None, None, None)
        acc_other, got, t2y, t3 = tie(acc_other, got, t2y, t3)
        t3y = hop(t2y, 2)
        totals = totals + got
        got = swap(totals, "spot", 2)
        acc_other, totals = tie(acc_other, totals)
        acc_other = fwd("other_more", [t2y, t3], [(*e_two, KC, 1), (*e_two, KC, 2)], acc_other, None, None)
        t1y, t3y, acc_other = tie(t1y, t3y, acc_other)
        other = [theirs, ty, t1, t1y, t2, t2y, t3, t3y]
        left_other = rows_left(where, other, rows, own_pick)
        left_other, got = tie(left_other, got)
        totals = totals + got
        got = swap(totals, "spot", 4)
        acc_other, _ = tie(acc_other, left_other)
        pred_other = fwd(
            "other_late", [t1y, t3y], [(*e_two, KC, 0), (*e_two, KC, 3)], acc_other, zinfo, None
        )
        pred_other, more = tie(pred_other, got)
        x_got = [x0, x1]
    else:
        totals = lax.psum(totals, "spot")
        more = jnp.zeros_like(totals)
        pred_other = fwd("other_late", other, whole, None, zinfo, None)
        left_other = rows_left(where, other, rows, own_pick)

    lefts = (left_own, left_other)
    sent, *highs, sums = back_sum(
        where, (pred_own, pred_other), (*x_own, *x_got), lefts, totals, more, spot, consts, rows, tile
    )
    got = swap(sent, "gene", 1)
    predicted = emit(where, after(pred_own, sent), pick, 2 * tile)
    predicted, got = tie(predicted, got)
    grad, loss = back_end(
        where, highs, lefts, sums, zinfo, dens_row, sent, got, logits, weights, consts, rows, tile
    )
    return loss, predicted, grad


def solution(mesh):
    return jax.shard_map(
        local,
        mesh=mesh,
        in_specs=(P(None, "spot"), P("spot", "gene"), P("spot", "gene"), P(), P("spot"), P("gene")),
        out_specs=(P(), P("spot", "gene"), P("gene", "spot")),
        check_vma=False,
    )
```

```python
import functools
import jax
import jax.numpy as jnp
from jax import lax
from jax.experimental import pallas as pl
from jax.experimental.pallas import tpu as pltpu
from jax.sharding import PartitionSpec as P

NB = 4
XS = 3
XCUT = (0, 2, 3, NB)
EPS = 1e-06
BF = jnp.bfloat16
F32 = jnp.float32
KC = 256
NT = (((1,), (1,)), ((), ()))
TN = (((0,), (0,)), ((), ()))
VMEM_LIMIT = 24 << 20
LARGE_LIMIT = 60 << 20
CHEAP = pl.CostEstimate(flops=1000, bytes_accessed=1000, transcendentals=0)


def split(value):
    high = value.astype(BF)
    return high, (value - high.astype(F32)).astype(BF)


def dot(left, right, dims=(((1,), (0,)), ((), ()))):
    return lax.dot_general(left, right, dims, preferred_element_type=F32)


def call(kernel, name, where, args, specs, out_shape, out_specs, grid, scratch=(), alias=None, limit=VMEM_LIMIT):
    return pl.pallas_call(
        kernel,
        out_shape=out_shape,
        grid_spec=pltpu.PrefetchScalarGridSpec(
            num_scalar_prefetch=1,
            grid=grid,
            in_specs=specs,
            out_specs=out_specs,
            scratch_shapes=list(scratch),
        ),
        input_output_aliases=alias or {},
        compiler_params=pltpu.CompilerParams(
            dimension_semantics=("arbitrary",), vmem_limit_bytes=limit
        ),
        cost_estimate=CHEAP,
        name=name,
    )(where, *args)


def limit_of(depth):
    return VMEM_LIMIT if depth <= 5 * KC else LARGE_LIMIT


def fixed(shape):
    return pl.BlockSpec(shape, lambda i, ix: (0,) * len(shape), pipeline_mode=pl.Buffered(1))


def by_tile(height, tile, row=0, start=0):
    return pl.BlockSpec((height, tile), lambda i, ix: (row, i + start))


def exp_kernel(cents, count, first, last, where, *refs):
    l_refs, w_refs, d_ref, refs = refs[:count], refs[count : 2 * count], refs[2 * count], refs[2 * count + 1 :]
    if not first:
        before_ref, refs = refs[0], refs[1:]
    high_ref, low_ref, info_ref, scal = refs
    step = pl.program_id(0)
    tile = d_ref.shape[1]

    @pl.when(step == 0)
    def _():
        scal[...] = jnp.zeros_like(scal)

    if first:
        total = weighted = jnp.zeros((1, tile), F32)
    else:
        total, weighted = before_ref[0:1, :], before_ref[1:2, :]
    start = 0
    for l_ref, w_ref in zip(l_refs, w_refs):
        for part in range(l_ref.shape[0] // KC):
            rows = slice(part * KC, part * KC + KC)
            value = jnp.exp(l_ref[rows, :])
            high, low = split(value)
            high_ref[start : start + KC, :] = high
            low_ref[start : start + KC, :] = low
            start += KC
            total = total + jnp.sum(value, axis=0, keepdims=True)
            weighted = weighted + jnp.sum(value * w_ref[rows, :], axis=0, keepdims=True)
    if not last:
        info_ref[...] = jnp.concatenate([total, weighted, jnp.zeros((6, tile), F32)], axis=0)
        return
    inv = 1.0 / total
    raw = weighted * inv
    dens = d_ref[...]
    scal[0:1] += dens
    scal[1:2] += raw
    scal[2:3] += dens * (jnp.log(dens) - jnp.log(raw * cents))
    sums = jnp.broadcast_to(jnp.sum(scal[...], axis=1, keepdims=True), (8, tile))
    info_ref[0:1, :] = inv
    info_ref[1:2, :] = raw
    info_ref[2:8, :] = sums[0:6]


def exp_parts(where, keys, deep, logits, weights, density, before, last, tile):
    cents, spots = logits.shape
    count = len(keys)
    specs = [
        pl.BlockSpec((deep, tile), functools.partial(lambda key, i, ix: (key(ix), i), key)) for key in keys
    ]
    specs += [pl.BlockSpec((deep, 1), functools.partial(lambda key, i, ix: (key(ix), 0), key)) for key in keys]
    specs.append(by_tile(1, tile))
    args = [*([logits] * count), *([weights] * count), density]
    if before is not None:
        specs.append(by_tile(8, tile))
        args.append(before)
    rows = deep * count
    return call(
        functools.partial(exp_kernel, float(cents), count, before is None, last),
        "exp_parts",
        where,
        args,
        specs,
        (
            jax.ShapeDtypeStruct((rows, spots), BF),
            jax.ShapeDtypeStruct((rows, spots), BF),
            jax.ShapeDtypeStruct((8, spots), F32),
        ),
        (by_tile(rows, tile), by_tile(rows, tile), by_tile(8, tile)),
        (spots // tile,),
        [pltpu.VMEM((8, tile), F32)],
        limit=limit_of(rows),
    )


def turn_kernel(where, pick_ref, x_ref, *out_refs):
    high, low = split(x_ref[...])
    pick = pick_ref[...]
    value = dot(pick, high, NT) + dot(pick, low, NT)
    start = 0
    for out_ref in out_refs:
        out_ref[...] = value[start : start + out_ref.shape[0]]
        start += out_ref.shape[0]


def heights(genes):
    return [(b - a) * genes // NB for a, b in zip(XCUT, XCUT[1:])]


def turn(where, pick, x, tile):
    spots, genes = x.shape
    return call(
        turn_kernel,
        "turn",
        where,
        [pick, x],
        [fixed((genes, genes)), pl.BlockSpec((tile, genes), lambda i, ix: (i, 0))],
        tuple(jax.ShapeDtypeStruct((height, spots), F32) for height in heights(genes)),
        tuple(by_tile(height, tile) for height in heights(genes)),
        (spots // tile,),
    )


def of_batch(refs, batch, width):
    place = sum(batch >= cut for cut in XCUT[1:])
    start = (batch - XCUT[place]) * width
    return refs[place][start : start + width, :]


def load_left(refs, high, low):
    at = 0
    for ref in refs:
        wide = ref.shape[1]
        high[:, at : at + wide], low[:, at : at + wide] = split(ref[...])
        at += wide


def product(high, low, e_high, e_low):
    right = jnp.concatenate([ref[...] for ref in e_high], axis=0)
    value = dot(high[...], right) + dot(low[...], right)
    return value + dot(high[...], jnp.concatenate([ref[...] for ref in e_low], axis=0))


def pred_kernel(blocks, count, first, last, stats, where, *refs):
    s_refs, refs = refs[:blocks], refs[blocks:]
    h_refs, l_refs = refs[:count], refs[count : 2 * count]
    refs = refs[2 * count :]
    if not first:
        acc_ref, refs = refs[0], refs[1:]
    if last:
        zinfo_ref, refs = refs[0], refs[1:]
    if stats:
        x_refs, (out_ref, info_ref, high, low, sums) = refs[:XS], refs[XS:]
    else:
        out_ref, high, low = refs
    step = pl.program_id(0)
    genes, tile = out_ref.shape
    width = genes // NB

    @pl.when(step == 0)
    def _():
        load_left(s_refs, high, low)
        if stats:
            sums[...] = jnp.zeros_like(sums)
            info_ref[...] = jnp.zeros_like(info_ref)

    value = product(high, low, h_refs, l_refs)
    if not first:
        value = value + acc_ref[...]
    if last:
        value = value * zinfo_ref[0:1, :]
    out_ref[...] = value
    if not stats:
        return
    rows = [[], [], []]
    for batch in range(NB):
        at = slice(batch * width, (batch + 1) * width)
        pred, x = value[at], of_batch(x_refs, batch, width)
        for number, term in enumerate((pred * x, pred * pred, x * x)):
            rows[number].append(jnp.sum(term, axis=0, keepdims=True))
            lanes = term[:, :128]
            for group in range(1, tile // 128):
                lanes = lanes + term[:, group * 128 : group * 128 + 128]
            sums[number, at] += lanes
    info_ref[0 : 3 * NB, pl.ds(pl.multiple_of(step * tile, 128), tile)] = jnp.concatenate(
        rows[0] + rows[1] + rows[2], axis=0
    )

    @pl.when(step == pl.num_programs(0) - 1)
    def _():
        for number in range(3):
            info_ref[12:13, number * genes : (number + 1) * genes] = jnp.sum(
                sums[number].T, axis=0, keepdims=True
            )


def pred_part(where, blocks, terms, acc, zinfo, x, tile, name):
    spots = terms[0][0].shape[1]
    genes, deep = blocks[0].shape
    first, last, stats = acc is None, zinfo is not None, x is not None
    specs = [fixed((genes, deep)) for _ in blocks]
    specs += [by_tile(rows, tile, place) for _, _, rows, place in terms] * 2
    args = [*blocks, *(term[0] for term in terms), *(term[1] for term in terms)]
    alias = {}
    if not first:
        alias = {len(args) + 1: 0}
        specs.append(by_tile(genes, tile))
        args.append(acc)
    if last:
        specs.append(by_tile(8, tile))
        args.append(zinfo)
    shapes = jax.ShapeDtypeStruct((genes, spots), F32)
    outs = by_tile(genes, tile)
    scratch = [pltpu.VMEM((genes, deep * len(blocks)), BF)] * 2
    if stats:
        specs += [by_tile(height, tile) for height in heights(genes)]
        args += x
        shapes = (shapes, jax.ShapeDtypeStruct((16, spots), F32))
        outs = (outs, fixed_out((16, spots)))
        scratch.append(pltpu.VMEM((3, genes, 128), F32))
    return call(
        functools.partial(pred_kernel, len(blocks), len(terms), first, last, stats),
        name,
        where,
        args,
        specs,
        shapes,
        outs,
        (spots // tile,),
        scratch,
        alias,
        limit_of(deep * len(blocks)),
    )


def fixed_out(shape):
    return pl.BlockSpec(shape, lambda i, ix: (0,) * len(shape))


def emit_kernel(where, pred_ref, pick_ref, out_ref):
    high, low = split(pred_ref[...].T)
    pick = pick_ref[...]
    out_ref[...] = dot(high, pick) + dot(low, pick)


def emit(where, pred, pick, tile):
    genes, spots = pred.shape
    return call(
        emit_kernel,
        "emit",
        where,
        [pred, pick],
        [by_tile(genes, tile), fixed((genes, genes))],
        jax.ShapeDtypeStruct((spots, genes), F32),
        pl.BlockSpec((tile, genes), lambda i, ix: (i, 0)),
        (spots // tile,),
        limit=VMEM_LIMIT,
    )


def cosine(inner, left, right):
    left = left + EPS
    inv = lax.rsqrt(left) * lax.rsqrt(right + EPS)
    cos = inner * inv
    return cos, inv, cos / left


def pack_kernel(mine_ref, theirs_ref, core_ref, z_ref, out_ref, spot_ref):
    genes = out_ref.shape[1] // 2
    totals = (mine_ref[...] + theirs_ref[...]) + core_ref[...]
    spot_ref[...] = totals
    cos, _, _ = cosine(totals[0:NB], totals[NB : 2 * NB], totals[2 * NB : 3 * NB])
    out_ref[...] = jnp.zeros_like(out_ref)
    spots = z_ref.shape[1]
    for number in range(3):
        at = slice(number * genes, (number + 1) * genes)
        out_ref[number : number + 1, 0:genes] = mine_ref[12:13, at]
        out_ref[number : number + 1, genes : 2 * genes] = theirs_ref[12:13, at]
        out_ref[3 + number : 4 + number, 0:128] = z_ref[2 + number : 3 + number, spots - 128 :]
    out_ref[6:7, 0:128] = jnp.broadcast_to(
        jnp.sum(jnp.sum(cos, axis=0, keepdims=True), axis=1, keepdims=True), (1, 128)
    )


def pack(mine, theirs, core, zinfo, genes):
    return pl.pallas_call(
        pack_kernel,
        out_shape=(
            jax.ShapeDtypeStruct((8, 2 * genes), F32),
            jax.ShapeDtypeStruct(mine.shape, F32),
        ),
        compiler_params=pltpu.CompilerParams(vmem_limit_bytes=VMEM_LIMIT),
        cost_estimate=CHEAP,
        name="pack",
    )(mine, theirs, core, zinfo)


def rows_kernel(count, chosen, where, *refs):
    s_refs, (high_ref, low_ref, buffer, sem) = refs[:count], refs[count:]
    rows = high_ref.shape[0] // 2
    pieces = rows // KC
    for slot in range(2 * pieces):
        which = where[1 - slot // pieces]
        piece = slot % pieces
        if chosen is not None:
            for hit, ref in zip(chosen(where, which * pieces + piece), s_refs):

                @pl.when(hit)
                def _(ref=ref):
                    pltpu.make_async_copy(ref, buffer.at[slot], sem.at[slot]).start()

        else:
            at = pl.ds(pl.multiple_of(which * rows + piece * KC, KC), KC)
            pltpu.make_async_copy(s_refs[0].at[:, at], buffer.at[slot], sem.at[slot]).start()
    for slot in range(2 * pieces):
        pltpu.make_async_copy(s_refs[0].at[:, 0:KC], buffer.at[slot], sem.at[slot]).wait()
        at = slice(slot * KC, slot * KC + KC)
        high_ref[at, :], low_ref[at, :] = split(buffer[slot].T)


def rows_left(where, blocks, rows, chosen):
    genes = blocks[0].shape[0]
    shape = jax.ShapeDtypeStruct((2 * rows, genes), BF)
    slots = 2 * rows // KC
    return call(
        functools.partial(rows_kernel, len(blocks), chosen),
        "rows_left",
        where,
        list(blocks),
        [pl.BlockSpec(memory_space=pl.ANY)] * len(blocks),
        (shape, shape),
        (fixed_out((2 * rows, genes)), fixed_out((2 * rows, genes))),
        (1,),
        [pltpu.VMEM((slots, genes, KC), F32), pltpu.SemaphoreType.DMA((slots,))],
        limit=VMEM_LIMIT,
    )


def back_dots(high_refs, low_refs, bhigh, blow, genes):
    value = None
    for part in range(2):
        at = slice(part * genes, (part + 1) * genes)
        one = dot(high_refs[part][...], bhigh[at]) + dot(low_refs[part][...], bhigh[at])
        one = one + dot(high_refs[part][...], blow[at])
        value = one if value is None else value + one
    return value


def back_sum_kernel(blocks, count, first, sizes, where, *refs):
    batch_scale, gene_scale = sizes
    s_refs, h_refs, l_refs = refs[:blocks], refs[blocks : blocks + count], refs[blocks + count : blocks + 2 * count]
    refs = refs[blocks + 2 * count :]
    if not first:
        acc_ref, refs = refs[0], refs[1:]
    z_ref, own_ref, x_refs, refs = refs[0], refs[1], refs[2 : 2 + 2 * XS], refs[2 + 2 * XS :]
    high_refs, low_refs = refs[0:2], refs[2:4]
    totals_ref, more_ref, spot_ref, out_ref, bhigh, blow, sum_ref, coef, other_ref, high, low = refs[4:]
    pred_refs = (own_ref, other_ref)
    genes, tile = own_ref.shape
    rows = high_refs[0].shape[0]
    width = genes // NB

    @pl.when(pl.program_id(0) == 0)
    def _():
        load_left(s_refs, high, low)
        totals = totals_ref[...] + more_ref[...]
        gene_cos, inv_gene, over_gene = cosine(totals[0:1], totals[1:2], totals[2:3])
        coef[0] = jnp.broadcast_to(-gene_scale * inv_gene, (128, 2 * genes)).T
        coef[1] = jnp.broadcast_to(gene_scale * over_gene, (128, 2 * genes)).T
        cos = jnp.broadcast_to(jnp.sum(gene_cos, axis=1, keepdims=True), (1, 128))
        sum_ref[...] = jnp.concatenate([totals[3:7, 0:128], cos, jnp.zeros((3, 128), F32)], axis=0)

    other = product(high, low, h_refs, l_refs)
    if not first:
        other = other + acc_ref[...]
    other_ref[...] = other * z_ref[0:1, :]
    spot = spot_ref[...]
    _, inv_spot, over_spot = cosine(spot[0:NB], spot[NB : 2 * NB], spot[2 * NB : 3 * NB])
    column = jnp.zeros((1, tile), F32)
    for part in range(2):
        for batch in range(NB):
            at = slice(batch * width, (batch + 1) * width)
            here = slice(part * genes + batch * width, part * genes + (batch + 1) * width)
            x_by = jnp.concatenate([coef[0, here]] * (tile // 128), axis=1) - (
                batch_scale * inv_spot[batch : batch + 1]
            )
            p_by = jnp.concatenate([coef[1, here]] * (tile // 128), axis=1) + (
                batch_scale * over_spot[batch : batch + 1]
            )
            pred = pred_refs[part][at, :]
            grad = of_batch(x_refs[part * XS :], batch, width) * x_by + pred * p_by
            bhigh[here], blow[here] = split(grad)
            column = column + jnp.sum(pred * grad, axis=0, keepdims=True)
    out_ref[0:rows] = back_dots(high_refs, low_refs, bhigh, blow, genes)
    out_ref[rows : rows + 1] = column
    out_ref[rows + 1 : rows + 2] = jnp.concatenate([sum_ref[4:5]] * (tile // 128), axis=1)
    out_ref[rows + 2 : rows + 8] = jnp.zeros((6, tile), F32)


def back_sum(where, blocks, terms, acc, zinfo, own, xs, lefts, totals, more, spot, consts, rows, tile):
    genes, spots = own.shape
    deep = blocks[0].shape[1]
    left = pl.BlockSpec((rows, genes), lambda i, ix: (0, 0), pipeline_mode=pl.Buffered(1))
    specs = [fixed((genes, deep)) for _ in blocks]
    specs += [by_tile(height, tile, place) for _, _, height, place in terms] * 2
    args = [*blocks, *(term[0] for term in terms), *(term[1] for term in terms)]
    if acc is not None:
        specs.append(by_tile(genes, tile))
        args.append(acc)
    specs += [by_tile(8, tile), by_tile(genes, tile)] + [by_tile(height, tile) for height in heights(genes)] * 2
    specs += [left] * 4 + [fixed((8, 2 * genes))] * 2 + [by_tile(16, tile)]
    args += [zinfo, own, *xs, lefts[0][0], lefts[1][0], lefts[0][1], lefts[1][1], totals, more, spot]
    return call(
        functools.partial(back_sum_kernel, len(blocks), len(terms), acc is None, consts[:2]),
        "back_sum",
        where,
        args,
        specs,
        (
            jax.ShapeDtypeStruct((rows + 8, spots), F32),
            jax.ShapeDtypeStruct((2 * genes, spots), BF),
            jax.ShapeDtypeStruct((2 * genes, spots), BF),
            jax.ShapeDtypeStruct((8, 128), F32),
        ),
        (by_tile(rows + 8, tile), by_tile(2 * genes, tile), by_tile(2 * genes, tile), fixed_out((8, 128))),
        (spots // tile,),
        [
            pltpu.VMEM((2, 2 * genes, 128), F32),
            pltpu.VMEM((genes, tile), F32),
            pltpu.VMEM((genes, deep * len(blocks)), BF),
            pltpu.VMEM((genes, deep * len(blocks)), BF),
        ],
        limit=limit_of(deep * len(blocks)),
    )


def back_end_kernel(sizes, where, *refs):
    scale, (gene_loss, spot_loss, cents, spots_all) = sizes
    high_refs, low_refs = refs[0:2], refs[2:4]
    bhigh, blow, sum_ref, z_ref, dens_ref, sent_ref, got_ref, logit_ref, w_ref, out_ref, loss_ref = refs[4:]
    rows, genes = high_refs[0].shape
    value = back_dots(high_refs, low_refs, bhigh, blow, genes)
    inv, raw = z_ref[0:1, :], z_ref[1:2, :]
    dens, mass = sum_ref[0:1, 0:1], sum_ref[1:2, 0:1]
    grad_raw = scale * (1.0 / mass - dens_ref[...] / (dens * raw))
    column = sent_ref[0:1, :] + got_ref[rows : rows + 1, :] + raw * grad_raw
    value = value + got_ref[0:rows, :] + w_ref[...] * grad_raw
    out_ref[...] = jnp.exp(logit_ref[...]) * inv * (value - column)

    @pl.when(pl.program_id(0) == 0)
    def _():
        dens, mass, log_sum, cos = (sum_ref[k : k + 1] for k in range(4))
        gene = (sum_ref[4:5] + got_ref[rows + 1 : rows + 2, 0:128]) * gene_loss
        kl = log_sum / dens + jnp.log(mass * (cents / spots_all)) - jnp.log(dens * (1.0 / spots_all))
        for number, term in enumerate((gene, cos * spot_loss, kl)):
            loss_ref[number] = term[0, 0]


def back_end(where, highs, lefts, sums, zinfo, density, sent, got, logits, weights, consts, rows, tile):
    twice, spots = highs[0].shape
    left = pl.BlockSpec((rows, twice // 2), lambda i, ix: (1, 0), pipeline_mode=pl.Buffered(1))
    specs = [left] * 4 + [by_tile(twice, tile)] * 2
    specs += [fixed((8, 128)), by_tile(8, tile), by_tile(1, tile), by_tile(8, tile, rows // 8), by_tile(rows + 8, tile)]
    specs += [
        pl.BlockSpec((rows, tile), lambda i, ix: (ix[0], i)),
        pl.BlockSpec((rows, 1), lambda i, ix: (ix[0], 0)),
    ]
    args = [lefts[0][0], lefts[1][0], lefts[0][1], lefts[1][1], *highs]
    args += [sums, zinfo, density, sent, got, logits, weights]
    return call(
        functools.partial(back_end_kernel, consts[2:]),
        "back_end",
        where,
        args,
        specs,
        (jax.ShapeDtypeStruct((rows, spots), F32), jax.ShapeDtypeStruct((3,), F32)),
        (by_tile(rows, tile), pl.BlockSpec(memory_space=pltpu.SMEM)),
        (spots // tile,),
        limit=VMEM_LIMIT,
    )


def swap(value, axis, bit):
    return lax.ppermute(value, axis, [(i, i ^ bit) for i in range(lax.axis_size(axis))])


def after(value, *others):
    return lax.optimization_barrier((value, *others))[0]


def tie(*values):
    return lax.optimization_barrier(values)


def local(logits, centroid_expr, spatial, cluster_cells, density, gene_order):
    n_spot = lax.axis_size("spot")
    n_gene = lax.axis_size("gene")
    me = lax.axis_index("spot")
    col = lax.axis_index("gene")
    cents, spots = logits.shape
    genes = spatial.shape[1]
    genes_all = genes * n_gene
    spots_all = spots * n_spot
    rows = cents // n_gene
    scale = float(spots_all * cents)
    consts = (
        scale / (NB * spots_all),
        scale / genes_all,
        scale,
        (-1.0 / genes_all, -1.0 / (NB * spots_all), float(cents), float(spots_all)),
    )
    ring = n_spot == 8 and cents // n_spot == KC
    where = jnp.stack([col, col ^ 1, me]).astype(jnp.int32)
    tile = 512

    order = (gene_order - col * genes).reshape(genes, 1)
    pick = order == lax.broadcasted_iota(jnp.int32, (genes, genes), 1)
    mine = lax.dot_general(
        pick.astype(F32), centroid_expr, NT, precision=lax.Precision.HIGH, preferred_element_type=F32
    )
    pick = pick.astype(BF)
    theirs = swap(mine, "gene", 2)
    weights = cluster_cells.astype(F32)
    weights = (weights / jnp.sum(weights)).reshape(cents, 1)
    dens_row = density.reshape(1, spots)
    fwd = lambda name, blocks, terms, acc, scale_by, x: pred_part(
        where, blocks, terms, acc, scale_by, x, tile, name
    )
    if ring:
        hop = lambda block, bit: swap(block, "spot", bit)
        send = lambda one, *others: swap(after(one, *others), "gene", 2)
        keys = lambda *order: [functools.partial(lambda k, ix: ix[2] ^ k, k) for k in order]
        o1, o2, oy = [hop(mine, bit) for bit in (2, 4, 1)]
        x_own = list(turn(where, pick, spatial, 2 * tile))
        x_own[0], oy = tie(x_own[0], oy)
        x0 = send(x_own[0])
        logits, *x_own = tie(logits, *x_own)
        *e_one, z_one = exp_parts(where, keys(0, 1, 2, 4), KC, logits, weights, dens_row, None, False, 2 * tile)
        o1, oy, o2, theirs, z_one, *x_own = tie(o1, oy, o2, theirs, z_one, *x_own)
        o2y, o3 = hop(o2, 1), hop(o2, 2)
        acc = fwd("own_early", [mine, oy, o1, o2], [(*e_one, 4 * KC, 0)], None, None, None)
        acc, o2y, o3, oy, theirs, z_one, logits = tie(acc, o2y, o3, oy, theirs, z_one, logits)
        o3y, o1y, ty = hop(o3, 1), hop(oy, 2), hop(theirs, 1)
        *e_two, zinfo = exp_parts(where, keys(3, 5, 6, 7), KC, logits, weights, dens_row, z_one, True, 2 * tile)
        acc, o3y, o1y, theirs, zinfo, held = tie(acc, o3y, o1y, theirs, zinfo, x_own[1])
        t1, t2, x1 = hop(theirs, 2), hop(theirs, 4), send(held)
        pred_own, info = fwd("own_late", [o1y, o2y, o3, o3y], [(*e_two, 4 * KC, 0)], acc, zinfo, x_own)
        own = [mine, oy, o1, o1y, o2, o2y, o3, o3y]
        own_pick = lambda ix, block: [(block ^ ix[2]) == key for key in range(n_spot)]
    else:
        x_own = turn(where, pick, spatial, 2 * tile)
        x_got = [swap(one, "gene", 2) for one in x_own]
        *e_all, zinfo = exp_parts(where, [lambda ix: 0], cents, logits, weights, dens_row, None, True, tile)
        own = [lax.all_gather(mine, "spot", axis=1, tiled=True)]
        other = [lax.all_gather(theirs, "spot", axis=1, tiled=True)]
        whole = [(*e_all, cents, 0)]
        pred_own, info = fwd("own_late", own, whole, None, zinfo, x_own)
        own_pick = None

    info_x = swap(info, "gene", 2)
    if ring:
        pred_own, t1, ty, t2, theirs, x0 = tie(pred_own, t1, ty, t2, theirs, x0)
        t2y, t3 = hop(t2, 1), hop(t2, 2)
        acc_other = fwd("other_mid", [theirs, ty, t1, t2], [(*e_one, 4 * KC, 0)], None, None, None)
        acc_other, t2y, t3, t1, x1, held, info_x = tie(acc_other, t2y, t3, t1, x1, x_own[2], info_x)
        x2, t3y, t1y = send(held), hop(t2y, 2), hop(t1, 1)
        x_got = [x0, x1, x2]
    totals, spot = pack(info, info_x, swap(info + info_x, "gene", 1), zinfo, genes)
    if ring:
        got = swap(totals, "spot", 1)
        acc_other, totals = tie(acc_other, totals)
        acc_other = fwd("other_more", [t2y, t3], [(*e_two, KC, 1), (*e_two, KC, 2)], acc_other, None, None)
        acc_other, got, mine = tie(acc_other, got, mine)
        totals = totals + got
        got = swap(totals, "spot", 2)
        own[0] = mine
        left_own = rows_left(where, own, rows, own_pick)
        left_own, got, t1y, t3y = tie(left_own, got, t1y, t3y)
        totals = totals + got
        more = swap(totals, "spot", 4)
        other = [theirs, ty, t1, t1y, t2, t2y, t3, t3y]
        last = ([t1y, t3y], [(*e_two, KC, 0), (*e_two, KC, 3)], acc_other)
    else:
        totals = lax.psum(totals, "spot")
        more = jnp.zeros_like(totals)
        left_own = rows_left(where, own, rows, own_pick)
        last = (other, whole, None)
    left_other = rows_left(where, other, rows, own_pick)
    if ring:
        left_other, more = tie(left_other, more)

    lefts = (left_own, left_other)
    sent, *highs, sums = back_sum(
        where, *last, zinfo, pred_own, (*x_own, *x_got), lefts, totals, more, spot, consts, rows, tile
    )
    got = swap(sent, "gene", 1)
    predicted = emit(where, after(pred_own, sent), pick, 2 * tile)
    predicted, got = tie(predicted, got)
    grad, loss = back_end(
        where, highs, lefts, sums, zinfo, dens_row, sent, got, logits, weights, consts, rows, tile
    )
    return loss, predicted, grad


def solution(mesh):
    return jax.shard_map(
        local,
        mesh=mesh,
        in_specs=(P(None, "spot"), P("spot", "gene"), P("spot", "gene"), P(), P("spot"), P("gene")),
        out_specs=(P(), P("spot", "gene"), P("gene", "spot")),
        check_vma=False,
    )
```

```python
import functools
import jax
import jax.numpy as jnp
from jax import lax
from jax.experimental import pallas as pl
from jax.experimental.pallas import tpu as pltpu
from jax.sharding import PartitionSpec as P

NB = 4
XS = 3
XCUT = (0, 2, 3, NB)
EPS = 1e-06
BF = jnp.bfloat16
F32 = jnp.float32
KC = 256
NT = (((1,), (1,)), ((), ()))
TN = (((0,), (0,)), ((), ()))
VMEM_LIMIT = 24 << 20
LARGE_LIMIT = 60 << 20
CHEAP = pl.CostEstimate(flops=1000, bytes_accessed=1000, transcendentals=0)


def split(value):
    high = value.astype(BF)
    return high, (value - high.astype(F32)).astype(BF)


def dot(left, right, dims=(((1,), (0,)), ((), ()))):
    return lax.dot_general(left, right, dims, preferred_element_type=F32)


def call(kernel, name, where, args, specs, out_shape, out_specs, grid, scratch=(), alias=None, limit=VMEM_LIMIT):
    return pl.pallas_call(
        kernel,
        out_shape=out_shape,
        grid_spec=pltpu.PrefetchScalarGridSpec(
            num_scalar_prefetch=1,
            grid=grid,
            in_specs=specs,
            out_specs=out_specs,
            scratch_shapes=list(scratch),
        ),
        input_output_aliases=alias or {},
        compiler_params=pltpu.CompilerParams(
            dimension_semantics=("arbitrary",), vmem_limit_bytes=limit
        ),
        cost_estimate=CHEAP,
        name=name,
    )(where, *args)


def limit_of(depth):
    return VMEM_LIMIT if depth <= 5 * KC else LARGE_LIMIT


def off_chip(value):
    return pltpu.with_memory_space_constraint(value, pltpu.HBM)


def fixed(shape):
    return pl.BlockSpec(shape, lambda i, ix: (0,) * len(shape), pipeline_mode=pl.Buffered(1))


def by_tile(height, tile, row=0, start=0):
    return pl.BlockSpec((height, tile), lambda i, ix: (row, i + start))


def exp_kernel(cents, count, first, last, where, *refs):
    l_refs, w_refs, d_ref, refs = refs[:count], refs[count : 2 * count], refs[2 * count], refs[2 * count + 1 :]
    if not first:
        before_ref, refs = refs[0], refs[1:]
    high_ref, low_ref, info_ref, scal = refs
    step = pl.program_id(0)
    tile = d_ref.shape[1]

    @pl.when(step == 0)
    def _():
        scal[...] = jnp.zeros_like(scal)

    if first:
        total = weighted = jnp.zeros((1, tile), F32)
    else:
        total, weighted = before_ref[0:1, :], before_ref[1:2, :]
    start = 0
    for l_ref, w_ref in zip(l_refs, w_refs):
        for part in range(l_ref.shape[0] // KC):
            rows = slice(part * KC, part * KC + KC)
            value = jnp.exp(l_ref[rows, :])
            high, low = split(value)
            high_ref[start : start + KC, :] = high
            low_ref[start : start + KC, :] = low
            start += KC
            total = total + jnp.sum(value, axis=0, keepdims=True)
            weighted = weighted + jnp.sum(value * w_ref[rows, :], axis=0, keepdims=True)
    if not last:
        info_ref[...] = jnp.concatenate([total, weighted, jnp.zeros((6, tile), F32)], axis=0)
        return
    inv = 1.0 / total
    raw = weighted * inv
    dens = d_ref[...]
    scal[0:1] += dens
    scal[1:2] += raw
    scal[2:3] += dens * (jnp.log(dens) - jnp.log(raw * cents))
    sums = jnp.broadcast_to(jnp.sum(scal[...], axis=1, keepdims=True), (8, tile))
    info_ref[0:1, :] = inv
    info_ref[1:2, :] = raw
    info_ref[2:8, :] = sums[0:6]


def exp_parts(where, keys, deep, logits, weights, density, before, last, tile):
    cents, spots = logits.shape
    count = len(keys)
    specs = [
        pl.BlockSpec((deep, tile), functools.partial(lambda key, i, ix: (key(ix), i), key)) for key in keys
    ]
    specs += [pl.BlockSpec((deep, 1), functools.partial(lambda key, i, ix: (key(ix), 0), key)) for key in keys]
    specs.append(by_tile(1, tile))
    args = [*([off_chip(logits)] * count), *([weights] * count), density]
    if before is not None:
        specs.append(by_tile(8, tile))
        args.append(before)
    rows = deep * count
    return call(
        functools.partial(exp_kernel, float(cents), count, before is None, last),
        "exp_parts",
        where,
        args,
        specs,
        (
            jax.ShapeDtypeStruct((rows, spots), BF),
            jax.ShapeDtypeStruct((rows, spots), BF),
            jax.ShapeDtypeStruct((8, spots), F32),
        ),
        (by_tile(rows, tile), by_tile(rows, tile), by_tile(8, tile)),
        (spots // tile,),
        [pltpu.VMEM((8, tile), F32)],
        limit=limit_of(rows),
    )


def turn_kernel(where, pick_ref, x_ref, *out_refs):
    high, low = split(x_ref[...])
    pick = pick_ref[...]
    value = dot(pick, high, NT) + dot(pick, low, NT)
    start = 0
    for out_ref in out_refs:
        out_ref[...] = value[start : start + out_ref.shape[0]]
        start += out_ref.shape[0]


def heights(genes):
    return [(b - a) * genes // NB for a, b in zip(XCUT, XCUT[1:])]


def turn(where, pick, x, tile):
    spots, genes = x.shape
    return call(
        turn_kernel,
        "turn",
        where,
        [pick, off_chip(x)],
        [fixed((genes, genes)), pl.BlockSpec((tile, genes), lambda i, ix: (i, 0))],
        tuple(jax.ShapeDtypeStruct((height, spots), F32) for height in heights(genes)),
        tuple(by_tile(height, tile) for height in heights(genes)),
        (spots // tile,),
    )


def of_batch(refs, batch, width):
    place = sum(batch >= cut for cut in XCUT[1:])
    start = (batch - XCUT[place]) * width
    return refs[place][start : start + width, :]


def load_left(refs, high, low):
    at = 0
    for ref in refs:
        wide = ref.shape[1]
        high[:, at : at + wide], low[:, at : at + wide] = split(ref[...])
        at += wide


def product(high, low, e_high, e_low):
    right = jnp.concatenate([ref[...] for ref in e_high], axis=0)
    value = dot(high[...], right) + dot(low[...], right)
    return value + dot(high[...], jnp.concatenate([ref[...] for ref in e_low], axis=0))


def pred_kernel(blocks, count, first, last, stats, where, *refs):
    s_refs, refs = refs[:blocks], refs[blocks:]
    h_refs, l_refs = refs[:count], refs[count : 2 * count]
    refs = refs[2 * count :]
    if not first:
        acc_ref, refs = refs[0], refs[1:]
    if last:
        zinfo_ref, refs = refs[0], refs[1:]
    if stats:
        x_refs, (out_ref, info_ref, high, low, sums) = refs[:XS], refs[XS:]
    else:
        out_ref, high, low = refs
    step = pl.program_id(0)
    genes, tile = out_ref.shape
    width = genes // NB

    @pl.when(step == 0)
    def _():
        load_left(s_refs, high, low)
        if stats:
            sums[...] = jnp.zeros_like(sums)
            info_ref[...] = jnp.zeros_like(info_ref)

    value = product(high, low, h_refs, l_refs)
    if not first:
        value = value + acc_ref[...]
    if last:
        value = value * zinfo_ref[0:1, :]
    out_ref[...] = value
    if not stats:
        return
    rows = [[], [], []]
    for batch in range(NB):
        at = slice(batch * width, (batch + 1) * width)
        pred, x = value[at], of_batch(x_refs, batch, width)
        for number, term in enumerate((pred * x, pred * pred, x * x)):
            rows[number].append(jnp.sum(term, axis=0, keepdims=True))
            lanes = term[:, :128]
            for group in range(1, tile // 128):
                lanes = lanes + term[:, group * 128 : group * 128 + 128]
            sums[number, at] += lanes
    info_ref[0 : 3 * NB, pl.ds(pl.multiple_of(step * tile, 128), tile)] = jnp.concatenate(
        rows[0] + rows[1] + rows[2], axis=0
    )

    @pl.when(step == pl.num_programs(0) - 1)
    def _():
        for number in range(3):
            info_ref[12:13, number * genes : (number + 1) * genes] = jnp.sum(
                sums[number].T, axis=0, keepdims=True
            )


def pred_part(where, blocks, terms, acc, zinfo, x, tile, name):
    spots = terms[0][0].shape[1]
    genes, deep = blocks[0].shape
    first, last, stats = acc is None, zinfo is not None, x is not None
    kept = stats or not first
    specs = [fixed((genes, deep)) for _ in blocks]
    specs += [by_tile(rows, tile, place) for _, _, rows, place in terms] * 2
    args = [*blocks, *(term[0] for term in terms), *(term[1] for term in terms)]
    alias = {}
    if not first:
        specs.append(by_tile(genes, tile))
        args.append(acc)
    if last:
        specs.append(by_tile(8, tile))
        args.append(zinfo)
    shapes = pltpu.HBM((genes, spots), F32) if kept else jax.ShapeDtypeStruct((genes, spots), F32)
    outs = by_tile(genes, tile)
    scratch = [pltpu.VMEM((genes, deep * len(blocks)), BF)] * 2
    if stats:
        specs += [by_tile(height, tile) for height in heights(genes)]
        args += x
        shapes = (shapes, jax.ShapeDtypeStruct((16, spots), F32))
        outs = (outs, fixed_out((16, spots)))
        scratch.append(pltpu.VMEM((3, genes, 128), F32))
    return call(
        functools.partial(pred_kernel, len(blocks), len(terms), first, last, stats),
        name,
        where,
        args,
        specs,
        shapes,
        outs,
        (spots // tile,),
        scratch,
        alias,
        limit_of(deep * len(blocks)),
    )


def fixed_out(shape):
    return pl.BlockSpec(shape, lambda i, ix: (0,) * len(shape))


def emit_kernel(where, pred_ref, pick_ref, out_ref):
    high, low = split(pred_ref[...].T)
    pick = pick_ref[...]
    out_ref[...] = dot(high, pick) + dot(low, pick)


def emit(where, pred, pick, tile):
    genes, spots = pred.shape
    return call(
        emit_kernel,
        "emit",
        where,
        [off_chip(pred), pick],
        [by_tile(genes, tile), fixed((genes, genes))],
        jax.ShapeDtypeStruct((spots, genes), F32),
        pl.BlockSpec((tile, genes), lambda i, ix: (i, 0)),
        (spots // tile,),
        limit=VMEM_LIMIT,
    )


def cosine(inner, left, right):
    left = left + EPS
    inv = lax.rsqrt(left) * lax.rsqrt(right + EPS)
    cos = inner * inv
    return cos, inv, cos / left


def pack_kernel(mine_ref, theirs_ref, core_ref, z_ref, out_ref, spot_ref):
    genes = out_ref.shape[1] // 2
    totals = (mine_ref[...] + theirs_ref[...]) + core_ref[...]
    spot_ref[...] = totals
    cos, _, _ = cosine(totals[0:NB], totals[NB : 2 * NB], totals[2 * NB : 3 * NB])
    out_ref[...] = jnp.zeros_like(out_ref)
    spots = z_ref.shape[1]
    for number in range(3):
        at = slice(number * genes, (number + 1) * genes)
        out_ref[number : number + 1, 0:genes] = mine_ref[12:13, at]
        out_ref[number : number + 1, genes : 2 * genes] = theirs_ref[12:13, at]
        out_ref[3 + number : 4 + number, 0:128] = z_ref[2 + number : 3 + number, spots - 128 :]
    out_ref[6:7, 0:128] = jnp.broadcast_to(
        jnp.sum(jnp.sum(cos, axis=0, keepdims=True), axis=1, keepdims=True), (1, 128)
    )


def pack(mine, theirs, core, zinfo, genes):
    return pl.pallas_call(
        pack_kernel,
        out_shape=(
            jax.ShapeDtypeStruct((8, 2 * genes), F32),
            jax.ShapeDtypeStruct(mine.shape, F32),
        ),
        compiler_params=pltpu.CompilerParams(vmem_limit_bytes=VMEM_LIMIT),
        cost_estimate=CHEAP,
        name="pack",
    )(mine, theirs, core, zinfo)


def rows_kernel(count, chosen, where, *refs):
    s_refs, (high_ref, low_ref, buffer, sem) = refs[:count], refs[count:]
    rows = high_ref.shape[0] // 2
    pieces = rows // KC
    for slot in range(2 * pieces):
        which = where[1 - slot // pieces]
        piece = slot % pieces
        if chosen is not None:
            for hit, ref in zip(chosen(where, which * pieces + piece), s_refs):

                @pl.when(hit)
                def _(ref=ref):
                    pltpu.make_async_copy(ref, buffer.at[slot], sem.at[slot]).start()

        else:
            at = pl.ds(pl.multiple_of(which * rows + piece * KC, KC), KC)
            pltpu.make_async_copy(s_refs[0].at[:, at], buffer.at[slot], sem.at[slot]).start()
    for slot in range(2 * pieces):
        pltpu.make_async_copy(s_refs[0].at[:, 0:KC], buffer.at[slot], sem.at[slot]).wait()
        at = slice(slot * KC, slot * KC + KC)
        high_ref[at, :], low_ref[at, :] = split(buffer[slot].T)


def rows_left(where, blocks, rows, chosen):
    genes = blocks[0].shape[0]
    shape = jax.ShapeDtypeStruct((2 * rows, genes), BF)
    slots = 2 * rows // KC
    return call(
        functools.partial(rows_kernel, len(blocks), chosen),
        "rows_left",
        where,
        list(blocks),
        [pl.BlockSpec(memory_space=pl.ANY)] * len(blocks),
        (shape, shape),
        (fixed_out((2 * rows, genes)), fixed_out((2 * rows, genes))),
        (1,),
        [pltpu.VMEM((slots, genes, KC), F32), pltpu.SemaphoreType.DMA((slots,))],
        limit=VMEM_LIMIT,
    )


def back_dots(high_refs, low_refs, bhigh, blow, genes):
    value = None
    for part in range(2):
        at = slice(part * genes, (part + 1) * genes)
        one = dot(high_refs[part][...], bhigh[at]) + dot(low_refs[part][...], bhigh[at])
        one = one + dot(high_refs[part][...], blow[at])
        value = one if value is None else value + one
    return value


def back_sum_kernel(blocks, count, first, sizes, where, *refs):
    batch_scale, gene_scale = sizes
    s_refs, h_refs, l_refs = refs[:blocks], refs[blocks : blocks + count], refs[blocks + count : blocks + 2 * count]
    refs = refs[blocks + 2 * count :]
    if not first:
        acc_ref, refs = refs[0], refs[1:]
    z_ref, own_ref, x_refs, refs = refs[0], refs[1], refs[2 : 2 + 2 * XS], refs[2 + 2 * XS :]
    high_refs, low_refs = refs[0:2], refs[2:4]
    totals_ref, more_ref, spot_ref, out_ref, bhigh, blow, sum_ref, coef, other_ref, high, low = refs[4:]
    pred_refs = (own_ref, other_ref)
    genes, tile = own_ref.shape
    rows = high_refs[0].shape[0]
    width = genes // NB

    @pl.when(pl.program_id(0) == 0)
    def _():
        load_left(s_refs, high, low)
        totals = totals_ref[...] + more_ref[...]
        gene_cos, inv_gene, over_gene = cosine(totals[0:1], totals[1:2], totals[2:3])
        coef[0] = jnp.broadcast_to(-gene_scale * inv_gene, (128, 2 * genes)).T
        coef[1] = jnp.broadcast_to(gene_scale * over_gene, (128, 2 * genes)).T
        cos = jnp.broadcast_to(jnp.sum(gene_cos, axis=1, keepdims=True), (1, 128))
        sum_ref[...] = jnp.concatenate([totals[3:7, 0:128], cos, jnp.zeros((3, 128), F32)], axis=0)

    other = product(high, low, h_refs, l_refs)
    if not first:
        other = other + acc_ref[...]
    other_ref[...] = other * z_ref[0:1, :]
    spot = spot_ref[...]
    _, inv_spot, over_spot = cosine(spot[0:NB], spot[NB : 2 * NB], spot[2 * NB : 3 * NB])
    column = jnp.zeros((1, tile), F32)
    for part in range(2):
        for batch in range(NB):
            at = slice(batch * width, (batch + 1) * width)
            here = slice(part * genes + batch * width, part * genes + (batch + 1) * width)
            x_by = jnp.concatenate([coef[0, here]] * (tile // 128), axis=1) - (
                batch_scale * inv_spot[batch : batch + 1]
            )
            p_by = jnp.concatenate([coef[1, here]] * (tile // 128), axis=1) + (
                batch_scale * over_spot[batch : batch + 1]
            )
            pred = pred_refs[part][at, :]
            grad = of_batch(x_refs[part * XS :], batch, width) * x_by + pred * p_by
            bhigh[here], blow[here] = split(grad)
            column = column + jnp.sum(pred * grad, axis=0, keepdims=True)
    out_ref[0:rows] = back_dots(high_refs, low_refs, bhigh, blow, genes)
    out_ref[rows : rows + 1] = column
    out_ref[rows + 1 : rows + 2] = jnp.concatenate([sum_ref[4:5]] * (tile // 128), axis=1)
    out_ref[rows + 2 : rows + 8] = jnp.zeros((6, tile), F32)


def back_sum(where, blocks, terms, acc, zinfo, own, xs, lefts, totals, more, spot, consts, rows, tile):
    genes, spots = own.shape
    deep = blocks[0].shape[1]
    left = pl.BlockSpec((rows, genes), lambda i, ix: (0, 0), pipeline_mode=pl.Buffered(1))
    specs = [fixed((genes, deep)) for _ in blocks]
    specs += [by_tile(height, tile, place) for _, _, height, place in terms] * 2
    args = [*blocks, *(term[0] for term in terms), *(term[1] for term in terms)]
    if acc is not None:
        specs.append(by_tile(genes, tile))
        args.append(off_chip(acc))
    specs += [by_tile(8, tile), by_tile(genes, tile)] + [by_tile(height, tile) for height in heights(genes)] * 2
    specs += [left] * 4 + [fixed((8, 2 * genes))] * 2 + [by_tile(16, tile)]
    args += [zinfo, off_chip(own), *xs, lefts[0][0], lefts[1][0], lefts[0][1], lefts[1][1], totals, more, spot]
    return call(
        functools.partial(back_sum_kernel, len(blocks), len(terms), acc is None, consts[:2]),
        "back_sum",
        where,
        args,
        specs,
        (
            jax.ShapeDtypeStruct((rows + 8, spots), F32),
            jax.ShapeDtypeStruct((2 * genes, spots), BF),
            jax.ShapeDtypeStruct((2 * genes, spots), BF),
            jax.ShapeDtypeStruct((8, 128), F32),
        ),
        (by_tile(rows + 8, tile), by_tile(2 * genes, tile), by_tile(2 * genes, tile), fixed_out((8, 128))),
        (spots // tile,),
        [
            pltpu.VMEM((2, 2 * genes, 128), F32),
            pltpu.VMEM((genes, tile), F32),
            pltpu.VMEM((genes, deep * len(blocks)), BF),
            pltpu.VMEM((genes, deep * len(blocks)), BF),
        ],
        limit=limit_of(deep * len(blocks)),
    )


def back_own_kernel(scale, where, *refs):
    high_refs, low_refs = refs[0:2], refs[2:4]
    bhigh, blow, sum_ref, z_ref, dens_ref, sent_ref, w_ref, out_ref = refs[4:]
    rows, genes = high_refs[0].shape
    value = back_dots(high_refs, low_refs, bhigh, blow, genes)
    raw = z_ref[1:2, :]
    dens, mass = sum_ref[0:1, 0:1], sum_ref[1:2, 0:1]
    grad_raw = scale * (1.0 / mass - dens_ref[...] / (dens * raw))
    out_ref[...] = value + w_ref[...] * grad_raw - (sent_ref[0:1, :] + raw * grad_raw)


def back_own(where, highs, lefts, sums, zinfo, density, sent, weights, scale, rows, tile):
    twice, spots = highs[0].shape
    left = pl.BlockSpec((rows, twice // 2), lambda i, ix: (1, 0), pipeline_mode=pl.Buffered(1))
    specs = [left] * 4 + [by_tile(twice, tile)] * 2
    specs += [fixed((8, 128)), by_tile(8, tile), by_tile(1, tile), by_tile(8, tile, rows // 8)]
    specs.append(pl.BlockSpec((rows, 1), lambda i, ix: (ix[0], 0)))
    args = [lefts[0][0], lefts[1][0], lefts[0][1], lefts[1][1], *highs]
    args += [sums, zinfo, density, off_chip(sent), weights]
    return call(
        functools.partial(back_own_kernel, scale),
        "back_own",
        where,
        args,
        specs,
        jax.ShapeDtypeStruct((rows, spots), F32),
        by_tile(rows, tile),
        (spots // tile,),
        limit=VMEM_LIMIT,
    )


def back_end_kernel(loss_scale, where, mine_ref, got_ref, logit_ref, z_ref, sum_ref, out_ref, loss_ref):
    gene_loss, spot_loss, cents, spots_all = loss_scale
    rows = out_ref.shape[0]
    value = mine_ref[...] + got_ref[0:rows, :] - got_ref[rows : rows + 1, :]
    out_ref[...] = jnp.exp(logit_ref[...]) * z_ref[0:1, :] * value

    @pl.when(pl.program_id(0) == 0)
    def _():
        dens, mass, log_sum, cos = (sum_ref[k : k + 1] for k in range(4))
        gene = (sum_ref[4:5] + got_ref[rows + 1 : rows + 2, 0:128]) * gene_loss
        kl = log_sum / dens + jnp.log(mass * (cents / spots_all)) - jnp.log(dens * (1.0 / spots_all))
        for number, term in enumerate((gene, cos * spot_loss, kl)):
            loss_ref[number] = term[0, 0]


def back_end(where, mine, got, logits, zinfo, sums, loss_scale, rows, tile):
    spots = mine.shape[1]
    return call(
        functools.partial(back_end_kernel, loss_scale),
        "back_end",
        where,
        [mine, got, off_chip(logits), zinfo, sums],
        [
            by_tile(rows, tile),
            by_tile(rows + 8, tile),
            pl.BlockSpec((rows, tile), lambda i, ix: (ix[0], i)),
            by_tile(8, tile),
            fixed((8, 128)),
        ],
        (jax.ShapeDtypeStruct((rows, spots), F32), jax.ShapeDtypeStruct((3,), F32)),
        (by_tile(rows, tile), pl.BlockSpec(memory_space=pltpu.SMEM)),
        (spots // tile,),
        limit=VMEM_LIMIT,
    )


def swap(value, axis, bit):
    return lax.ppermute(value, axis, [(i, i ^ bit) for i in range(lax.axis_size(axis))])


def after(value, *others):
    return lax.optimization_barrier((value, *others))[0]


def tie(*values):
    return lax.optimization_barrier(values)


def local(logits, centroid_expr, spatial, cluster_cells, density, gene_order):
    n_spot = lax.axis_size("spot")
    n_gene = lax.axis_size("gene")
    me = lax.axis_index("spot")
    col = lax.axis_index("gene")
    cents, spots = logits.shape
    genes = spatial.shape[1]
    genes_all = genes * n_gene
    spots_all = spots * n_spot
    rows = cents // n_gene
    scale = float(spots_all * cents)
    consts = (
        scale / (NB * spots_all),
        scale / genes_all,
        scale,
        (-1.0 / genes_all, -1.0 / (NB * spots_all), float(cents), float(spots_all)),
    )
    ring = n_spot == 8 and cents // n_spot == KC
    where = jnp.stack([col, col ^ 1, me]).astype(jnp.int32)
    tile = 512

    order = (gene_order - col * genes).reshape(genes, 1)
    pick = order == lax.broadcasted_iota(jnp.int32, (genes, genes), 1)
    mine = lax.dot_general(
        pick.astype(F32), centroid_expr, NT, precision=lax.Precision.HIGH, preferred_element_type=F32
    )
    pick = pick.astype(BF)
    theirs = swap(mine, "gene", 2)
    weights = cluster_cells.astype(F32)
    weights = (weights / jnp.sum(weights)).reshape(cents, 1)
    dens_row = density.reshape(1, spots)
    fwd = lambda name, blocks, terms, acc, scale_by, x: pred_part(
        where, blocks, terms, acc, scale_by, x, tile, name
    )
    if ring:
        hop = lambda block, bit: swap(block, "spot", bit)
        send = lambda one, *others: swap(after(one, *others), "gene", 2)
        keys = lambda *order: [functools.partial(lambda k, ix: ix[2] ^ k, k) for k in order]
        o1, o2, oy = [hop(mine, bit) for bit in (2, 4, 1)]
        x_own = list(turn(where, pick, spatial, 2 * tile))
        x_own[0], oy = tie(x_own[0], oy)
        x0 = send(x_own[0])
        logits, *x_own = tie(logits, *x_own)
        *e_one, z_one = exp_parts(where, keys(0, 1, 2, 4), KC, logits, weights, dens_row, None, False, 2 * tile)
        o1, oy, o2, theirs, z_one, *x_own = tie(o1, oy, o2, theirs, z_one, *x_own)
        o2y, o3 = hop(o2, 1), hop(o2, 2)
        acc = fwd("own_early", [mine, oy, o1, o2], [(*e_one, 4 * KC, 0)], None, None, None)
        acc, o2y, o3, oy, theirs, z_one, logits = tie(acc, o2y, o3, oy, theirs, z_one, logits)
        o3y, o1y, ty = hop(o3, 1), hop(oy, 2), hop(theirs, 1)
        *e_two, zinfo = exp_parts(where, keys(3, 5, 6, 7), KC, logits, weights, dens_row, z_one, True, 2 * tile)
        o1y, theirs, zinfo, held = tie(o1y, theirs, zinfo, x_own[1])
        t1, t2, x1 = hop(theirs, 2), hop(theirs, 4), send(held)
        acc, o3y, zinfo = tie(acc, o3y, zinfo)
        pred_own, info = fwd("own_late", [o1y, o2y, o3, o3y], [(*e_two, 4 * KC, 0)], acc, zinfo, x_own)
        own = [mine, oy, o1, o1y, o2, o2y, o3, o3y]
        own_pick = lambda ix, block: [(block ^ ix[2]) == key for key in range(n_spot)]
    else:
        x_own = turn(where, pick, spatial, 2 * tile)
        x_got = [swap(one, "gene", 2) for one in x_own]
        *e_all, zinfo = exp_parts(where, [lambda ix: 0], cents, logits, weights, dens_row, None, True, tile)
        own = [lax.all_gather(mine, "spot", axis=1, tiled=True)]
        other = [lax.all_gather(theirs, "spot", axis=1, tiled=True)]
        whole = [(*e_all, cents, 0)]
        pred_own, info = fwd("own_late", own, whole, None, zinfo, x_own)
        own_pick = None

    info_x = swap(info, "gene", 2)
    predicted = emit(where, pred_own, pick, 2 * tile)
    if ring:
        predicted, t1, ty, t2, theirs, x0 = tie(predicted, t1, ty, t2, theirs, x0)
        t2y, t3 = hop(t2, 1), hop(t2, 2)
        acc_other = fwd("other_mid", [theirs, ty, t1, t2], [(*e_one, 4 * KC, 0)], None, None, None)
        acc_other, t2y, t3, t1, x1, held, info_x = tie(acc_other, t2y, t3, t1, x1, x_own[2], info_x)
        x2, t3y = send(held), hop(t2y, 2)
        x_got = [x0, x1, x2]
    totals, spot = pack(info, info_x, swap(info + info_x, "gene", 1), zinfo, genes)
    if ring:
        got = swap(totals, "spot", 1)
        own[0] = after(mine, totals)
        left_own = rows_left(where, own, rows, own_pick)
        got, left_own, t1 = tie(got, left_own, t1)
        t1y = hop(t1, 1)
        totals = totals + got
        got = swap(totals, "spot", 2)
        acc_other, totals = tie(acc_other, totals)
        acc_other = fwd("other_more", [t2y, t3], [(*e_two, KC, 1), (*e_two, KC, 2)], acc_other, None, None)
        acc_other, got = tie(acc_other, got)
        totals = totals + got
        more = swap(totals, "spot", 4)
        t1y, t3y, acc_other = tie(t1y, t3y, acc_other)
        other = [theirs, ty, t1, t1y, t2, t2y, t3, t3y]
        last = ([t1y, t3y], [(*e_two, KC, 0), (*e_two, KC, 3)], acc_other)
    else:
        totals = lax.psum(totals, "spot")
        more = jnp.zeros_like(totals)
        left_own = rows_left(where, own, rows, own_pick)
        last = (other, whole, None)
    left_other = rows_left(where, other, rows, own_pick)
    if ring:
        left_other, more = tie(left_other, more)

    lefts = (left_own, left_other)
    sent, *highs, sums = back_sum(
        where, *last, zinfo, pred_own, (*x_own, *x_got), lefts, totals, more, spot, consts, rows, tile
    )
    got = swap(sent, "gene", 1)
    rest = back_own(where, highs, lefts, sums, zinfo, dens_row, sent, weights, consts[2], rows, tile)
    rest, got = tie(rest, got)
    grad, loss = back_end(where, rest, got, logits, zinfo, sums, consts[3], rows, tile)
    return loss, predicted, grad


def solution(mesh):
    return jax.shard_map(
        local,
        mesh=mesh,
        in_specs=(P(None, "spot"), P("spot", "gene"), P("spot", "gene"), P(), P("spot"), P("gene")),
        out_specs=(P(), P("spot", "gene"), P("gene", "spot")),
        check_vma=False,
    )
```

```python
import functools
import jax
import jax.numpy as jnp
from jax import lax
from jax.experimental import pallas as pl
from jax.experimental.pallas import tpu as pltpu
from jax.sharding import PartitionSpec as P

NB = 4
XS = 3
XCUT = (0, 8, 11, 16)
EPS = 1e-06
BF = jnp.bfloat16
F32 = jnp.float32
KC = 256
NT = (((1,), (1,)), ((), ()))
TN = (((0,), (0,)), ((), ()))
VMEM_LIMIT = 24 << 20
LARGE_LIMIT = 60 << 20
CHEAP = pl.CostEstimate(flops=1000, bytes_accessed=1000, transcendentals=0)


def split(value):
    high = value.astype(BF)
    return high, (value - high.astype(F32)).astype(BF)


def dot(left, right, dims=(((1,), (0,)), ((), ()))):
    return lax.dot_general(left, right, dims, preferred_element_type=F32)


def call(kernel, name, where, args, specs, out_shape, out_specs, grid, scratch=(), alias=None, limit=VMEM_LIMIT):
    return pl.pallas_call(
        kernel,
        out_shape=out_shape,
        grid_spec=pltpu.PrefetchScalarGridSpec(
            num_scalar_prefetch=1,
            grid=grid,
            in_specs=specs,
            out_specs=out_specs,
            scratch_shapes=list(scratch),
        ),
        input_output_aliases=alias or {},
        compiler_params=pltpu.CompilerParams(
            dimension_semantics=("arbitrary",), vmem_limit_bytes=limit
        ),
        cost_estimate=CHEAP,
        name=name,
    )(where, *args)


def limit_of(depth):
    return VMEM_LIMIT if depth <= 5 * KC else LARGE_LIMIT


def off_chip(value):
    return pltpu.with_memory_space_constraint(value, pltpu.HBM)


def fixed(shape):
    return pl.BlockSpec(shape, lambda i, ix: (0,) * len(shape), pipeline_mode=pl.Buffered(1))


def by_tile(height, tile, row=0, start=0):
    return pl.BlockSpec((height, tile), lambda i, ix: (row, i + start))


def exp_kernel(cents, count, first, last, where, *refs):
    l_refs, w_refs, d_ref, refs = refs[:count], refs[count : 2 * count], refs[2 * count], refs[2 * count + 1 :]
    if not first:
        before_ref, refs = refs[0], refs[1:]
    high_ref, low_ref, info_ref, scal = refs
    step = pl.program_id(0)
    tile = d_ref.shape[1]

    @pl.when(step == 0)
    def _():
        scal[...] = jnp.zeros_like(scal)

    if first:
        total = weighted = jnp.zeros((1, tile), F32)
    else:
        total, weighted = before_ref[0:1, :], before_ref[1:2, :]
    start = 0
    for l_ref, w_ref in zip(l_refs, w_refs):
        for part in range(l_ref.shape[0] // KC):
            rows = slice(part * KC, part * KC + KC)
            value = jnp.exp(l_ref[rows, :])
            high, low = split(value)
            high_ref[start : start + KC, :] = high
            low_ref[start : start + KC, :] = low
            start += KC
            total = total + jnp.sum(value, axis=0, keepdims=True)
            weighted = weighted + jnp.sum(value * w_ref[rows, :], axis=0, keepdims=True)
    if not last:
        info_ref[...] = jnp.concatenate([total, weighted, jnp.zeros((6, tile), F32)], axis=0)
        return
    inv = 1.0 / total
    raw = weighted * inv
    dens = d_ref[...]
    scal[0:1] += dens
    scal[1:2] += raw
    scal[2:3] += dens * (jnp.log(dens) - jnp.log(raw * cents))
    sums = jnp.broadcast_to(jnp.sum(scal[...], axis=1, keepdims=True), (8, tile))
    info_ref[0:1, :] = inv
    info_ref[1:2, :] = raw
    info_ref[2:8, :] = sums[0:6]


def exp_parts(where, keys, deep, logits, weights, density, before, last, tile):
    cents, spots = logits.shape
    count = len(keys)
    specs = [
        pl.BlockSpec((deep, tile), functools.partial(lambda key, i, ix: (key(ix), i), key)) for key in keys
    ]
    specs += [pl.BlockSpec((deep, 1), functools.partial(lambda key, i, ix: (key(ix), 0), key)) for key in keys]
    specs.append(by_tile(1, tile))
    args = [*([off_chip(logits)] * count), *([weights] * count), density]
    if before is not None:
        specs.append(by_tile(8, tile))
        args.append(before)
    rows = deep * count
    return call(
        functools.partial(exp_kernel, float(cents), count, before is None, last),
        "exp_parts",
        where,
        args,
        specs,
        (
            jax.ShapeDtypeStruct((rows, spots), BF),
            jax.ShapeDtypeStruct((rows, spots), BF),
            jax.ShapeDtypeStruct((8, spots), F32),
        ),
        (by_tile(rows, tile), by_tile(rows, tile), by_tile(8, tile)),
        (spots // tile,),
        [pltpu.VMEM((8, tile), F32)],
        limit=limit_of(rows),
    )


def turn_kernel(where, pick_ref, x_ref, *out_refs):
    high, low = split(x_ref[...])
    pick = pick_ref[...]
    value = dot(pick, high, NT) + dot(pick, low, NT)
    start = 0
    for out_ref in out_refs:
        out_ref[...] = value[start : start + out_ref.shape[0]]
        start += out_ref.shape[0]


def heights(genes):
    return [(b - a) * genes // XCUT[-1] for a, b in zip(XCUT, XCUT[1:])]


def turn(where, pick, x, tile):
    spots, genes = x.shape
    return call(
        turn_kernel,
        "turn",
        where,
        [pick, off_chip(x)],
        [fixed((genes, genes)), pl.BlockSpec((tile, genes), lambda i, ix: (i, 0))],
        tuple(jax.ShapeDtypeStruct((height, spots), F32) for height in heights(genes)),
        tuple(by_tile(height, tile) for height in heights(genes)),
        (spots // tile,),
    )


def of_batch(refs, batch, width):
    start, stop, at, pieces = batch * width, (batch + 1) * width, 0, []
    for ref in refs[:XS]:
        height = ref.shape[0]
        low, high = max(start, at), min(stop, at + height)
        if low < high:
            pieces.append(ref[low - at : high - at, :])
        at += height
    return pieces[0] if len(pieces) == 1 else jnp.concatenate(pieces, axis=0)


def load_left(refs, high, low):
    at = 0
    for ref in refs:
        wide = ref.shape[1]
        high[:, at : at + wide], low[:, at : at + wide] = split(ref[...])
        at += wide


def product(high, low, e_high, e_low):
    right = jnp.concatenate([ref[...] for ref in e_high], axis=0)
    value = dot(high[...], right) + dot(low[...], right)
    return value + dot(high[...], jnp.concatenate([ref[...] for ref in e_low], axis=0))


def pred_kernel(blocks, count, first, last, stats, where, *refs):
    s_refs, refs = refs[:blocks], refs[blocks:]
    h_refs, l_refs = refs[:count], refs[count : 2 * count]
    refs = refs[2 * count :]
    if not first:
        acc_ref, refs = refs[0], refs[1:]
    if last:
        zinfo_ref, refs = refs[0], refs[1:]
    if stats:
        x_refs, (out_ref, info_ref, high, low, sums) = refs[:XS], refs[XS:]
    else:
        out_ref, high, low = refs
    step = pl.program_id(0)
    genes, tile = out_ref.shape
    width = genes // NB

    @pl.when(step == 0)
    def _():
        load_left(s_refs, high, low)
        if stats:
            sums[...] = jnp.zeros_like(sums)
            info_ref[...] = jnp.zeros_like(info_ref)

    value = product(high, low, h_refs, l_refs)
    if not first:
        value = value + acc_ref[...]
    if last:
        value = value * zinfo_ref[0:1, :]
    out_ref[...] = value
    if not stats:
        return
    rows = [[], [], []]
    for batch in range(NB):
        at = slice(batch * width, (batch + 1) * width)
        pred, x = value[at], of_batch(x_refs, batch, width)
        for number, term in enumerate((pred * x, pred * pred, x * x)):
            rows[number].append(jnp.sum(term, axis=0, keepdims=True))
            lanes = term[:, :128]
            for group in range(1, tile // 128):
                lanes = lanes + term[:, group * 128 : group * 128 + 128]
            sums[number, at] += lanes
    info_ref[0 : 3 * NB, pl.ds(pl.multiple_of(step * tile, 128), tile)] = jnp.concatenate(
        rows[0] + rows[1] + rows[2], axis=0
    )

    @pl.when(step == pl.num_programs(0) - 1)
    def _():
        for number in range(3):
            info_ref[12:13, number * genes : (number + 1) * genes] = jnp.sum(
                sums[number].T, axis=0, keepdims=True
            )


def pred_part(where, blocks, terms, acc, zinfo, x, tile, name):
    spots = terms[0][0].shape[1]
    genes, deep = blocks[0].shape
    first, last, stats = acc is None, zinfo is not None, x is not None
    kept = stats or not first
    specs = [fixed((genes, deep)) for _ in blocks]
    specs += [by_tile(rows, tile, place) for _, _, rows, place in terms] * 2
    args = [*blocks, *(term[0] for term in terms), *(term[1] for term in terms)]
    alias = {}
    if not first:
        specs.append(by_tile(genes, tile))
        args.append(acc)
    if last:
        specs.append(by_tile(8, tile))
        args.append(zinfo)
    shapes = pltpu.HBM((genes, spots), F32) if kept else jax.ShapeDtypeStruct((genes, spots), F32)
    outs = by_tile(genes, tile)
    scratch = [pltpu.VMEM((genes, deep * len(blocks)), BF)] * 2
    if stats:
        specs += [by_tile(height, tile) for height in heights(genes)]
        args += x
        shapes = (shapes, jax.ShapeDtypeStruct((16, spots), F32))
        outs = (outs, fixed_out((16, spots)))
        scratch.append(pltpu.VMEM((3, genes, 128), F32))
    return call(
        functools.partial(pred_kernel, len(blocks), len(terms), first, last, stats),
        name,
        where,
        args,
        specs,
        shapes,
        outs,
        (spots // tile,),
        scratch,
        alias,
        limit_of(deep * len(blocks)),
    )


def fixed_out(shape):
    return pl.BlockSpec(shape, lambda i, ix: (0,) * len(shape))


def emit_kernel(where, pred_ref, pick_ref, out_ref):
    high, low = split(pred_ref[...].T)
    pick = pick_ref[...]
    out_ref[...] = dot(high, pick) + dot(low, pick)


def emit(where, pred, pick, tile):
    genes, spots = pred.shape
    return call(
        emit_kernel,
        "emit",
        where,
        [off_chip(pred), pick],
        [by_tile(genes, tile), fixed((genes, genes))],
        jax.ShapeDtypeStruct((spots, genes), F32),
        pl.BlockSpec((tile, genes), lambda i, ix: (i, 0)),
        (spots // tile,),
        limit=VMEM_LIMIT,
    )


def cosine(inner, left, right):
    left = left + EPS
    inv = lax.rsqrt(left) * lax.rsqrt(right + EPS)
    cos = inner * inv
    return cos, inv, cos / left


def pack_kernel(mine_ref, theirs_ref, core_ref, z_ref, out_ref, spot_ref):
    genes = out_ref.shape[1] // 2
    totals = (mine_ref[...] + theirs_ref[...]) + core_ref[...]
    spot_ref[...] = totals
    cos, _, _ = cosine(totals[0:NB], totals[NB : 2 * NB], totals[2 * NB : 3 * NB])
    out_ref[...] = jnp.zeros_like(out_ref)
    spots = z_ref.shape[1]
    for number in range(3):
        at = slice(number * genes, (number + 1) * genes)
        out_ref[number : number + 1, 0:genes] = mine_ref[12:13, at]
        out_ref[number : number + 1, genes : 2 * genes] = theirs_ref[12:13, at]
        out_ref[3 + number : 4 + number, 0:128] = z_ref[2 + number : 3 + number, spots - 128 :]
    out_ref[6:7, 0:128] = jnp.broadcast_to(
        jnp.sum(jnp.sum(cos, axis=0, keepdims=True), axis=1, keepdims=True), (1, 128)
    )


def pack(mine, theirs, core, zinfo, genes):
    return pl.pallas_call(
        pack_kernel,
        out_shape=(
            jax.ShapeDtypeStruct((8, 2 * genes), F32),
            jax.ShapeDtypeStruct(mine.shape, F32),
        ),
        compiler_params=pltpu.CompilerParams(vmem_limit_bytes=VMEM_LIMIT),
        cost_estimate=CHEAP,
        name="pack",
    )(mine, theirs, core, zinfo)


def rows_kernel(count, chosen, where, *refs):
    s_refs, (high_ref, low_ref, buffer, sem) = refs[:count], refs[count:]
    rows = high_ref.shape[0] // 2
    pieces = rows // KC
    for slot in range(2 * pieces):
        which = where[1 - slot // pieces]
        piece = slot % pieces
        if chosen is not None:
            for hit, ref in zip(chosen(where, which * pieces + piece), s_refs):

                @pl.when(hit)
                def _(ref=ref):
                    pltpu.make_async_copy(ref, buffer.at[slot], sem.at[slot]).start()

        else:
            at = pl.ds(pl.multiple_of(which * rows + piece * KC, KC), KC)
            pltpu.make_async_copy(s_refs[0].at[:, at], buffer.at[slot], sem.at[slot]).start()
    for slot in range(2 * pieces):
        pltpu.make_async_copy(s_refs[0].at[:, 0:KC], buffer.at[slot], sem.at[slot]).wait()
        at = slice(slot * KC, slot * KC + KC)
        high_ref[at, :], low_ref[at, :] = split(buffer[slot].T)


def rows_left(where, blocks, rows, chosen):
    genes = blocks[0].shape[0]
    shape = jax.ShapeDtypeStruct((2 * rows, genes), BF)
    slots = 2 * rows // KC
    return call(
        functools.partial(rows_kernel, len(blocks), chosen),
        "rows_left",
        where,
        list(blocks),
        [pl.BlockSpec(memory_space=pl.ANY)] * len(blocks),
        (shape, shape),
        (fixed_out((2 * rows, genes)), fixed_out((2 * rows, genes))),
        (1,),
        [pltpu.VMEM((slots, genes, KC), F32), pltpu.SemaphoreType.DMA((slots,))],
        limit=VMEM_LIMIT,
    )


def back_dots(high_refs, low_refs, bhigh, blow, genes):
    value = None
    for part in range(2):
        at = slice(part * genes, (part + 1) * genes)
        one = dot(high_refs[part][...], bhigh[at]) + dot(low_refs[part][...], bhigh[at])
        one = one + dot(high_refs[part][...], blow[at])
        value = one if value is None else value + one
    return value


def back_sum_kernel(blocks, count, first, sizes, where, *refs):
    batch_scale, gene_scale = sizes
    s_refs, h_refs, l_refs = refs[:blocks], refs[blocks : blocks + count], refs[blocks + count : blocks + 2 * count]
    refs = refs[blocks + 2 * count :]
    if not first:
        acc_ref, refs = refs[0], refs[1:]
    z_ref, own_ref, x_refs, refs = refs[0], refs[1], refs[2 : 2 + 2 * XS], refs[2 + 2 * XS :]
    high_refs, low_refs = refs[0:2], refs[2:4]
    totals_ref, more_ref, spot_ref, out_ref, bhigh, blow, sum_ref, coef, other_ref, high, low = refs[4:]
    pred_refs = (own_ref, other_ref)
    genes, tile = own_ref.shape
    rows = high_refs[0].shape[0]
    width = genes // NB

    @pl.when(pl.program_id(0) == 0)
    def _():
        load_left(s_refs, high, low)
        totals = totals_ref[...] + more_ref[...]
        gene_cos, inv_gene, over_gene = cosine(totals[0:1], totals[1:2], totals[2:3])
        coef[0] = jnp.broadcast_to(-gene_scale * inv_gene, (128, 2 * genes)).T
        coef[1] = jnp.broadcast_to(gene_scale * over_gene, (128, 2 * genes)).T
        cos = jnp.broadcast_to(jnp.sum(gene_cos, axis=1, keepdims=True), (1, 128))
        sum_ref[...] = jnp.concatenate([totals[3:7, 0:128], cos, jnp.zeros((3, 128), F32)], axis=0)

    other = product(high, low, h_refs, l_refs)
    if not first:
        other = other + acc_ref[...]
    other_ref[...] = other * z_ref[0:1, :]
    spot = spot_ref[...]
    _, inv_spot, over_spot = cosine(spot[0:NB], spot[NB : 2 * NB], spot[2 * NB : 3 * NB])
    column = jnp.zeros((1, tile), F32)
    for part in range(2):
        for batch in range(NB):
            at = slice(batch * width, (batch + 1) * width)
            here = slice(part * genes + batch * width, part * genes + (batch + 1) * width)
            x_by = jnp.concatenate([coef[0, here]] * (tile // 128), axis=1) - (
                batch_scale * inv_spot[batch : batch + 1]
            )
            p_by = jnp.concatenate([coef[1, here]] * (tile // 128), axis=1) + (
                batch_scale * over_spot[batch : batch + 1]
            )
            pred = pred_refs[part][at, :]
            grad = of_batch(x_refs[part * XS :], batch, width) * x_by + pred * p_by
            bhigh[here], blow[here] = split(grad)
            column = column + jnp.sum(pred * grad, axis=0, keepdims=True)
    out_ref[0:rows] = back_dots(high_refs, low_refs, bhigh, blow, genes)
    out_ref[rows : rows + 1] = column
    out_ref[rows + 1 : rows + 2] = jnp.concatenate([sum_ref[4:5]] * (tile // 128), axis=1)
    out_ref[rows + 2 : rows + 8] = jnp.zeros((6, tile), F32)


def back_sum(where, blocks, terms, acc, zinfo, own, xs, lefts, totals, more, spot, consts, rows, tile):
    genes, spots = own.shape
    deep = blocks[0].shape[1]
    left = pl.BlockSpec((rows, genes), lambda i, ix: (0, 0), pipeline_mode=pl.Buffered(1))
    specs = [fixed((genes, deep)) for _ in blocks]
    specs += [by_tile(height, tile, place) for _, _, height, place in terms] * 2
    args = [*blocks, *(term[0] for term in terms), *(term[1] for term in terms)]
    if acc is not None:
        specs.append(by_tile(genes, tile))
        args.append(off_chip(acc))
    specs += [by_tile(8, tile), by_tile(genes, tile)] + [by_tile(height, tile) for height in heights(genes)] * 2
    specs += [left] * 4 + [fixed((8, 2 * genes))] * 2 + [by_tile(16, tile)]
    args += [zinfo, off_chip(own), *xs, lefts[0][0], lefts[1][0], lefts[0][1], lefts[1][1], totals, more, spot]
    return call(
        functools.partial(back_sum_kernel, len(blocks), len(terms), acc is None, consts[:2]),
        "back_sum",
        where,
        args,
        specs,
        (
            jax.ShapeDtypeStruct((rows + 8, spots), F32),
            jax.ShapeDtypeStruct((2 * genes, spots), BF),
            jax.ShapeDtypeStruct((2 * genes, spots), BF),
            jax.ShapeDtypeStruct((8, 128), F32),
        ),
        (by_tile(rows + 8, tile), by_tile(2 * genes, tile), by_tile(2 * genes, tile), fixed_out((8, 128))),
        (spots // tile,),
        [
            pltpu.VMEM((2, 2 * genes, 128), F32),
            pltpu.VMEM((genes, tile), F32),
            pltpu.VMEM((genes, deep * len(blocks)), BF),
            pltpu.VMEM((genes, deep * len(blocks)), BF),
        ],
        limit=limit_of(deep * len(blocks)),
    )


def back_own_kernel(scale, where, *refs):
    high_refs, low_refs = refs[0:2], refs[2:4]
    bhigh, blow, sum_ref, z_ref, dens_ref, sent_ref, w_ref, out_ref = refs[4:]
    rows, genes = high_refs[0].shape
    value = back_dots(high_refs, low_refs, bhigh, blow, genes)
    raw = z_ref[1:2, :]
    dens, mass = sum_ref[0:1, 0:1], sum_ref[1:2, 0:1]
    grad_raw = scale * (1.0 / mass - dens_ref[...] / (dens * raw))
    out_ref[...] = value + w_ref[...] * grad_raw - (sent_ref[0:1, :] + raw * grad_raw)


def back_own(where, highs, lefts, sums, zinfo, density, sent, weights, scale, rows, tile):
    twice, spots = highs[0].shape
    left = pl.BlockSpec((rows, twice // 2), lambda i, ix: (1, 0), pipeline_mode=pl.Buffered(1))
    specs = [left] * 4 + [by_tile(twice, tile)] * 2
    specs += [fixed((8, 128)), by_tile(8, tile), by_tile(1, tile), by_tile(8, tile, rows // 8)]
    specs.append(pl.BlockSpec((rows, 1), lambda i, ix: (ix[0], 0)))
    args = [lefts[0][0], lefts[1][0], lefts[0][1], lefts[1][1], *highs]
    args += [sums, zinfo, density, off_chip(sent), weights]
    return call(
        functools.partial(back_own_kernel, scale),
        "back_own",
        where,
        args,
        specs,
        jax.ShapeDtypeStruct((rows, spots), F32),
        by_tile(rows, tile),
        (spots // tile,),
        limit=VMEM_LIMIT,
    )


def back_end_kernel(loss_scale, where, mine_ref, got_ref, logit_ref, z_ref, sum_ref, out_ref, loss_ref):
    gene_loss, spot_loss, cents, spots_all = loss_scale
    rows = out_ref.shape[0]
    value = mine_ref[...] + got_ref[0:rows, :] - got_ref[rows : rows + 1, :]
    out_ref[...] = jnp.exp(logit_ref[...]) * z_ref[0:1, :] * value

    @pl.when(pl.program_id(0) == 0)
    def _():
        dens, mass, log_sum, cos = (sum_ref[k : k + 1] for k in range(4))
        gene = (sum_ref[4:5] + got_ref[rows + 1 : rows + 2, 0:128]) * gene_loss
        kl = log_sum / dens + jnp.log(mass * (cents / spots_all)) - jnp.log(dens * (1.0 / spots_all))
        for number, term in enumerate((gene, cos * spot_loss, kl)):
            loss_ref[number] = term[0, 0]


def back_end(where, mine, got, logits, zinfo, sums, loss_scale, rows, tile):
    spots = mine.shape[1]
    return call(
        functools.partial(back_end_kernel, loss_scale),
        "back_end",
        where,
        [mine, got, off_chip(logits), zinfo, sums],
        [
            by_tile(rows, tile),
            by_tile(rows + 8, tile),
            pl.BlockSpec((rows, tile), lambda i, ix: (ix[0], i)),
            by_tile(8, tile),
            fixed((8, 128)),
        ],
        (jax.ShapeDtypeStruct((rows, spots), F32), jax.ShapeDtypeStruct((3,), F32)),
        (by_tile(rows, tile), pl.BlockSpec(memory_space=pltpu.SMEM)),
        (spots // tile,),
        limit=VMEM_LIMIT,
    )


def swap(value, axis, bit):
    return lax.ppermute(value, axis, [(i, i ^ bit) for i in range(lax.axis_size(axis))])


def after(value, *others):
    return lax.optimization_barrier((value, *others))[0]


def tie(*values):
    return lax.optimization_barrier(values)


def local(logits, centroid_expr, spatial, cluster_cells, density, gene_order):
    n_spot = lax.axis_size("spot")
    n_gene = lax.axis_size("gene")
    me = lax.axis_index("spot")
    col = lax.axis_index("gene")
    cents, spots = logits.shape
    genes = spatial.shape[1]
    genes_all = genes * n_gene
    spots_all = spots * n_spot
    rows = cents // n_gene
    scale = float(spots_all * cents)
    consts = (
        scale / (NB * spots_all),
        scale / genes_all,
        scale,
        (-1.0 / genes_all, -1.0 / (NB * spots_all), float(cents), float(spots_all)),
    )
    ring = n_spot == 8 and cents // n_spot == KC
    where = jnp.stack([col, col ^ 1, me]).astype(jnp.int32)
    tile = 512

    order = (gene_order - col * genes).reshape(genes, 1)
    pick = order == lax.broadcasted_iota(jnp.int32, (genes, genes), 1)
    mine = lax.dot_general(
        pick.astype(F32), centroid_expr, NT, precision=lax.Precision.HIGH, preferred_element_type=F32
    )
    pick = pick.astype(BF)
    theirs = swap(mine, "gene", 2)
    weights = cluster_cells.astype(F32)
    weights = (weights / jnp.sum(weights)).reshape(cents, 1)
    dens_row = density.reshape(1, spots)
    fwd = lambda name, blocks, terms, acc, scale_by, x: pred_part(
        where, blocks, terms, acc, scale_by, x, tile, name
    )
    if ring:
        hop = lambda block, bit: swap(block, "spot", bit)
        send = lambda one, *others: swap(after(one, *others), "gene", 2)
        keys = lambda *order: [functools.partial(lambda k, ix: ix[2] ^ k, k) for k in order]
        o1, o2, oy = [hop(mine, bit) for bit in (2, 4, 1)]
        x_own = list(turn(where, pick, spatial, 2 * tile))
        x_own[0], oy = tie(x_own[0], oy)
        x0 = send(x_own[0])
        logits, *x_own = tie(logits, *x_own)
        *e_one, z_one = exp_parts(where, keys(0, 1, 2, 4), KC, logits, weights, dens_row, None, False, 2 * tile)
        o1, oy, o2, theirs, z_one, *x_own = tie(o1, oy, o2, theirs, z_one, *x_own)
        o2y, o3 = hop(o2, 1), hop(o2, 2)
        acc = fwd("own_early", [mine, oy, o1, o2], [(*e_one, 4 * KC, 0)], None, None, None)
        acc, o2y, o3, oy, theirs, z_one, logits = tie(acc, o2y, o3, oy, theirs, z_one, logits)
        o3y, o1y, ty = hop(o3, 1), hop(oy, 2), hop(theirs, 1)
        *e_two, zinfo = exp_parts(where, keys(3, 5, 6, 7), KC, logits, weights, dens_row, z_one, True, 2 * tile)
        o1y, theirs, zinfo, held = tie(o1y, theirs, zinfo, x_own[1])
        t1, t2, x1 = hop(theirs, 2), hop(theirs, 4), send(held)
        acc, o3y, zinfo = tie(acc, o3y, zinfo)
        pred_own, info = fwd("own_late", [o1y, o2y, o3, o3y], [(*e_two, 4 * KC, 0)], acc, zinfo, x_own)
        own = [mine, oy, o1, o1y, o2, o2y, o3, o3y]
        own_pick = lambda ix, block: [(block ^ ix[2]) == key for key in range(n_spot)]
    else:
        x_own = turn(where, pick, spatial, 2 * tile)
        x_got = [swap(one, "gene", 2) for one in x_own]
        *e_all, zinfo = exp_parts(where, [lambda ix: 0], cents, logits, weights, dens_row, None, True, tile)
        own = [lax.all_gather(mine, "spot", axis=1, tiled=True)]
        other = [lax.all_gather(theirs, "spot", axis=1, tiled=True)]
        whole = [(*e_all, cents, 0)]
        pred_own, info = fwd("own_late", own, whole, None, zinfo, x_own)
        own_pick = None

    info_x = swap(info, "gene", 2)
    predicted = emit(where, pred_own, pick, 2 * tile)
    if ring:
        predicted, info_x, t1, ty, t2, theirs, x0, x1, held = tie(
            predicted, info_x, t1, ty, t2, theirs, x0, x1, x_own[2]
        )
        t2y, t3, x2, t1y = hop(t2, 1), hop(t2, 2), send(held), hop(t1, 1)
        x_got = [x0, x1, x2]
    totals, spot = pack(info, info_x, swap(info + info_x, "gene", 1), zinfo, genes)
    if ring:
        got = swap(totals, "spot", 2)
        theirs, totals = tie(theirs, totals)
        acc_other = fwd("other_mid", [theirs, ty, t1, t2], [(*e_one, 4 * KC, 0)], None, None, None)
        acc_other, got, t2y, t3 = tie(acc_other, got, t2y, t3)
        totals = totals + got
        got = swap(totals, "spot", 1)
        t3y = hop(t2y, 2)
        acc_other, totals = tie(acc_other, totals)
        acc_other = fwd("other_more", [t2y, t3], [(*e_two, KC, 1), (*e_two, KC, 2)], acc_other, None, None)
        acc_other, got, mine = tie(acc_other, got, mine)
        totals = totals + got
        more = swap(totals, "spot", 4)
        own[0] = mine
        left_own = rows_left(where, own, rows, own_pick)
        t1y, t3y, left_own = tie(t1y, t3y, left_own)
        other = [theirs, ty, t1, t1y, t2, t2y, t3, t3y]
        last = ([t1y, t3y], [(*e_two, KC, 0), (*e_two, KC, 3)], acc_other)
    else:
        totals = lax.psum(totals, "spot")
        more = jnp.zeros_like(totals)
        left_own = rows_left(where, own, rows, own_pick)
        last = (other, whole, None)
    left_other = rows_left(where, other, rows, own_pick)
    if ring:
        left_other, more = tie(left_other, more)

    lefts = (left_own, left_other)
    sent, *highs, sums = back_sum(
        where, *last, zinfo, pred_own, (*x_own, *x_got), lefts, totals, more, spot, consts, rows, tile
    )
    got = swap(sent, "gene", 1)
    rest = back_own(where, highs, lefts, sums, zinfo, dens_row, sent, weights, consts[2], rows, tile)
    rest, got = tie(rest, got)
    grad, loss = back_end(where, rest, got, logits, zinfo, sums, consts[3], rows, tile)
    return loss, predicted, grad


def solution(mesh):
    return jax.shard_map(
        local,
        mesh=mesh,
        in_specs=(P(None, "spot"), P("spot", "gene"), P("spot", "gene"), P(), P("spot"), P("gene")),
        out_specs=(P(), P("spot", "gene"), P("gene", "spot")),
        check_vma=False,
    )
```

```python
import functools
import jax
import jax.numpy as jnp
from jax import lax
from jax.experimental import pallas as pl
from jax.experimental.pallas import tpu as pltpu
from jax.sharding import PartitionSpec as P

NB = 4
XS = 3
XCUT = (0, 8, 11, 16)
EPS = 1e-06
BF = jnp.bfloat16
F32 = jnp.float32
KC = 256
NT = (((1,), (1,)), ((), ()))
TN = (((0,), (0,)), ((), ()))
VMEM_LIMIT = 22 << 20
LARGE_LIMIT = 60 << 20
CHEAP = pl.CostEstimate(flops=1000, bytes_accessed=1000, transcendentals=0)


def split(value):
    high = value.astype(BF)
    return high, (value - high.astype(F32)).astype(BF)


def dot(left, right, dims=(((1,), (0,)), ((), ()))):
    return lax.dot_general(left, right, dims, preferred_element_type=F32)


def call(kernel, name, where, args, specs, out_shape, out_specs, grid, scratch=(), alias=None, limit=VMEM_LIMIT):
    return pl.pallas_call(
        kernel,
        out_shape=out_shape,
        grid_spec=pltpu.PrefetchScalarGridSpec(
            num_scalar_prefetch=1,
            grid=grid,
            in_specs=specs,
            out_specs=out_specs,
            scratch_shapes=list(scratch),
        ),
        input_output_aliases=alias or {},
        compiler_params=pltpu.CompilerParams(
            dimension_semantics=("arbitrary",), vmem_limit_bytes=limit
        ),
        cost_estimate=CHEAP,
        name=name,
    )(where, *args)


def limit_of(depth):
    return VMEM_LIMIT if depth <= 5 * KC else LARGE_LIMIT


def off_chip(value):
    return pltpu.with_memory_space_constraint(value, pltpu.HBM)


def fixed(shape):
    return pl.BlockSpec(shape, lambda i, ix: (0,) * len(shape), pipeline_mode=pl.Buffered(1))


def by_tile(height, tile, row=0, start=0):
    return pl.BlockSpec((height, tile), lambda i, ix: (row, i + start))


def exp_kernel(cents, count, first, last, where, *refs):
    l_refs, w_refs, d_ref, refs = refs[:count], refs[count : 2 * count], refs[2 * count], refs[2 * count + 1 :]
    if not first:
        before_ref, refs = refs[0], refs[1:]
    high_ref, low_ref, info_ref, scal = refs
    step = pl.program_id(0)
    tile = d_ref.shape[1]

    @pl.when(step == 0)
    def _():
        scal[...] = jnp.zeros_like(scal)

    if first:
        total = weighted = jnp.zeros((1, tile), F32)
    else:
        total, weighted = before_ref[0:1, :], before_ref[1:2, :]
    start = 0
    for l_ref, w_ref in zip(l_refs, w_refs):
        for part in range(l_ref.shape[0] // KC):
            rows = slice(part * KC, part * KC + KC)
            value = jnp.exp(l_ref[rows, :])
            high, low = split(value)
            high_ref[start : start + KC, :] = high
            low_ref[start : start + KC, :] = low
            start += KC
            total = total + jnp.sum(value, axis=0, keepdims=True)
            weighted = weighted + jnp.sum(value * w_ref[rows, :], axis=0, keepdims=True)
    if not last:
        info_ref[...] = jnp.concatenate([total, weighted, jnp.zeros((6, tile), F32)], axis=0)
        return
    inv = 1.0 / total
    raw = weighted * inv
    dens = d_ref[...]
    scal[0:1] += dens
    scal[1:2] += raw
    scal[2:3] += dens * (jnp.log(dens) - jnp.log(raw * cents))
    sums = jnp.broadcast_to(jnp.sum(scal[...], axis=1, keepdims=True), (8, tile))
    info_ref[0:1, :] = inv
    info_ref[1:2, :] = raw
    info_ref[2:8, :] = sums[0:6]


def exp_parts(where, keys, deep, logits, weights, density, before, last, tile):
    cents, spots = logits.shape
    count = len(keys)
    specs = [
        pl.BlockSpec((deep, tile), functools.partial(lambda key, i, ix: (key(ix), i), key)) for key in keys
    ]
    specs += [pl.BlockSpec((deep, 1), functools.partial(lambda key, i, ix: (key(ix), 0), key)) for key in keys]
    specs.append(by_tile(1, tile))
    args = [*([off_chip(logits)] * count), *([weights] * count), density]
    if before is not None:
        specs.append(by_tile(8, tile))
        args.append(before)
    rows = deep * count
    return call(
        functools.partial(exp_kernel, float(cents), count, before is None, last),
        "exp_parts",
        where,
        args,
        specs,
        (
            jax.ShapeDtypeStruct((rows, spots), BF),
            jax.ShapeDtypeStruct((rows, spots), BF),
            jax.ShapeDtypeStruct((8, spots), F32),
        ),
        (by_tile(rows, tile), by_tile(rows, tile), by_tile(8, tile)),
        (spots // tile,),
        [pltpu.VMEM((8, tile), F32)],
        limit=limit_of(rows),
    )


def turn_kernel(where, pick_ref, x_ref, *out_refs):
    high, low = split(x_ref[...])
    pick = pick_ref[...]
    value = dot(pick, high, NT) + dot(pick, low, NT)
    start = 0
    for out_ref in out_refs:
        out_ref[...] = value[start : start + out_ref.shape[0]]
        start += out_ref.shape[0]


def heights(genes):
    return [(b - a) * genes // XCUT[-1] for a, b in zip(XCUT, XCUT[1:])]


def turn(where, pick, x, tile):
    spots, genes = x.shape
    return call(
        turn_kernel,
        "turn",
        where,
        [pick, off_chip(x)],
        [fixed((genes, genes)), pl.BlockSpec((tile, genes), lambda i, ix: (i, 0))],
        tuple(jax.ShapeDtypeStruct((height, spots), F32) for height in heights(genes)),
        tuple(by_tile(height, tile) for height in heights(genes)),
        (spots // tile,),
    )


def of_batch(refs, batch, width):
    start, stop, at, pieces = batch * width, (batch + 1) * width, 0, []
    for ref in refs[:XS]:
        height = ref.shape[0]
        low, high = max(start, at), min(stop, at + height)
        if low < high:
            pieces.append(ref[low - at : high - at, :])
        at += height
    return pieces[0] if len(pieces) == 1 else jnp.concatenate(pieces, axis=0)


def load_left(refs, high, low):
    at = 0
    for ref in refs:
        wide = ref.shape[1]
        high[:, at : at + wide], low[:, at : at + wide] = split(ref[...])
        at += wide


def product(high, low, e_high, e_low):
    right = jnp.concatenate([ref[...] for ref in e_high], axis=0)
    value = dot(high[...], right) + dot(low[...], right)
    return value + dot(high[...], jnp.concatenate([ref[...] for ref in e_low], axis=0))


def pred_kernel(blocks, count, first, last, stats, where, *refs):
    s_refs, refs = refs[:blocks], refs[blocks:]
    h_refs, l_refs = refs[:count], refs[count : 2 * count]
    refs = refs[2 * count :]
    if not first:
        acc_ref, refs = refs[0], refs[1:]
    if last:
        zinfo_ref, refs = refs[0], refs[1:]
    if stats:
        x_refs, (out_ref, info_ref, high, low, sums) = refs[:XS], refs[XS:]
    else:
        out_ref, high, low = refs
    step = pl.program_id(0)
    genes, tile = out_ref.shape
    width = genes // NB

    @pl.when(step == 0)
    def _():
        load_left(s_refs, high, low)
        if stats:
            sums[...] = jnp.zeros_like(sums)
            info_ref[...] = jnp.zeros_like(info_ref)

    value = product(high, low, h_refs, l_refs)
    if not first:
        value = value + acc_ref[...]
    if last:
        value = value * zinfo_ref[0:1, :]
    out_ref[...] = value
    if not stats:
        return
    rows = [[], [], []]
    for batch in range(NB):
        at = slice(batch * width, (batch + 1) * width)
        pred, x = value[at], of_batch(x_refs, batch, width)
        for number, term in enumerate((pred * x, pred * pred, x * x)):
            rows[number].append(jnp.sum(term, axis=0, keepdims=True))
            lanes = term[:, :128]
            for group in range(1, tile // 128):
                lanes = lanes + term[:, group * 128 : group * 128 + 128]
            sums[number, at] += lanes
    info_ref[0 : 3 * NB, pl.ds(pl.multiple_of(step * tile, 128), tile)] = jnp.concatenate(
        rows[0] + rows[1] + rows[2], axis=0
    )

    @pl.when(step == pl.num_programs(0) - 1)
    def _():
        for number in range(3):
            info_ref[12:13, number * genes : (number + 1) * genes] = jnp.sum(
                sums[number].T, axis=0, keepdims=True
            )


def pred_part(where, blocks, terms, acc, zinfo, x, tile, name):
    spots = terms[0][0].shape[1]
    genes, deep = blocks[0].shape
    first, last, stats = acc is None, zinfo is not None, x is not None
    kept = stats or not first
    specs = [fixed((genes, deep)) for _ in blocks]
    specs += [by_tile(rows, tile, place) for _, _, rows, place in terms] * 2
    args = [*blocks, *(term[0] for term in terms), *(term[1] for term in terms)]
    alias = {}
    if not first:
        specs.append(by_tile(genes, tile))
        args.append(acc)
    if last:
        specs.append(by_tile(8, tile))
        args.append(zinfo)
    shapes = pltpu.HBM((genes, spots), F32) if kept else jax.ShapeDtypeStruct((genes, spots), F32)
    outs = by_tile(genes, tile)
    scratch = [pltpu.VMEM((genes, deep * len(blocks)), BF)] * 2
    if stats:
        specs += [by_tile(height, tile) for height in heights(genes)]
        args += x
        shapes = (shapes, jax.ShapeDtypeStruct((16, spots), F32))
        outs = (outs, fixed_out((16, spots)))
        scratch.append(pltpu.VMEM((3, genes, 128), F32))
    return call(
        functools.partial(pred_kernel, len(blocks), len(terms), first, last, stats),
        name,
        where,
        args,
        specs,
        shapes,
        outs,
        (spots // tile,),
        scratch,
        alias,
        limit_of(deep * len(blocks)),
    )


def fixed_out(shape):
    return pl.BlockSpec(shape, lambda i, ix: (0,) * len(shape))


def emit_kernel(where, pred_ref, pick_ref, out_ref):
    high, low = split(pred_ref[...].T)
    pick = pick_ref[...]
    out_ref[...] = dot(high, pick) + dot(low, pick)


def emit(where, pred, pick, tile):
    genes, spots = pred.shape
    return call(
        emit_kernel,
        "emit",
        where,
        [off_chip(pred), pick],
        [by_tile(genes, tile), fixed((genes, genes))],
        jax.ShapeDtypeStruct((spots, genes), F32),
        pl.BlockSpec((tile, genes), lambda i, ix: (i, 0)),
        (spots // tile,),
        limit=VMEM_LIMIT,
    )


def cosine(inner, left, right):
    left = left + EPS
    inv = lax.rsqrt(left) * lax.rsqrt(right + EPS)
    cos = inner * inv
    return cos, inv, cos / left


def pack_kernel(mine_ref, theirs_ref, core_ref, z_ref, out_ref, spot_ref):
    genes = out_ref.shape[1] // 2
    totals = (mine_ref[...] + theirs_ref[...]) + core_ref[...]
    spot_ref[...] = totals
    cos, _, _ = cosine(totals[0:NB], totals[NB : 2 * NB], totals[2 * NB : 3 * NB])
    out_ref[...] = jnp.zeros_like(out_ref)
    spots = z_ref.shape[1]
    for number in range(3):
        at = slice(number * genes, (number + 1) * genes)
        out_ref[number : number + 1, 0:genes] = mine_ref[12:13, at]
        out_ref[number : number + 1, genes : 2 * genes] = theirs_ref[12:13, at]
        out_ref[3 + number : 4 + number, 0:128] = z_ref[2 + number : 3 + number, spots - 128 :]
    out_ref[6:7, 0:128] = jnp.broadcast_to(
        jnp.sum(jnp.sum(cos, axis=0, keepdims=True), axis=1, keepdims=True), (1, 128)
    )


def pack(mine, theirs, core, zinfo, genes):
    return pl.pallas_call(
        pack_kernel,
        out_shape=(
            jax.ShapeDtypeStruct((8, 2 * genes), F32),
            jax.ShapeDtypeStruct(mine.shape, F32),
        ),
        compiler_params=pltpu.CompilerParams(vmem_limit_bytes=VMEM_LIMIT),
        cost_estimate=CHEAP,
        name="pack",
    )(mine, theirs, core, zinfo)


def rows_kernel(count, chosen, where, *refs):
    s_refs, (high_ref, low_ref, buffer, sem) = refs[:count], refs[count:]
    rows = high_ref.shape[0] // 2
    pieces = rows // KC
    for slot in range(2 * pieces):
        which = where[1 - slot // pieces]
        piece = slot % pieces
        if chosen is not None:
            for hit, ref in zip(chosen(where, which * pieces + piece), s_refs):

                @pl.when(hit)
                def _(ref=ref):
                    pltpu.make_async_copy(ref, buffer.at[slot], sem.at[slot]).start()

        else:
            at = pl.ds(pl.multiple_of(which * rows + piece * KC, KC), KC)
            pltpu.make_async_copy(s_refs[0].at[:, at], buffer.at[slot], sem.at[slot]).start()
    for slot in range(2 * pieces):
        pltpu.make_async_copy(s_refs[0].at[:, 0:KC], buffer.at[slot], sem.at[slot]).wait()
        at = slice(slot * KC, slot * KC + KC)
        high_ref[at, :], low_ref[at, :] = split(buffer[slot].T)


def rows_left(where, blocks, rows, chosen):
    genes = blocks[0].shape[0]
    shape = jax.ShapeDtypeStruct((2 * rows, genes), BF)
    slots = 2 * rows // KC
    return call(
        functools.partial(rows_kernel, len(blocks), chosen),
        "rows_left",
        where,
        list(blocks),
        [pl.BlockSpec(memory_space=pl.ANY)] * len(blocks),
        (shape, shape),
        (fixed_out((2 * rows, genes)), fixed_out((2 * rows, genes))),
        (1,),
        [pltpu.VMEM((slots, genes, KC), F32), pltpu.SemaphoreType.DMA((slots,))],
        limit=VMEM_LIMIT,
    )


def back_dots(high_refs, low_refs, bhigh, blow, genes):
    value = None
    for part in range(2):
        at = slice(part * genes, (part + 1) * genes)
        one = dot(high_refs[part][...], bhigh[at]) + dot(low_refs[part][...], bhigh[at])
        one = one + dot(high_refs[part][...], blow[at])
        value = one if value is None else value + one
    return value


def back_sum_kernel(blocks, count, first, sizes, where, *refs):
    batch_scale, gene_scale = sizes
    s_refs, h_refs, l_refs = refs[:blocks], refs[blocks : blocks + count], refs[blocks + count : blocks + 2 * count]
    refs = refs[blocks + 2 * count :]
    if not first:
        acc_ref, refs = refs[0], refs[1:]
    z_ref, own_ref, x_refs, refs = refs[0], refs[1], refs[2 : 2 + 2 * XS], refs[2 + 2 * XS :]
    high_refs, low_refs = refs[0:2], refs[2:4]
    totals_ref, more_ref, spot_ref, out_ref, bhigh, blow, sum_ref, coef, other_ref, high, low = refs[4:]
    pred_refs = (own_ref, other_ref)
    genes, tile = own_ref.shape
    rows = high_refs[0].shape[0]
    width = genes // NB

    @pl.when(pl.program_id(0) == 0)
    def _():
        load_left(s_refs, high, low)
        totals = totals_ref[...] + more_ref[...]
        gene_cos, inv_gene, over_gene = cosine(totals[0:1], totals[1:2], totals[2:3])
        coef[0] = jnp.broadcast_to(-gene_scale * inv_gene, (128, 2 * genes)).T
        coef[1] = jnp.broadcast_to(gene_scale * over_gene, (128, 2 * genes)).T
        cos = jnp.broadcast_to(jnp.sum(gene_cos, axis=1, keepdims=True), (1, 128))
        sum_ref[...] = jnp.concatenate([totals[3:7, 0:128], cos, jnp.zeros((3, 128), F32)], axis=0)

    other = product(high, low, h_refs, l_refs)
    if not first:
        other = other + acc_ref[...]
    other_ref[...] = other * z_ref[0:1, :]
    spot = spot_ref[...]
    _, inv_spot, over_spot = cosine(spot[0:NB], spot[NB : 2 * NB], spot[2 * NB : 3 * NB])
    column = jnp.zeros((1, tile), F32)
    for part in range(2):
        for batch in range(NB):
            at = slice(batch * width, (batch + 1) * width)
            here = slice(part * genes + batch * width, part * genes + (batch + 1) * width)
            x_by = jnp.concatenate([coef[0, here]] * (tile // 128), axis=1) - (
                batch_scale * inv_spot[batch : batch + 1]
            )
            p_by = jnp.concatenate([coef[1, here]] * (tile // 128), axis=1) + (
                batch_scale * over_spot[batch : batch + 1]
            )
            pred = pred_refs[part][at, :]
            grad = of_batch(x_refs[part * XS :], batch, width) * x_by + pred * p_by
            bhigh[here], blow[here] = split(grad)
            column = column + jnp.sum(pred * grad, axis=0, keepdims=True)
    out_ref[0:rows] = back_dots(high_refs, low_refs, bhigh, blow, genes)
    out_ref[rows : rows + 1] = column
    out_ref[rows + 1 : rows + 2] = jnp.concatenate([sum_ref[4:5]] * (tile // 128), axis=1)
    out_ref[rows + 2 : rows + 8] = jnp.zeros((6, tile), F32)


def back_sum(where, blocks, terms, acc, zinfo, own, xs, lefts, totals, more, spot, consts, rows, tile):
    genes, spots = own.shape
    deep = blocks[0].shape[1]
    left = pl.BlockSpec((rows, genes), lambda i, ix: (0, 0), pipeline_mode=pl.Buffered(1))
    specs = [fixed((genes, deep)) for _ in blocks]
    specs += [by_tile(height, tile, place) for _, _, height, place in terms] * 2
    args = [*blocks, *(term[0] for term in terms), *(term[1] for term in terms)]
    if acc is not None:
        specs.append(by_tile(genes, tile))
        args.append(off_chip(acc))
    specs += [by_tile(8, tile), by_tile(genes, tile)] + [by_tile(height, tile) for height in heights(genes)] * 2
    specs += [left] * 4 + [fixed((8, 2 * genes))] * 2 + [by_tile(16, tile)]
    args += [zinfo, off_chip(own), *xs, lefts[0][0], lefts[1][0], lefts[0][1], lefts[1][1], totals, more, spot]
    return call(
        functools.partial(back_sum_kernel, len(blocks), len(terms), acc is None, consts[:2]),
        "back_sum",
        where,
        args,
        specs,
        (
            jax.ShapeDtypeStruct((rows + 8, spots), F32),
            jax.ShapeDtypeStruct((2 * genes, spots), BF),
            jax.ShapeDtypeStruct((2 * genes, spots), BF),
            jax.ShapeDtypeStruct((8, 128), F32),
        ),
        (by_tile(rows + 8, tile), by_tile(2 * genes, tile), by_tile(2 * genes, tile), fixed_out((8, 128))),
        (spots // tile,),
        [
            pltpu.VMEM((2, 2 * genes, 128), F32),
            pltpu.VMEM((genes, tile), F32),
            pltpu.VMEM((genes, deep * len(blocks)), BF),
            pltpu.VMEM((genes, deep * len(blocks)), BF),
        ],
        limit=limit_of(deep * len(blocks)),
    )


def back_own_kernel(scale, where, *refs):
    high_refs, low_refs = refs[0:2], refs[2:4]
    bhigh, blow, sum_ref, z_ref, dens_ref, sent_ref, w_ref, out_ref = refs[4:]
    rows, genes = high_refs[0].shape
    value = back_dots(high_refs, low_refs, bhigh, blow, genes)
    raw = z_ref[1:2, :]
    dens, mass = sum_ref[0:1, 0:1], sum_ref[1:2, 0:1]
    grad_raw = scale * (1.0 / mass - dens_ref[...] / (dens * raw))
    out_ref[...] = value + w_ref[...] * grad_raw - (sent_ref[0:1, :] + raw * grad_raw)


def back_own(where, highs, lefts, sums, zinfo, density, sent, weights, scale, rows, tile):
    twice, spots = highs[0].shape
    left = pl.BlockSpec((rows, twice // 2), lambda i, ix: (1, 0), pipeline_mode=pl.Buffered(1))
    specs = [left] * 4 + [by_tile(twice, tile)] * 2
    specs += [fixed((8, 128)), by_tile(8, tile), by_tile(1, tile), by_tile(8, tile, rows // 8)]
    specs.append(pl.BlockSpec((rows, 1), lambda i, ix: (ix[0], 0)))
    args = [lefts[0][0], lefts[1][0], lefts[0][1], lefts[1][1], *highs]
    args += [sums, zinfo, density, off_chip(sent), weights]
    return call(
        functools.partial(back_own_kernel, scale),
        "back_own",
        where,
        args,
        specs,
        jax.ShapeDtypeStruct((rows, spots), F32),
        by_tile(rows, tile),
        (spots // tile,),
        limit=VMEM_LIMIT,
    )


def back_end_kernel(loss_scale, where, mine_ref, got_ref, logit_ref, z_ref, sum_ref, out_ref, loss_ref):
    gene_loss, spot_loss, cents, spots_all = loss_scale
    rows = out_ref.shape[0]
    value = mine_ref[...] + got_ref[0:rows, :] - got_ref[rows : rows + 1, :]
    out_ref[...] = jnp.exp(logit_ref[...]) * z_ref[0:1, :] * value

    @pl.when(pl.program_id(0) == 0)
    def _():
        dens, mass, log_sum, cos = (sum_ref[k : k + 1] for k in range(4))
        gene = (sum_ref[4:5] + got_ref[rows + 1 : rows + 2, 0:128]) * gene_loss
        kl = log_sum / dens + jnp.log(mass * (cents / spots_all)) - jnp.log(dens * (1.0 / spots_all))
        for number, term in enumerate((gene, cos * spot_loss, kl)):
            loss_ref[number] = term[0, 0]


def back_end(where, mine, got, logits, zinfo, sums, loss_scale, rows, tile):
    spots = mine.shape[1]
    return call(
        functools.partial(back_end_kernel, loss_scale),
        "back_end",
        where,
        [mine, got, off_chip(logits), zinfo, sums],
        [
            by_tile(rows, tile),
            by_tile(rows + 8, tile),
            pl.BlockSpec((rows, tile), lambda i, ix: (ix[0], i)),
            by_tile(8, tile),
            fixed((8, 128)),
        ],
        (jax.ShapeDtypeStruct((rows, spots), F32), jax.ShapeDtypeStruct((3,), F32)),
        (by_tile(rows, tile), pl.BlockSpec(memory_space=pltpu.SMEM)),
        (spots // tile,),
        limit=VMEM_LIMIT,
    )


def swap(value, axis, bit):
    return lax.ppermute(value, axis, [(i, i ^ bit) for i in range(lax.axis_size(axis))])


def after(value, *others):
    return lax.optimization_barrier((value, *others))[0]


def tie(*values):
    return lax.optimization_barrier(values)


def local(logits, centroid_expr, spatial, cluster_cells, density, gene_order):
    n_spot = lax.axis_size("spot")
    n_gene = lax.axis_size("gene")
    me = lax.axis_index("spot")
    col = lax.axis_index("gene")
    cents, spots = logits.shape
    genes = spatial.shape[1]
    genes_all = genes * n_gene
    spots_all = spots * n_spot
    rows = cents // n_gene
    scale = float(spots_all * cents)
    consts = (
        scale / (NB * spots_all),
        scale / genes_all,
        scale,
        (-1.0 / genes_all, -1.0 / (NB * spots_all), float(cents), float(spots_all)),
    )
    ring = n_spot == 8 and cents // n_spot == KC
    where = jnp.stack([col, col ^ 1, me]).astype(jnp.int32)
    tile = 512

    order = (gene_order - col * genes).reshape(genes, 1)
    pick = order == lax.broadcasted_iota(jnp.int32, (genes, genes), 1)
    mine = lax.dot_general(
        pick.astype(F32), centroid_expr, NT, precision=lax.Precision.HIGH, preferred_element_type=F32
    )
    pick = pick.astype(BF)
    theirs = swap(mine, "gene", 2)
    weights = cluster_cells.astype(F32)
    weights = (weights / jnp.sum(weights)).reshape(cents, 1)
    dens_row = density.reshape(1, spots)
    fwd = lambda name, blocks, terms, acc, scale_by, x: pred_part(
        where, blocks, terms, acc, scale_by, x, tile, name
    )
    if ring:
        hop = lambda block, bit: swap(block, "spot", bit)
        send = lambda one, *others: swap(after(one, *others), "gene", 2)
        keys = lambda *order: [functools.partial(lambda k, ix: ix[2] ^ k, k) for k in order]
        o1, o2, oy = [hop(mine, bit) for bit in (2, 4, 1)]
        x_own = list(turn(where, pick, spatial, 2 * tile))
        x_own[0], oy = tie(x_own[0], oy)
        x0 = send(x_own[0])
        logits, *x_own = tie(logits, *x_own)
        *e_one, z_one = exp_parts(where, keys(0, 1, 2, 4), KC, logits, weights, dens_row, None, False, 2 * tile)
        o1, oy, o2, theirs, z_one, *x_own = tie(o1, oy, o2, theirs, z_one, *x_own)
        o2y, o3 = hop(o2, 1), hop(o2, 2)
        acc = fwd("own_early", [mine, oy, o1, o2], [(*e_one, 4 * KC, 0)], None, None, None)
        acc, o2y, o3, oy, theirs, z_one, logits = tie(acc, o2y, o3, oy, theirs, z_one, logits)
        o3y, o1y, ty = hop(o3, 1), hop(oy, 2), hop(theirs, 1)
        *e_two, zinfo = exp_parts(where, keys(3, 5, 6, 7), KC, logits, weights, dens_row, z_one, True, 2 * tile)
        o1y, theirs, zinfo, held = tie(o1y, theirs, zinfo, x_own[1])
        t1, t2, x1 = hop(theirs, 2), hop(theirs, 4), send(held)
        acc, o3y, zinfo = tie(acc, o3y, zinfo)
        pred_own, info = fwd("own_late", [o1y, o2y, o3, o3y], [(*e_two, 4 * KC, 0)], acc, zinfo, x_own)
        own = [mine, oy, o1, o1y, o2, o2y, o3, o3y]
        own_pick = lambda ix, block: [(block ^ ix[2]) == key for key in range(n_spot)]
    else:
        x_own = turn(where, pick, spatial, 2 * tile)
        x_got = [swap(one, "gene", 2) for one in x_own]
        *e_all, zinfo = exp_parts(where, [lambda ix: 0], cents, logits, weights, dens_row, None, True, tile)
        own = [lax.all_gather(mine, "spot", axis=1, tiled=True)]
        other = [lax.all_gather(theirs, "spot", axis=1, tiled=True)]
        whole = [(*e_all, cents, 0)]
        pred_own, info = fwd("own_late", own, whole, None, zinfo, x_own)
        own_pick = None

    info_x = swap(info, "gene", 2)
    predicted = emit(where, pred_own, pick, 2 * tile)
    if ring:
        predicted, info_x, t1, ty, t2, theirs, x0, x1, held = tie(
            predicted, info_x, t1, ty, t2, theirs, x0, x1, x_own[2]
        )
        t2y, t3, x2, t1y = hop(t2, 1), hop(t2, 2), send(held), hop(t1, 1)
        x_got = [x0, x1, x2]
    totals, spot = pack(info, info_x, swap(info + info_x, "gene", 1), zinfo, genes)
    if ring:
        got = swap(totals, "spot", 2)
        theirs, totals = tie(theirs, totals)
        acc_other = fwd("other_mid", [theirs, ty, t1, t2], [(*e_one, 4 * KC, 0)], None, None, None)
        acc_other, got, t2y, t3 = tie(acc_other, got, t2y, t3)
        totals = totals + got
        got = swap(totals, "spot", 1)
        t3y = hop(t2y, 2)
        acc_other, totals = tie(acc_other, totals)
        acc_other = fwd("other_more", [t2y, t3], [(*e_two, KC, 1), (*e_two, KC, 2)], acc_other, None, None)
        acc_other, got, mine = tie(acc_other, got, mine)
        totals = totals + got
        more = swap(totals, "spot", 4)
        own[0] = mine
        left_own = rows_left(where, own, rows, own_pick)
        t1y, t3y, left_own = tie(t1y, t3y, left_own)
        other = [theirs, ty, t1, t1y, t2, t2y, t3, t3y]
        last = ([t1y, t3y], [(*e_two, KC, 0), (*e_two, KC, 3)], acc_other)
    else:
        totals = lax.psum(totals, "spot")
        more = jnp.zeros_like(totals)
        left_own = rows_left(where, own, rows, own_pick)
        last = (other, whole, None)
    left_other = rows_left(where, other, rows, own_pick)
    if ring:
        left_other, more = tie(left_other, more)

    lefts = (left_own, left_other)
    sent, *highs, sums = back_sum(
        where, *last, zinfo, pred_own, (*x_own, *x_got), lefts, totals, more, spot, consts, rows, tile
    )
    got = swap(sent, "gene", 1)
    rest = back_own(where, highs, lefts, sums, zinfo, dens_row, sent, weights, consts[2], rows, tile)
    rest, got = tie(rest, got)
    grad, loss = back_end(where, rest, got, logits, zinfo, sums, consts[3], rows, 2 * tile)
    return loss, predicted, grad


def solution(mesh):
    return jax.shard_map(
        local,
        mesh=mesh,
        in_specs=(P(None, "spot"), P("spot", "gene"), P("spot", "gene"), P(), P("spot"), P("gene")),
        out_specs=(P(), P("spot", "gene"), P("gene", "spot")),
        check_vma=False,
    )
```

```python
import functools
import jax
import jax.numpy as jnp
from jax import lax
from jax.experimental import pallas as pl
from jax.experimental.pallas import tpu as pltpu
from jax.sharding import PartitionSpec as P

NB = 4
XS = 3
XCUT = (0, 16, 21, 32)
EPS = 1e-06
BF = jnp.bfloat16
F32 = jnp.float32
KC = 256
NT = (((1,), (1,)), ((), ()))
TN = (((0,), (0,)), ((), ()))
VMEM_LIMIT = 22 << 20
LARGE_LIMIT = 60 << 20
CHEAP = pl.CostEstimate(flops=1000, bytes_accessed=1000, transcendentals=0)


def split(value):
    high = value.astype(BF)
    return high, (value - high.astype(F32)).astype(BF)


def dot(left, right, dims=(((1,), (0,)), ((), ()))):
    return lax.dot_general(left, right, dims, preferred_element_type=F32)


def call(kernel, name, where, args, specs, out_shape, out_specs, grid, scratch=(), alias=None, limit=VMEM_LIMIT):
    return pl.pallas_call(
        kernel,
        out_shape=out_shape,
        grid_spec=pltpu.PrefetchScalarGridSpec(
            num_scalar_prefetch=1,
            grid=grid,
            in_specs=specs,
            out_specs=out_specs,
            scratch_shapes=list(scratch),
        ),
        input_output_aliases=alias or {},
        compiler_params=pltpu.CompilerParams(
            dimension_semantics=("arbitrary",), vmem_limit_bytes=limit
        ),
        cost_estimate=CHEAP,
        name=name,
    )(where, *args)


def limit_of(depth):
    return VMEM_LIMIT if depth <= 5 * KC else LARGE_LIMIT


def off_chip(value):
    return pltpu.with_memory_space_constraint(value, pltpu.HBM)


def fixed(shape):
    return pl.BlockSpec(shape, lambda i, ix: (0,) * len(shape), pipeline_mode=pl.Buffered(1))


def by_tile(height, tile, row=0, start=0):
    return pl.BlockSpec((height, tile), lambda i, ix: (row, i + start))


def exp_kernel(cents, count, first, last, where, *refs):
    l_refs, w_refs, d_ref, refs = refs[:count], refs[count : 2 * count], refs[2 * count], refs[2 * count + 1 :]
    if not first:
        before_ref, refs = refs[0], refs[1:]
    high_ref, low_ref, info_ref, scal = refs
    step = pl.program_id(0)
    tile = d_ref.shape[1]

    @pl.when(step == 0)
    def _():
        scal[...] = jnp.zeros_like(scal)

    if first:
        total = weighted = jnp.zeros((1, tile), F32)
    else:
        total, weighted = before_ref[0:1, :], before_ref[1:2, :]
    start = 0
    for l_ref, w_ref in zip(l_refs, w_refs):
        for part in range(l_ref.shape[0] // KC):
            rows = slice(part * KC, part * KC + KC)
            value = jnp.exp(l_ref[rows, :])
            high, low = split(value)
            high_ref[start : start + KC, :] = high
            low_ref[start : start + KC, :] = low
            start += KC
            total = total + jnp.sum(value, axis=0, keepdims=True)
            weighted = weighted + jnp.sum(value * w_ref[rows, :], axis=0, keepdims=True)
    if not last:
        info_ref[...] = jnp.concatenate([total, weighted, jnp.zeros((6, tile), F32)], axis=0)
        return
    inv = 1.0 / total
    raw = weighted * inv
    dens = d_ref[...]
    scal[0:1] += dens
    scal[1:2] += raw
    scal[2:3] += dens * (jnp.log(dens) - jnp.log(raw * cents))
    sums = jnp.broadcast_to(jnp.sum(scal[...], axis=1, keepdims=True), (8, tile))
    info_ref[0:1, :] = inv
    info_ref[1:2, :] = raw
    info_ref[2:8, :] = sums[0:6]


def exp_parts(where, keys, deep, logits, weights, density, before, last, tile):
    cents, spots = logits.shape
    count = len(keys)
    specs = [
        pl.BlockSpec((deep, tile), functools.partial(lambda key, i, ix: (key(ix), i), key)) for key in keys
    ]
    specs += [pl.BlockSpec((deep, 1), functools.partial(lambda key, i, ix: (key(ix), 0), key)) for key in keys]
    specs.append(by_tile(1, tile))
    args = [*([off_chip(logits)] * count), *([weights] * count), density]
    if before is not None:
        specs.append(by_tile(8, tile))
        args.append(before)
    rows = deep * count
    return call(
        functools.partial(exp_kernel, float(cents), count, before is None, last),
        "exp_parts",
        where,
        args,
        specs,
        (
            jax.ShapeDtypeStruct((rows, spots), BF),
            jax.ShapeDtypeStruct((rows, spots), BF),
            jax.ShapeDtypeStruct((8, spots), F32),
        ),
        (by_tile(rows, tile), by_tile(rows, tile), by_tile(8, tile)),
        (spots // tile,),
        [pltpu.VMEM((8, tile), F32)],
        limit=limit_of(rows),
    )


def turn_kernel(where, pick_ref, x_ref, *out_refs):
    high, low = split(x_ref[...])
    pick = pick_ref[...]
    value = dot(pick, high, NT) + dot(pick, low, NT)
    start = 0
    for out_ref in out_refs:
        out_ref[...] = value[start : start + out_ref.shape[0]]
        start += out_ref.shape[0]


def heights(genes):
    return [(b - a) * genes // XCUT[-1] for a, b in zip(XCUT, XCUT[1:])]


def turn(where, pick, x, tile):
    spots, genes = x.shape
    return call(
        turn_kernel,
        "turn",
        where,
        [pick, off_chip(x)],
        [fixed((genes, genes)), pl.BlockSpec((tile, genes), lambda i, ix: (i, 0))],
        tuple(jax.ShapeDtypeStruct((height, spots), F32) for height in heights(genes)),
        tuple(by_tile(height, tile) for height in heights(genes)),
        (spots // tile,),
    )


def of_batch(refs, batch, width):
    start, stop, at, pieces = batch * width, (batch + 1) * width, 0, []
    for ref in refs[:XS]:
        height = ref.shape[0]
        low, high = max(start, at), min(stop, at + height)
        if low < high:
            pieces.append(ref[low - at : high - at, :])
        at += height
    return pieces[0] if len(pieces) == 1 else jnp.concatenate(pieces, axis=0)


def load_left(refs, high, low):
    at = 0
    for ref in refs:
        wide = ref.shape[1]
        high[:, at : at + wide], low[:, at : at + wide] = split(ref[...])
        at += wide


def product(high, low, e_high, e_low):
    right = jnp.concatenate([ref[...] for ref in e_high], axis=0)
    value = dot(high[...], right) + dot(low[...], right)
    return value + dot(high[...], jnp.concatenate([ref[...] for ref in e_low], axis=0))


def pred_kernel(blocks, count, first, last, stats, where, *refs):
    s_refs, refs = refs[:blocks], refs[blocks:]
    h_refs, l_refs = refs[:count], refs[count : 2 * count]
    refs = refs[2 * count :]
    if not first:
        acc_ref, refs = refs[0], refs[1:]
    if last:
        zinfo_ref, refs = refs[0], refs[1:]
    if stats:
        x_refs, (out_ref, info_ref, high, low, sums) = refs[:XS], refs[XS:]
    else:
        out_ref, high, low = refs
    step = pl.program_id(0)
    genes, tile = out_ref.shape
    width = genes // NB

    @pl.when(step == 0)
    def _():
        load_left(s_refs, high, low)
        if stats:
            sums[...] = jnp.zeros_like(sums)
            info_ref[...] = jnp.zeros_like(info_ref)

    value = product(high, low, h_refs, l_refs)
    if not first:
        value = value + acc_ref[...]
    if last:
        value = value * zinfo_ref[0:1, :]
    out_ref[...] = value
    if not stats:
        return
    rows = [[], [], []]
    for batch in range(NB):
        at = slice(batch * width, (batch + 1) * width)
        pred, x = value[at], of_batch(x_refs, batch, width)
        for number, term in enumerate((pred * x, pred * pred, x * x)):
            rows[number].append(jnp.sum(term, axis=0, keepdims=True))
            lanes = term[:, :128]
            for group in range(1, tile // 128):
                lanes = lanes + term[:, group * 128 : group * 128 + 128]
            sums[number, at] += lanes
    info_ref[0 : 3 * NB, pl.ds(pl.multiple_of(step * tile, 128), tile)] = jnp.concatenate(
        rows[0] + rows[1] + rows[2], axis=0
    )

    @pl.when(step == pl.num_programs(0) - 1)
    def _():
        for number in range(3):
            info_ref[12:13, number * genes : (number + 1) * genes] = jnp.sum(
                sums[number].T, axis=0, keepdims=True
            )


def pred_part(where, blocks, terms, acc, zinfo, x, tile, name):
    spots = terms[0][0].shape[1]
    genes, deep = blocks[0].shape
    first, last, stats = acc is None, zinfo is not None, x is not None
    kept = stats or not first
    specs = [fixed((genes, deep)) for _ in blocks]
    specs += [by_tile(rows, tile, place) for _, _, rows, place in terms] * 2
    args = [*blocks, *(term[0] for term in terms), *(term[1] for term in terms)]
    alias = {}
    if not first:
        specs.append(by_tile(genes, tile))
        args.append(acc)
    if last:
        specs.append(by_tile(8, tile))
        args.append(zinfo)
    shapes = pltpu.HBM((genes, spots), F32) if kept else jax.ShapeDtypeStruct((genes, spots), F32)
    outs = by_tile(genes, tile)
    scratch = [pltpu.VMEM((genes, deep * len(blocks)), BF)] * 2
    if stats:
        specs += [by_tile(height, tile) for height in heights(genes)]
        args += x
        shapes = (shapes, jax.ShapeDtypeStruct((16, spots), F32))
        outs = (outs, fixed_out((16, spots)))
        scratch.append(pltpu.VMEM((3, genes, 128), F32))
    return call(
        functools.partial(pred_kernel, len(blocks), len(terms), first, last, stats),
        name,
        where,
        args,
        specs,
        shapes,
        outs,
        (spots // tile,),
        scratch,
        alias,
        limit_of(deep * len(blocks)),
    )


def fixed_out(shape):
    return pl.BlockSpec(shape, lambda i, ix: (0,) * len(shape))


def emit_kernel(where, pred_ref, pick_ref, out_ref):
    high, low = split(pred_ref[...].T)
    pick = pick_ref[...]
    out_ref[...] = dot(high, pick) + dot(low, pick)


def emit(where, pred, pick, tile):
    genes, spots = pred.shape
    return call(
        emit_kernel,
        "emit",
        where,
        [off_chip(pred), pick],
        [by_tile(genes, tile), fixed((genes, genes))],
        jax.ShapeDtypeStruct((spots, genes), F32),
        pl.BlockSpec((tile, genes), lambda i, ix: (i, 0)),
        (spots // tile,),
        limit=VMEM_LIMIT,
    )


def cosine(inner, left, right):
    left = left + EPS
    inv = lax.rsqrt(left) * lax.rsqrt(right + EPS)
    cos = inner * inv
    return cos, inv, cos / left


def pack_kernel(mine_ref, theirs_ref, core_ref, z_ref, out_ref, spot_ref):
    genes = out_ref.shape[1] // 2
    totals = (mine_ref[...] + theirs_ref[...]) + core_ref[...]
    spot_ref[...] = totals
    cos, _, _ = cosine(totals[0:NB], totals[NB : 2 * NB], totals[2 * NB : 3 * NB])
    out_ref[...] = jnp.zeros_like(out_ref)
    spots = z_ref.shape[1]
    for number in range(3):
        at = slice(number * genes, (number + 1) * genes)
        out_ref[number : number + 1, 0:genes] = mine_ref[12:13, at]
        out_ref[number : number + 1, genes : 2 * genes] = theirs_ref[12:13, at]
        out_ref[3 + number : 4 + number, 0:128] = z_ref[2 + number : 3 + number, spots - 128 :]
    out_ref[6:7, 0:128] = jnp.broadcast_to(
        jnp.sum(jnp.sum(cos, axis=0, keepdims=True), axis=1, keepdims=True), (1, 128)
    )


def pack(mine, theirs, core, zinfo, genes):
    return pl.pallas_call(
        pack_kernel,
        out_shape=(
            jax.ShapeDtypeStruct((8, 2 * genes), F32),
            jax.ShapeDtypeStruct(mine.shape, F32),
        ),
        compiler_params=pltpu.CompilerParams(vmem_limit_bytes=VMEM_LIMIT),
        cost_estimate=CHEAP,
        name="pack",
    )(mine, theirs, core, zinfo)


def rows_kernel(count, chosen, where, *refs):
    s_refs, (high_ref, low_ref, buffer, sem) = refs[:count], refs[count:]
    rows = high_ref.shape[0] // 2
    pieces = rows // KC
    for slot in range(2 * pieces):
        which = where[1 - slot // pieces]
        piece = slot % pieces
        if chosen is not None:
            for hit, ref in zip(chosen(where, which * pieces + piece), s_refs):

                @pl.when(hit)
                def _(ref=ref):
                    pltpu.make_async_copy(ref, buffer.at[slot], sem.at[slot]).start()

        else:
            at = pl.ds(pl.multiple_of(which * rows + piece * KC, KC), KC)
            pltpu.make_async_copy(s_refs[0].at[:, at], buffer.at[slot], sem.at[slot]).start()
    for slot in range(2 * pieces):
        pltpu.make_async_copy(s_refs[0].at[:, 0:KC], buffer.at[slot], sem.at[slot]).wait()
        at = slice(slot * KC, slot * KC + KC)
        high_ref[at, :], low_ref[at, :] = split(buffer[slot].T)


def rows_left(where, blocks, rows, chosen):
    genes = blocks[0].shape[0]
    shape = jax.ShapeDtypeStruct((2 * rows, genes), BF)
    slots = 2 * rows // KC
    return call(
        functools.partial(rows_kernel, len(blocks), chosen),
        "rows_left",
        where,
        list(blocks),
        [pl.BlockSpec(memory_space=pl.ANY)] * len(blocks),
        (shape, shape),
        (fixed_out((2 * rows, genes)), fixed_out((2 * rows, genes))),
        (1,),
        [pltpu.VMEM((slots, genes, KC), F32), pltpu.SemaphoreType.DMA((slots,))],
        limit=VMEM_LIMIT,
    )


def back_dots(high_refs, low_refs, bhigh, blow, genes):
    value = None
    for part in range(2):
        at = slice(part * genes, (part + 1) * genes)
        one = dot(high_refs[part][...], bhigh[at]) + dot(low_refs[part][...], bhigh[at])
        one = one + dot(high_refs[part][...], blow[at])
        value = one if value is None else value + one
    return value


def back_sum_kernel(blocks, count, first, sizes, where, *refs):
    batch_scale, gene_scale = sizes
    s_refs, h_refs, l_refs = refs[:blocks], refs[blocks : blocks + count], refs[blocks + count : blocks + 2 * count]
    refs = refs[blocks + 2 * count :]
    if not first:
        acc_ref, refs = refs[0], refs[1:]
    z_ref, own_ref, x_refs, refs = refs[0], refs[1], refs[2 : 2 + 2 * XS], refs[2 + 2 * XS :]
    high_refs, low_refs = refs[0:2], refs[2:4]
    totals_ref, more_ref, spot_ref, out_ref, bhigh, blow, sum_ref, coef, other_ref, high, low = refs[4:]
    pred_refs = (own_ref, other_ref)
    genes, tile = own_ref.shape
    rows = high_refs[0].shape[0]
    width = genes // NB

    @pl.when(pl.program_id(0) == 0)
    def _():
        load_left(s_refs, high, low)
        totals = totals_ref[...] + more_ref[...]
        gene_cos, inv_gene, over_gene = cosine(totals[0:1], totals[1:2], totals[2:3])
        coef[0] = jnp.broadcast_to(-gene_scale * inv_gene, (128, 2 * genes)).T
        coef[1] = jnp.broadcast_to(gene_scale * over_gene, (128, 2 * genes)).T
        cos = jnp.broadcast_to(jnp.sum(gene_cos, axis=1, keepdims=True), (1, 128))
        sum_ref[...] = jnp.concatenate([totals[3:7, 0:128], cos, jnp.zeros((3, 128), F32)], axis=0)

    other = product(high, low, h_refs, l_refs)
    if not first:
        other = other + acc_ref[...]
    other_ref[...] = other * z_ref[0:1, :]
    spot = spot_ref[...]
    _, inv_spot, over_spot = cosine(spot[0:NB], spot[NB : 2 * NB], spot[2 * NB : 3 * NB])
    column = jnp.zeros((1, tile), F32)
    for part in range(2):
        for batch in range(NB):
            at = slice(batch * width, (batch + 1) * width)
            here = slice(part * genes + batch * width, part * genes + (batch + 1) * width)
            x_by = jnp.concatenate([coef[0, here]] * (tile // 128), axis=1) - (
                batch_scale * inv_spot[batch : batch + 1]
            )
            p_by = jnp.concatenate([coef[1, here]] * (tile // 128), axis=1) + (
                batch_scale * over_spot[batch : batch + 1]
            )
            pred = pred_refs[part][at, :]
            grad = of_batch(x_refs[part * XS :], batch, width) * x_by + pred * p_by
            bhigh[here], blow[here] = split(grad)
            column = column + jnp.sum(pred * grad, axis=0, keepdims=True)
    out_ref[0:rows] = back_dots(high_refs, low_refs, bhigh, blow, genes)
    out_ref[rows : rows + 1] = column
    out_ref[rows + 1 : rows + 2] = jnp.concatenate([sum_ref[4:5]] * (tile // 128), axis=1)
    out_ref[rows + 2 : rows + 8] = jnp.zeros((6, tile), F32)


def back_sum(where, blocks, terms, acc, zinfo, own, xs, lefts, totals, more, spot, consts, rows, tile):
    genes, spots = own.shape
    deep = blocks[0].shape[1]
    left = pl.BlockSpec((rows, genes), lambda i, ix: (0, 0), pipeline_mode=pl.Buffered(1))
    specs = [fixed((genes, deep)) for _ in blocks]
    specs += [by_tile(height, tile, place) for _, _, height, place in terms] * 2
    args = [*blocks, *(term[0] for term in terms), *(term[1] for term in terms)]
    if acc is not None:
        specs.append(by_tile(genes, tile))
        args.append(off_chip(acc))
    specs += [by_tile(8, tile), by_tile(genes, tile)] + [by_tile(height, tile) for height in heights(genes)] * 2
    specs += [left] * 4 + [fixed((8, 2 * genes))] * 2 + [by_tile(16, tile)]
    args += [zinfo, off_chip(own), *xs, lefts[0][0], lefts[1][0], lefts[0][1], lefts[1][1], totals, more, spot]
    return call(
        functools.partial(back_sum_kernel, len(blocks), len(terms), acc is None, consts[:2]),
        "back_sum",
        where,
        args,
        specs,
        (
            jax.ShapeDtypeStruct((rows + 8, spots), F32),
            jax.ShapeDtypeStruct((2 * genes, spots), BF),
            jax.ShapeDtypeStruct((2 * genes, spots), BF),
            jax.ShapeDtypeStruct((8, 128), F32),
        ),
        (by_tile(rows + 8, tile), by_tile(2 * genes, tile), by_tile(2 * genes, tile), fixed_out((8, 128))),
        (spots // tile,),
        [
            pltpu.VMEM((2, 2 * genes, 128), F32),
            pltpu.VMEM((genes, tile), F32),
            pltpu.VMEM((genes, deep * len(blocks)), BF),
            pltpu.VMEM((genes, deep * len(blocks)), BF),
        ],
        limit=limit_of(deep * len(blocks)),
    )


def back_own_kernel(scale, where, *refs):
    high_refs, low_refs = refs[0:2], refs[2:4]
    bhigh, blow, sum_ref, z_ref, dens_ref, sent_ref, w_ref, out_ref = refs[4:]
    rows, genes = high_refs[0].shape
    value = back_dots(high_refs, low_refs, bhigh, blow, genes)
    raw = z_ref[1:2, :]
    dens, mass = sum_ref[0:1, 0:1], sum_ref[1:2, 0:1]
    grad_raw = scale * (1.0 / mass - dens_ref[...] / (dens * raw))
    out_ref[...] = value + w_ref[...] * grad_raw - (sent_ref[0:1, :] + raw * grad_raw)


def back_own(where, highs, lefts, sums, zinfo, density, sent, weights, scale, rows, tile):
    twice, spots = highs[0].shape
    left = pl.BlockSpec((rows, twice // 2), lambda i, ix: (1, 0), pipeline_mode=pl.Buffered(1))
    specs = [left] * 4 + [by_tile(twice, tile)] * 2
    specs += [fixed((8, 128)), by_tile(8, tile), by_tile(1, tile), by_tile(8, tile, rows // 8)]
    specs.append(pl.BlockSpec((rows, 1), lambda i, ix: (ix[0], 0)))
    args = [lefts[0][0], lefts[1][0], lefts[0][1], lefts[1][1], *highs]
    args += [sums, zinfo, density, off_chip(sent), weights]
    return call(
        functools.partial(back_own_kernel, scale),
        "back_own",
        where,
        args,
        specs,
        jax.ShapeDtypeStruct((rows, spots), F32),
        by_tile(rows, tile),
        (spots // tile,),
        limit=VMEM_LIMIT,
    )


def back_end_kernel(loss_scale, where, mine_ref, got_ref, logit_ref, z_ref, sum_ref, out_ref, loss_ref):
    gene_loss, spot_loss, cents, spots_all = loss_scale
    rows = out_ref.shape[0]
    value = mine_ref[...] + got_ref[0:rows, :] - got_ref[rows : rows + 1, :]
    out_ref[...] = jnp.exp(logit_ref[...]) * z_ref[0:1, :] * value

    @pl.when(pl.program_id(0) == 0)
    def _():
        dens, mass, log_sum, cos = (sum_ref[k : k + 1] for k in range(4))
        gene = (sum_ref[4:5] + got_ref[rows + 1 : rows + 2, 0:128]) * gene_loss
        kl = log_sum / dens + jnp.log(mass * (cents / spots_all)) - jnp.log(dens * (1.0 / spots_all))
        for number, term in enumerate((gene, cos * spot_loss, kl)):
            loss_ref[number] = term[0, 0]


def back_end(where, mine, got, logits, zinfo, sums, loss_scale, rows, tile):
    spots = mine.shape[1]
    return call(
        functools.partial(back_end_kernel, loss_scale),
        "back_end",
        where,
        [mine, got, off_chip(logits), zinfo, sums],
        [
            by_tile(rows, tile),
            by_tile(rows + 8, tile),
            pl.BlockSpec((rows, tile), lambda i, ix: (ix[0], i)),
            by_tile(8, tile),
            fixed((8, 128)),
        ],
        (jax.ShapeDtypeStruct((rows, spots), F32), jax.ShapeDtypeStruct((3,), F32)),
        (by_tile(rows, tile), pl.BlockSpec(memory_space=pltpu.SMEM)),
        (spots // tile,),
        limit=VMEM_LIMIT,
    )


def swap(value, axis, bit):
    return lax.ppermute(value, axis, [(i, i ^ bit) for i in range(lax.axis_size(axis))])


def after(value, *others):
    return lax.optimization_barrier((value, *others))[0]


def tie(*values):
    return lax.optimization_barrier(values)


def local(logits, centroid_expr, spatial, cluster_cells, density, gene_order):
    n_spot = lax.axis_size("spot")
    n_gene = lax.axis_size("gene")
    me = lax.axis_index("spot")
    col = lax.axis_index("gene")
    cents, spots = logits.shape
    genes = spatial.shape[1]
    genes_all = genes * n_gene
    spots_all = spots * n_spot
    rows = cents // n_gene
    scale = float(spots_all * cents)
    consts = (
        scale / (NB * spots_all),
        scale / genes_all,
        scale,
        (-1.0 / genes_all, -1.0 / (NB * spots_all), float(cents), float(spots_all)),
    )
    ring = n_spot == 8 and cents // n_spot == KC
    where = jnp.stack([col, col ^ 1, me]).astype(jnp.int32)
    tile = 512

    order = (gene_order - col * genes).reshape(genes, 1)
    pick = order == lax.broadcasted_iota(jnp.int32, (genes, genes), 1)
    mine = lax.dot_general(
        pick.astype(F32), centroid_expr, NT, precision=lax.Precision.HIGH, preferred_element_type=F32
    )
    pick = pick.astype(BF)
    theirs = swap(mine, "gene", 2)
    weights = cluster_cells.astype(F32)
    weights = (weights / jnp.sum(weights)).reshape(cents, 1)
    dens_row = density.reshape(1, spots)
    fwd = lambda name, blocks, terms, acc, scale_by, x: pred_part(
        where, blocks, terms, acc, scale_by, x, tile, name
    )
    if ring:
        hop = lambda block, bit: swap(block, "spot", bit)
        send = lambda one, *others: swap(after(one, *others), "gene", 2)
        keys = lambda *order: [functools.partial(lambda k, ix: ix[2] ^ k, k) for k in order]
        o1, o2, oy = [hop(mine, bit) for bit in (2, 4, 1)]
        x_own = list(turn(where, pick, spatial, 2 * tile))
        x_own[0], oy = tie(x_own[0], oy)
        x0 = send(x_own[0])
        logits, *x_own = tie(logits, *x_own)
        *e_one, z_one = exp_parts(where, keys(0, 1, 2, 4), KC, logits, weights, dens_row, None, False, 2 * tile)
        theirs, o1, oy, o2, z_one, *x_own = tie(theirs, o1, oy, o2, z_one, *x_own)
        o2y, o3 = hop(o2, 1), hop(o2, 2)
        acc = fwd("own_early", [mine, oy, o1, o2], [(*e_one, 4 * KC, 0)], None, None, None)
        acc, o2y, o3, oy, theirs, z_one, logits = tie(acc, o2y, o3, oy, theirs, z_one, logits)
        o3y, o1y, ty = hop(o3, 1), hop(oy, 2), hop(theirs, 1)
        *e_two, zinfo = exp_parts(where, keys(3, 5, 6, 7), KC, logits, weights, dens_row, z_one, True, 2 * tile)
        o1y, theirs, zinfo, held = tie(o1y, theirs, zinfo, x_own[1])
        t1, t2, x1 = hop(theirs, 2), hop(theirs, 4), send(held)
        acc, o3y, zinfo = tie(acc, o3y, zinfo)
        pred_own, info = fwd("own_late", [o1y, o2y, o3, o3y], [(*e_two, 4 * KC, 0)], acc, zinfo, x_own)
        own = [mine, oy, o1, o1y, o2, o2y, o3, o3y]
        own_pick = lambda ix, block: [(block ^ ix[2]) == key for key in range(n_spot)]
    else:
        x_own = turn(where, pick, spatial, 2 * tile)
        x_got = [swap(one, "gene", 2) for one in x_own]
        *e_all, zinfo = exp_parts(where, [lambda ix: 0], cents, logits, weights, dens_row, None, True, tile)
        own = [lax.all_gather(mine, "spot", axis=1, tiled=True)]
        other = [lax.all_gather(theirs, "spot", axis=1, tiled=True)]
        whole = [(*e_all, cents, 0)]
        pred_own, info = fwd("own_late", own, whole, None, zinfo, x_own)
        own_pick = None

    info_x = swap(info, "gene", 2)
    predicted = emit(where, pred_own, pick, 2 * tile)
    if ring:
        predicted, info_x, x1, ty, t1, t2, theirs, x0, held = tie(
            predicted, info_x, x1, ty, t1, t2, theirs, x0, x_own[2]
        )
        t2y, t3, x2, t1y = hop(t2, 1), hop(t2, 2), send(held), hop(t1, 1)
        x_got = [x0, x1, x2]
    totals, spot = pack(info, info_x, swap(info + info_x, "gene", 1), zinfo, genes)
    if ring:
        got = swap(totals, "spot", 2)
        theirs, totals = tie(theirs, totals)
        acc_other = fwd("other_mid", [theirs, ty, t1, t2], [(*e_one, 4 * KC, 0)], None, None, None)
        acc_other, got, t2y, t3 = tie(acc_other, got, t2y, t3)
        totals = totals + got
        got = swap(totals, "spot", 1)
        t3y = hop(t2y, 2)
        acc_other, totals = tie(acc_other, totals)
        acc_other = fwd("other_more", [t2y, t3], [(*e_two, KC, 1), (*e_two, KC, 2)], acc_other, None, None)
        acc_other, got, mine = tie(acc_other, got, mine)
        totals = totals + got
        more = swap(totals, "spot", 4)
        own[0] = mine
        left_own = rows_left(where, own, rows, own_pick)
        t1y, t3y, left_own = tie(t1y, t3y, left_own)
        other = [theirs, ty, t1, t1y, t2, t2y, t3, t3y]
        last = ([t1y, t3y], [(*e_two, KC, 0), (*e_two, KC, 3)], acc_other)
    else:
        totals = lax.psum(totals, "spot")
        more = jnp.zeros_like(totals)
        left_own = rows_left(where, own, rows, own_pick)
        last = (other, whole, None)
    left_other = rows_left(where, other, rows, own_pick)
    if ring:
        left_other, more = tie(left_other, more)

    lefts = (left_own, left_other)
    sent, *highs, sums = back_sum(
        where, *last, zinfo, pred_own, (*x_own, *x_got), lefts, totals, more, spot, consts, rows, tile
    )
    got = swap(sent, "gene", 1)
    rest = back_own(where, highs, lefts, sums, zinfo, dens_row, sent, weights, consts[2], rows, tile)
    rest, got = tie(rest, got)
    grad, loss = back_end(where, rest, got, logits, zinfo, sums, consts[3], rows, 2 * tile)
    return loss, predicted, grad


def solution(mesh):
    return jax.shard_map(
        local,
        mesh=mesh,
        in_specs=(P(None, "spot"), P("spot", "gene"), P("spot", "gene"), P(), P("spot"), P("gene")),
        out_specs=(P(), P("spot", "gene"), P("gene", "spot")),
        check_vma=False,
    )
```

```python
import functools
import jax
import jax.numpy as jnp
from jax import lax
from jax.experimental import pallas as pl
from jax.experimental.pallas import tpu as pltpu
from jax.sharding import PartitionSpec as P

NB = 4
XS = 3
XCUT = (0, 16, 21, 32)
EPS = 1e-06
BF = jnp.bfloat16
F32 = jnp.float32
KC = 256
NT = (((1,), (1,)), ((), ()))
TN = (((0,), (0,)), ((), ()))
VMEM_LIMIT = 21 << 20
LARGE_LIMIT = 60 << 20
CHEAP = pl.CostEstimate(flops=1000, bytes_accessed=1000, transcendentals=0)


def split(value):
    high = value.astype(BF)
    return high, (value - high.astype(F32)).astype(BF)


def dot(left, right, dims=(((1,), (0,)), ((), ()))):
    return lax.dot_general(left, right, dims, preferred_element_type=F32)


def call(kernel, name, where, args, specs, out_shape, out_specs, grid, scratch=(), alias=None, limit=VMEM_LIMIT):
    return pl.pallas_call(
        kernel,
        out_shape=out_shape,
        grid_spec=pltpu.PrefetchScalarGridSpec(
            num_scalar_prefetch=1,
            grid=grid,
            in_specs=specs,
            out_specs=out_specs,
            scratch_shapes=list(scratch),
        ),
        input_output_aliases=alias or {},
        compiler_params=pltpu.CompilerParams(
            dimension_semantics=("arbitrary",), vmem_limit_bytes=limit
        ),
        cost_estimate=CHEAP,
        name=name,
    )(where, *args)


def limit_of(depth):
    return VMEM_LIMIT if depth <= 5 * KC else LARGE_LIMIT


def off_chip(value):
    return pltpu.with_memory_space_constraint(value, pltpu.HBM)


def fixed(shape):
    return pl.BlockSpec(shape, lambda i, ix: (0,) * len(shape), pipeline_mode=pl.Buffered(1))


def by_tile(height, tile, row=0, start=0):
    return pl.BlockSpec((height, tile), lambda i, ix: (row, i + start))


def exp_kernel(cents, count, first, last, where, *refs):
    l_refs, w_refs, d_ref, refs = refs[:count], refs[count : 2 * count], refs[2 * count], refs[2 * count + 1 :]
    if not first:
        before_ref, refs = refs[0], refs[1:]
    high_ref, low_ref, info_ref, scal = refs
    step = pl.program_id(0)
    tile = d_ref.shape[1]

    @pl.when(step == 0)
    def _():
        scal[...] = jnp.zeros_like(scal)

    if first:
        total = weighted = jnp.zeros((1, tile), F32)
    else:
        total, weighted = before_ref[0:1, :], before_ref[1:2, :]
    start = 0
    for l_ref, w_ref in zip(l_refs, w_refs):
        for part in range(l_ref.shape[0] // KC):
            rows = slice(part * KC, part * KC + KC)
            value = jnp.exp(l_ref[rows, :])
            high, low = split(value)
            high_ref[start : start + KC, :] = high
            low_ref[start : start + KC, :] = low
            start += KC
            total = total + jnp.sum(value, axis=0, keepdims=True)
            weighted = weighted + jnp.sum(value * w_ref[rows, :], axis=0, keepdims=True)
    if not last:
        info_ref[...] = jnp.concatenate([total, weighted, jnp.zeros((6, tile), F32)], axis=0)
        return
    inv = 1.0 / total
    raw = weighted * inv
    dens = d_ref[...]
    scal[0:1] += dens
    scal[1:2] += raw
    scal[2:3] += dens * (jnp.log(dens) - jnp.log(raw * cents))
    sums = jnp.broadcast_to(jnp.sum(scal[...], axis=1, keepdims=True), (8, tile))
    info_ref[0:1, :] = inv
    info_ref[1:2, :] = raw
    info_ref[2:8, :] = sums[0:6]


def exp_parts(where, keys, deep, logits, weights, density, before, last, tile):
    cents, spots = logits.shape
    count = len(keys)
    specs = [
        pl.BlockSpec((deep, tile), functools.partial(lambda key, i, ix: (key(ix), i), key)) for key in keys
    ]
    specs += [pl.BlockSpec((deep, 1), functools.partial(lambda key, i, ix: (key(ix), 0), key)) for key in keys]
    specs.append(by_tile(1, tile))
    args = [*([off_chip(logits)] * count), *([weights] * count), density]
    if before is not None:
        specs.append(by_tile(8, tile))
        args.append(before)
    rows = deep * count
    return call(
        functools.partial(exp_kernel, float(cents), count, before is None, last),
        "exp_parts",
        where,
        args,
        specs,
        (
            jax.ShapeDtypeStruct((rows, spots), BF),
            jax.ShapeDtypeStruct((rows, spots), BF),
            jax.ShapeDtypeStruct((8, spots), F32),
        ),
        (by_tile(rows, tile), by_tile(rows, tile), by_tile(8, tile)),
        (spots // tile,),
        [pltpu.VMEM((8, tile), F32)],
        limit=limit_of(rows),
    )


def turn_kernel(where, pick_ref, x_ref, *out_refs):
    high, low = split(x_ref[...])
    pick = pick_ref[...]
    value = dot(pick, high, NT) + dot(pick, low, NT)
    start = 0
    for out_ref in out_refs:
        out_ref[...] = value[start : start + out_ref.shape[0]]
        start += out_ref.shape[0]


def heights(genes):
    return [(b - a) * genes // XCUT[-1] for a, b in zip(XCUT, XCUT[1:])]


def turn(where, pick, x, tile):
    spots, genes = x.shape
    return call(
        turn_kernel,
        "turn",
        where,
        [pick, off_chip(x)],
        [fixed((genes, genes)), pl.BlockSpec((tile, genes), lambda i, ix: (i, 0))],
        tuple(jax.ShapeDtypeStruct((height, spots), F32) for height in heights(genes)),
        tuple(by_tile(height, tile) for height in heights(genes)),
        (spots // tile,),
    )


def of_batch(refs, batch, width):
    start, stop, at, pieces = batch * width, (batch + 1) * width, 0, []
    for ref in refs[:XS]:
        height = ref.shape[0]
        low, high = max(start, at), min(stop, at + height)
        if low < high:
            pieces.append(ref[low - at : high - at, :])
        at += height
    return pieces[0] if len(pieces) == 1 else jnp.concatenate(pieces, axis=0)


def load_left(refs, high, low):
    at = 0
    for ref in refs:
        wide = ref.shape[1]
        high[:, at : at + wide], low[:, at : at + wide] = split(ref[...])
        at += wide


def product(high, low, e_high, e_low):
    right = jnp.concatenate([ref[...] for ref in e_high], axis=0)
    value = dot(high[...], right) + dot(low[...], right)
    return value + dot(high[...], jnp.concatenate([ref[...] for ref in e_low], axis=0))


def pred_kernel(blocks, count, first, last, stats, where, *refs):
    s_refs, refs = refs[:blocks], refs[blocks:]
    h_refs, l_refs = refs[:count], refs[count : 2 * count]
    refs = refs[2 * count :]
    if not first:
        acc_ref, refs = refs[0], refs[1:]
    if last:
        zinfo_ref, refs = refs[0], refs[1:]
    if stats:
        x_refs, (out_ref, info_ref, high, low, sums) = refs[:XS], refs[XS:]
    else:
        out_ref, high, low = refs
    step = pl.program_id(0)
    genes, tile = out_ref.shape
    width = genes // NB

    @pl.when(step == 0)
    def _():
        load_left(s_refs, high, low)
        if stats:
            sums[...] = jnp.zeros_like(sums)
            info_ref[...] = jnp.zeros_like(info_ref)

    value = product(high, low, h_refs, l_refs)
    if not first:
        value = value + acc_ref[...]
    if last:
        value = value * zinfo_ref[0:1, :]
    out_ref[...] = value
    if not stats:
        return
    rows = [[], [], []]
    for batch in range(NB):
        at = slice(batch * width, (batch + 1) * width)
        pred, x = value[at], of_batch(x_refs, batch, width)
        for number, term in enumerate((pred * x, pred * pred, x * x)):
            rows[number].append(jnp.sum(term, axis=0, keepdims=True))
            lanes = term[:, :128]
            for group in range(1, tile // 128):
                lanes = lanes + term[:, group * 128 : group * 128 + 128]
            sums[number, at] += lanes
    info_ref[0 : 3 * NB, pl.ds(pl.multiple_of(step * tile, 128), tile)] = jnp.concatenate(
        rows[0] + rows[1] + rows[2], axis=0
    )

    @pl.when(step == pl.num_programs(0) - 1)
    def _():
        for number in range(3):
            info_ref[12:13, number * genes : (number + 1) * genes] = jnp.sum(
                sums[number].T, axis=0, keepdims=True
            )


def pred_part(where, blocks, terms, acc, zinfo, x, tile, name):
    spots = terms[0][0].shape[1]
    genes, deep = blocks[0].shape
    first, last, stats = acc is None, zinfo is not None, x is not None
    kept = stats or not first
    specs = [fixed((genes, deep)) for _ in blocks]
    specs += [by_tile(rows, tile, place) for _, _, rows, place in terms] * 2
    args = [*blocks, *(term[0] for term in terms), *(term[1] for term in terms)]
    alias = {}
    if not first:
        specs.append(by_tile(genes, tile))
        args.append(acc)
    if last:
        specs.append(by_tile(8, tile))
        args.append(zinfo)
    shapes = pltpu.HBM((genes, spots), F32) if kept else jax.ShapeDtypeStruct((genes, spots), F32)
    outs = by_tile(genes, tile)
    scratch = [pltpu.VMEM((genes, deep * len(blocks)), BF)] * 2
    if stats:
        specs += [by_tile(height, tile) for height in heights(genes)]
        args += x
        shapes = (shapes, jax.ShapeDtypeStruct((16, spots), F32))
        outs = (outs, fixed_out((16, spots)))
        scratch.append(pltpu.VMEM((3, genes, 128), F32))
    return call(
        functools.partial(pred_kernel, len(blocks), len(terms), first, last, stats),
        name,
        where,
        args,
        specs,
        shapes,
        outs,
        (spots // tile,),
        scratch,
        alias,
        limit_of(deep * len(blocks)),
    )


def fixed_out(shape):
    return pl.BlockSpec(shape, lambda i, ix: (0,) * len(shape))


def emit_kernel(where, pred_ref, pick_ref, out_ref):
    high, low = split(pred_ref[...].T)
    pick = pick_ref[...]
    out_ref[...] = dot(high, pick) + dot(low, pick)


def emit(where, pred, pick, tile):
    genes, spots = pred.shape
    return call(
        emit_kernel,
        "emit",
        where,
        [off_chip(pred), pick],
        [by_tile(genes, tile), fixed((genes, genes))],
        jax.ShapeDtypeStruct((spots, genes), F32),
        pl.BlockSpec((tile, genes), lambda i, ix: (i, 0)),
        (spots // tile,),
        limit=VMEM_LIMIT,
    )


def cosine(inner, left, right):
    left = left + EPS
    inv = lax.rsqrt(left) * lax.rsqrt(right + EPS)
    cos = inner * inv
    return cos, inv, cos / left


def pack_kernel(mine_ref, theirs_ref, core_ref, z_ref, out_ref, spot_ref):
    genes = out_ref.shape[1] // 2
    totals = (mine_ref[...] + theirs_ref[...]) + core_ref[...]
    spot_ref[...] = totals
    cos, _, _ = cosine(totals[0:NB], totals[NB : 2 * NB], totals[2 * NB : 3 * NB])
    out_ref[...] = jnp.zeros_like(out_ref)
    spots = z_ref.shape[1]
    for number in range(3):
        at = slice(number * genes, (number + 1) * genes)
        out_ref[number : number + 1, 0:genes] = mine_ref[12:13, at]
        out_ref[number : number + 1, genes : 2 * genes] = theirs_ref[12:13, at]
        out_ref[3 + number : 4 + number, 0:128] = z_ref[2 + number : 3 + number, spots - 128 :]
    out_ref[6:7, 0:128] = jnp.broadcast_to(
        jnp.sum(jnp.sum(cos, axis=0, keepdims=True), axis=1, keepdims=True), (1, 128)
    )


def pack(mine, theirs, core, zinfo, genes):
    return pl.pallas_call(
        pack_kernel,
        out_shape=(
            jax.ShapeDtypeStruct((8, 2 * genes), F32),
            jax.ShapeDtypeStruct(mine.shape, F32),
        ),
        compiler_params=pltpu.CompilerParams(vmem_limit_bytes=VMEM_LIMIT),
        cost_estimate=CHEAP,
        name="pack",
    )(mine, theirs, core, zinfo)


def rows_kernel(count, chosen, where, *refs):
    s_refs, (high_ref, low_ref, buffer, sem) = refs[:count], refs[count:]
    rows = high_ref.shape[0] // 2
    pieces = rows // KC
    for slot in range(2 * pieces):
        which = where[1 - slot // pieces]
        piece = slot % pieces
        if chosen is not None:
            for hit, ref in zip(chosen(where, which * pieces + piece), s_refs):

                @pl.when(hit)
                def _(ref=ref):
                    pltpu.make_async_copy(ref, buffer.at[slot], sem.at[slot]).start()

        else:
            at = pl.ds(pl.multiple_of(which * rows + piece * KC, KC), KC)
            pltpu.make_async_copy(s_refs[0].at[:, at], buffer.at[slot], sem.at[slot]).start()
    for slot in range(2 * pieces):
        pltpu.make_async_copy(s_refs[0].at[:, 0:KC], buffer.at[slot], sem.at[slot]).wait()
        at = slice(slot * KC, slot * KC + KC)
        high_ref[at, :], low_ref[at, :] = split(buffer[slot].T)


def rows_left(where, blocks, rows, chosen):
    genes = blocks[0].shape[0]
    shape = jax.ShapeDtypeStruct((2 * rows, genes), BF)
    slots = 2 * rows // KC
    return call(
        functools.partial(rows_kernel, len(blocks), chosen),
        "rows_left",
        where,
        list(blocks),
        [pl.BlockSpec(memory_space=pl.ANY)] * len(blocks),
        (shape, shape),
        (fixed_out((2 * rows, genes)), fixed_out((2 * rows, genes))),
        (1,),
        [pltpu.VMEM((slots, genes, KC), F32), pltpu.SemaphoreType.DMA((slots,))],
        limit=VMEM_LIMIT,
    )


def back_dots(high_refs, low_refs, bhigh, blow, genes):
    value = None
    for part in range(2):
        at = slice(part * genes, (part + 1) * genes)
        one = dot(high_refs[part][...], bhigh[at]) + dot(low_refs[part][...], bhigh[at])
        one = one + dot(high_refs[part][...], blow[at])
        value = one if value is None else value + one
    return value


def back_sum_kernel(blocks, count, first, sizes, where, *refs):
    batch_scale, gene_scale = sizes
    s_refs, h_refs, l_refs = refs[:blocks], refs[blocks : blocks + count], refs[blocks + count : blocks + 2 * count]
    refs = refs[blocks + 2 * count :]
    if not first:
        acc_ref, refs = refs[0], refs[1:]
    z_ref, own_ref, x_refs, refs = refs[0], refs[1], refs[2 : 2 + 2 * XS], refs[2 + 2 * XS :]
    high_refs, low_refs = refs[0:2], refs[2:4]
    totals_ref, more_ref, spot_ref, out_ref, bhigh, blow, sum_ref, coef, other_ref, high, low = refs[4:]
    pred_refs = (own_ref, other_ref)
    genes, tile = own_ref.shape
    rows = high_refs[0].shape[0]
    width = genes // NB

    @pl.when(pl.program_id(0) == 0)
    def _():
        load_left(s_refs, high, low)
        totals = totals_ref[...] + more_ref[...]
        gene_cos, inv_gene, over_gene = cosine(totals[0:1], totals[1:2], totals[2:3])
        coef[0] = jnp.broadcast_to(-gene_scale * inv_gene, (128, 2 * genes)).T
        coef[1] = jnp.broadcast_to(gene_scale * over_gene, (128, 2 * genes)).T
        cos = jnp.broadcast_to(jnp.sum(gene_cos, axis=1, keepdims=True), (1, 128))
        sum_ref[...] = jnp.concatenate([totals[3:7, 0:128], cos, jnp.zeros((3, 128), F32)], axis=0)

    other = product(high, low, h_refs, l_refs)
    if not first:
        other = other + acc_ref[...]
    other_ref[...] = other * z_ref[0:1, :]
    spot = spot_ref[...]
    _, inv_spot, over_spot = cosine(spot[0:NB], spot[NB : 2 * NB], spot[2 * NB : 3 * NB])
    column = jnp.zeros((1, tile), F32)
    for part in range(2):
        for batch in range(NB):
            at = slice(batch * width, (batch + 1) * width)
            here = slice(part * genes + batch * width, part * genes + (batch + 1) * width)
            x_by = jnp.concatenate([coef[0, here]] * (tile // 128), axis=1) - (
                batch_scale * inv_spot[batch : batch + 1]
            )
            p_by = jnp.concatenate([coef[1, here]] * (tile // 128), axis=1) + (
                batch_scale * over_spot[batch : batch + 1]
            )
            pred = pred_refs[part][at, :]
            grad = of_batch(x_refs[part * XS :], batch, width) * x_by + pred * p_by
            bhigh[here], blow[here] = split(grad)
            column = column + jnp.sum(pred * grad, axis=0, keepdims=True)
    out_ref[0:rows] = back_dots(high_refs, low_refs, bhigh, blow, genes)
    out_ref[rows : rows + 1] = column
    out_ref[rows + 1 : rows + 2] = jnp.concatenate([sum_ref[4:5]] * (tile // 128), axis=1)
    out_ref[rows + 2 : rows + 8] = jnp.zeros((6, tile), F32)


def back_sum(where, blocks, terms, acc, zinfo, own, xs, lefts, totals, more, spot, consts, rows, tile):
    genes, spots = own.shape
    deep = blocks[0].shape[1]
    left = pl.BlockSpec((rows, genes), lambda i, ix: (0, 0), pipeline_mode=pl.Buffered(1))
    specs = [fixed((genes, deep)) for _ in blocks]
    specs += [by_tile(height, tile, place) for _, _, height, place in terms] * 2
    args = [*blocks, *(term[0] for term in terms), *(term[1] for term in terms)]
    if acc is not None:
        specs.append(by_tile(genes, tile))
        args.append(off_chip(acc))
    specs += [by_tile(8, tile), by_tile(genes, tile)] + [by_tile(height, tile) for height in heights(genes)] * 2
    specs += [left] * 4 + [fixed((8, 2 * genes))] * 2 + [by_tile(16, tile)]
    args += [zinfo, off_chip(own), *xs, lefts[0][0], lefts[1][0], lefts[0][1], lefts[1][1], totals, more, spot]
    return call(
        functools.partial(back_sum_kernel, len(blocks), len(terms), acc is None, consts[:2]),
        "back_sum",
        where,
        args,
        specs,
        (
            jax.ShapeDtypeStruct((rows + 8, spots), F32),
            jax.ShapeDtypeStruct((2 * genes, spots), BF),
            jax.ShapeDtypeStruct((2 * genes, spots), BF),
            jax.ShapeDtypeStruct((8, 128), F32),
        ),
        (by_tile(rows + 8, tile), by_tile(2 * genes, tile), by_tile(2 * genes, tile), fixed_out((8, 128))),
        (spots // tile,),
        [
            pltpu.VMEM((2, 2 * genes, 128), F32),
            pltpu.VMEM((genes, tile), F32),
            pltpu.VMEM((genes, deep * len(blocks)), BF),
            pltpu.VMEM((genes, deep * len(blocks)), BF),
        ],
        limit=limit_of(deep * len(blocks)),
    )


def back_own_kernel(scale, where, *refs):
    high_refs, low_refs = refs[0:2], refs[2:4]
    bhigh, blow, sum_ref, z_ref, dens_ref, sent_ref, w_ref, out_ref = refs[4:]
    rows, genes = high_refs[0].shape
    value = back_dots(high_refs, low_refs, bhigh, blow, genes)
    raw = z_ref[1:2, :]
    dens, mass = sum_ref[0:1, 0:1], sum_ref[1:2, 0:1]
    grad_raw = scale * (1.0 / mass - dens_ref[...] / (dens * raw))
    out_ref[...] = value + w_ref[...] * grad_raw - (sent_ref[0:1, :] + raw * grad_raw)


def back_own(where, highs, lefts, sums, zinfo, density, sent, weights, scale, rows, tile):
    twice, spots = highs[0].shape
    left = pl.BlockSpec((rows, twice // 2), lambda i, ix: (1, 0), pipeline_mode=pl.Buffered(1))
    specs = [left] * 4 + [by_tile(twice, tile)] * 2
    specs += [fixed((8, 128)), by_tile(8, tile), by_tile(1, tile), by_tile(8, tile, rows // 8)]
    specs.append(pl.BlockSpec((rows, 1), lambda i, ix: (ix[0], 0)))
    args = [lefts[0][0], lefts[1][0], lefts[0][1], lefts[1][1], *highs]
    args += [sums, zinfo, density, off_chip(sent), weights]
    return call(
        functools.partial(back_own_kernel, scale),
        "back_own",
        where,
        args,
        specs,
        jax.ShapeDtypeStruct((rows, spots), F32),
        by_tile(rows, tile),
        (spots // tile,),
        limit=VMEM_LIMIT,
    )


def back_end_kernel(loss_scale, where, mine_ref, got_ref, logit_ref, z_ref, sum_ref, out_ref, loss_ref):
    gene_loss, spot_loss, cents, spots_all = loss_scale
    rows = out_ref.shape[0]
    value = mine_ref[...] + got_ref[0:rows, :] - got_ref[rows : rows + 1, :]
    out_ref[...] = jnp.exp(logit_ref[...]) * z_ref[0:1, :] * value

    @pl.when(pl.program_id(0) == 0)
    def _():
        dens, mass, log_sum, cos = (sum_ref[k : k + 1] for k in range(4))
        gene = (sum_ref[4:5] + got_ref[rows + 1 : rows + 2, 0:128]) * gene_loss
        kl = log_sum / dens + jnp.log(mass * (cents / spots_all)) - jnp.log(dens * (1.0 / spots_all))
        for number, term in enumerate((gene, cos * spot_loss, kl)):
            loss_ref[number] = term[0, 0]


def back_end(where, mine, got, logits, zinfo, sums, loss_scale, rows, tile):
    spots = mine.shape[1]
    return call(
        functools.partial(back_end_kernel, loss_scale),
        "back_end",
        where,
        [mine, got, off_chip(logits), zinfo, sums],
        [
            by_tile(rows, tile),
            by_tile(rows + 8, tile),
            pl.BlockSpec((rows, tile), lambda i, ix: (ix[0], i)),
            by_tile(8, tile),
            fixed((8, 128)),
        ],
        (jax.ShapeDtypeStruct((rows, spots), F32), jax.ShapeDtypeStruct((3,), F32)),
        (by_tile(rows, tile), pl.BlockSpec(memory_space=pltpu.SMEM)),
        (spots // tile,),
        limit=VMEM_LIMIT,
    )


def swap(value, axis, bit):
    return lax.ppermute(value, axis, [(i, i ^ bit) for i in range(lax.axis_size(axis))])


def after(value, *others):
    return lax.optimization_barrier((value, *others))[0]


def tie(*values):
    return lax.optimization_barrier(values)


def local(logits, centroid_expr, spatial, cluster_cells, density, gene_order):
    n_spot = lax.axis_size("spot")
    n_gene = lax.axis_size("gene")
    me = lax.axis_index("spot")
    col = lax.axis_index("gene")
    cents, spots = logits.shape
    genes = spatial.shape[1]
    genes_all = genes * n_gene
    spots_all = spots * n_spot
    rows = cents // n_gene
    scale = float(spots_all * cents)
    consts = (
        scale / (NB * spots_all),
        scale / genes_all,
        scale,
        (-1.0 / genes_all, -1.0 / (NB * spots_all), float(cents), float(spots_all)),
    )
    ring = n_spot == 8 and cents // n_spot == KC
    where = jnp.stack([col, col ^ 1, me]).astype(jnp.int32)
    tile = 512

    order = (gene_order - col * genes).reshape(genes, 1)
    pick = order == lax.broadcasted_iota(jnp.int32, (genes, genes), 1)
    mine = lax.dot_general(
        pick.astype(F32), centroid_expr, NT, precision=lax.Precision.HIGH, preferred_element_type=F32
    )
    pick = pick.astype(BF)
    theirs = swap(mine, "gene", 2)
    weights = cluster_cells.astype(F32)
    weights = (weights / jnp.sum(weights)).reshape(cents, 1)
    dens_row = density.reshape(1, spots)
    fwd = lambda name, blocks, terms, acc, scale_by, x: pred_part(
        where, blocks, terms, acc, scale_by, x, tile, name
    )
    if ring:
        hop = lambda block, bit: swap(block, "spot", bit)
        send = lambda one, *others: swap(after(one, *others), "gene", 2)
        keys = lambda *order: [functools.partial(lambda k, ix: ix[2] ^ k, k) for k in order]
        o1, o2, oy = [hop(mine, bit) for bit in (2, 4, 1)]
        x_own = list(turn(where, pick, spatial, 2 * tile))
        x_own[0], oy = tie(x_own[0], oy)
        x0 = send(x_own[0])
        logits, *x_own = tie(logits, *x_own)
        *e_one, z_one = exp_parts(where, keys(0, 1, 2, 4), KC, logits, weights, dens_row, None, False, 2 * tile)
        theirs, o1, oy, o2, z_one, *x_own = tie(theirs, o1, oy, o2, z_one, *x_own)
        o2y, o3 = hop(o2, 1), hop(o2, 2)
        acc = fwd("own_early", [mine, oy, o1, o2], [(*e_one, 4 * KC, 0)], None, None, None)
        acc, o2y, o3, oy, theirs, z_one, logits = tie(acc, o2y, o3, oy, theirs, z_one, logits)
        o3y, o1y, ty = hop(o2y, 2), hop(o1, 1), hop(theirs, 1)
        *e_two, zinfo = exp_parts(where, keys(3, 5, 6, 7), KC, logits, weights, dens_row, z_one, True, 2 * tile)
        o1y, theirs, zinfo, held = tie(o1y, theirs, zinfo, x_own[1])
        t1, t2, x1 = hop(theirs, 2), hop(theirs, 4), send(held)
        acc, o3y, zinfo = tie(acc, o3y, zinfo)
        pred_own, info = fwd("own_late", [o1y, o2y, o3, o3y], [(*e_two, 4 * KC, 0)], acc, zinfo, x_own)
        own = [mine, oy, o1, o1y, o2, o2y, o3, o3y]
        own_pick = lambda ix, block: [(block ^ ix[2]) == key for key in range(n_spot)]
    else:
        x_own = turn(where, pick, spatial, 2 * tile)
        x_got = [swap(one, "gene", 2) for one in x_own]
        *e_all, zinfo = exp_parts(where, [lambda ix: 0], cents, logits, weights, dens_row, None, True, tile)
        own = [lax.all_gather(mine, "spot", axis=1, tiled=True)]
        other = [lax.all_gather(theirs, "spot", axis=1, tiled=True)]
        whole = [(*e_all, cents, 0)]
        pred_own, info = fwd("own_late", own, whole, None, zinfo, x_own)
        own_pick = None

    info_x = swap(info, "gene", 2)
    predicted = emit(where, pred_own, pick, 2 * tile)
    if ring:
        predicted, info_x, x1, ty, t1, t2, theirs, x0, held = tie(
            predicted, info_x, x1, ty, t1, t2, theirs, x0, x_own[2]
        )
        t2y, t3, x2, t1y = hop(t2, 1), hop(t2, 2), send(held), hop(t1, 1)
        x_got = [x0, x1, x2]
    totals, spot = pack(info, info_x, swap(info + info_x, "gene", 1), zinfo, genes)
    if ring:
        got = swap(totals, "spot", 2)
        theirs, totals = tie(theirs, totals)
        acc_other = fwd("other_mid", [theirs, ty, t1, t2], [(*e_one, 4 * KC, 0)], None, None, None)
        acc_other, got, t2y, t3 = tie(acc_other, got, t2y, t3)
        totals = totals + got
        got = swap(totals, "spot", 1)
        t3y = hop(t2y, 2)
        acc_other, totals = tie(acc_other, totals)
        acc_other = fwd("other_more", [t2y, t3], [(*e_two, KC, 1), (*e_two, KC, 2)], acc_other, None, None)
        acc_other, got, mine = tie(acc_other, got, mine)
        totals = totals + got
        more = swap(totals, "spot", 4)
        own[0] = mine
        left_own = rows_left(where, own, rows, own_pick)
        t1y, t3y, left_own = tie(t1y, t3y, left_own)
        other = [theirs, ty, t1, t1y, t2, t2y, t3, t3y]
        last = ([t1y, t3y], [(*e_two, KC, 0), (*e_two, KC, 3)], acc_other)
    else:
        totals = lax.psum(totals, "spot")
        more = jnp.zeros_like(totals)
        left_own = rows_left(where, own, rows, own_pick)
        last = (other, whole, None)
    left_other = rows_left(where, other, rows, own_pick)
    if ring:
        left_other, more = tie(left_other, more)

    lefts = (left_own, left_other)
    sent, *highs, sums = back_sum(
        where, *last, zinfo, pred_own, (*x_own, *x_got), lefts, totals, more, spot, consts, rows, tile
    )
    got = swap(sent, "gene", 1)
    rest = back_own(where, highs, lefts, sums, zinfo, dens_row, sent, weights, consts[2], rows, tile)
    rest, got = tie(rest, got)
    grad, loss = back_end(where, rest, got, logits, zinfo, sums, consts[3], rows, 2 * tile)
    return loss, predicted, grad


def solution(mesh):
    return jax.shard_map(
        local,
        mesh=mesh,
        in_specs=(P(None, "spot"), P("spot", "gene"), P("spot", "gene"), P(), P("spot"), P("gene")),
        out_specs=(P(), P("spot", "gene"), P("gene", "spot")),
        check_vma=False,
    )
```

```python
import functools
import jax
import jax.numpy as jnp
from jax import lax
from jax.experimental import pallas as pl
from jax.experimental.pallas import tpu as pltpu
from jax.sharding import PartitionSpec as P

NB = 4
XS = 3
XCUT = (0, 16, 21, 32)
EPS = 1e-06
BF = jnp.bfloat16
F32 = jnp.float32
KC = 256
NT = (((1,), (1,)), ((), ()))
TN = (((0,), (0,)), ((), ()))
VMEM_LIMIT = 21 << 20
LARGE_LIMIT = 60 << 20
CHEAP = pl.CostEstimate(flops=1000, bytes_accessed=1000, transcendentals=0)


def split(value):
    high = value.astype(BF)
    return high, (value - high.astype(F32)).astype(BF)


def dot(left, right, dims=(((1,), (0,)), ((), ()))):
    return lax.dot_general(left, right, dims, preferred_element_type=F32)


def call(kernel, name, where, args, specs, out_shape, out_specs, grid, scratch=(), alias=None, limit=VMEM_LIMIT):
    return pl.pallas_call(
        kernel,
        out_shape=out_shape,
        grid_spec=pltpu.PrefetchScalarGridSpec(
            num_scalar_prefetch=1,
            grid=grid,
            in_specs=specs,
            out_specs=out_specs,
            scratch_shapes=list(scratch),
        ),
        input_output_aliases=alias or {},
        compiler_params=pltpu.CompilerParams(
            dimension_semantics=("arbitrary",), vmem_limit_bytes=limit
        ),
        cost_estimate=CHEAP,
        name=name,
    )(where, *args)


def limit_of(depth):
    return VMEM_LIMIT if depth <= 5 * KC else LARGE_LIMIT


def off_chip(value):
    return pltpu.with_memory_space_constraint(value, pltpu.HBM)


def fixed(shape):
    return pl.BlockSpec(shape, lambda i, ix: (0,) * len(shape), pipeline_mode=pl.Buffered(1))


def by_tile(height, tile, row=0, start=0):
    return pl.BlockSpec((height, tile), lambda i, ix: (row, i + start))


def exp_kernel(cents, count, first, last, where, *refs):
    l_refs, w_refs, d_ref, refs = refs[:count], refs[count : 2 * count], refs[2 * count], refs[2 * count + 1 :]
    if not first:
        before_ref, refs = refs[0], refs[1:]
    high_ref, low_ref, info_ref, scal = refs
    step = pl.program_id(0)
    tile = d_ref.shape[1]

    @pl.when(step == 0)
    def _():
        scal[...] = jnp.zeros_like(scal)

    if first:
        total = weighted = jnp.zeros((1, tile), F32)
    else:
        total, weighted = before_ref[0:1, :], before_ref[1:2, :]
    start = 0
    for l_ref, w_ref in zip(l_refs, w_refs):
        for part in range(l_ref.shape[0] // KC):
            rows = slice(part * KC, part * KC + KC)
            value = jnp.exp(l_ref[rows, :])
            high, low = split(value)
            high_ref[start : start + KC, :] = high
            low_ref[start : start + KC, :] = low
            start += KC
            total = total + jnp.sum(value, axis=0, keepdims=True)
            weighted = weighted + jnp.sum(value * w_ref[rows, :], axis=0, keepdims=True)
    if not last:
        info_ref[...] = jnp.concatenate([total, weighted, jnp.zeros((6, tile), F32)], axis=0)
        return
    inv = 1.0 / total
    raw = weighted * inv
    dens = d_ref[...]
    scal[0:1] += dens
    scal[1:2] += raw
    scal[2:3] += dens * (jnp.log(dens) - jnp.log(raw * cents))
    sums = jnp.broadcast_to(jnp.sum(scal[...], axis=1, keepdims=True), (8, tile))
    info_ref[0:1, :] = inv
    info_ref[1:2, :] = raw
    info_ref[2:8, :] = sums[0:6]


def exp_parts(where, keys, deep, logits, weights, density, before, last, tile):
    cents, spots = logits.shape
    count = len(keys)
    specs = [
        pl.BlockSpec((deep, tile), functools.partial(lambda key, i, ix: (key(ix), i), key)) for key in keys
    ]
    specs += [pl.BlockSpec((deep, 1), functools.partial(lambda key, i, ix: (key(ix), 0), key)) for key in keys]
    specs.append(by_tile(1, tile))
    args = [*([off_chip(logits)] * count), *([weights] * count), density]
    if before is not None:
        specs.append(by_tile(8, tile))
        args.append(before)
    rows = deep * count
    return call(
        functools.partial(exp_kernel, float(cents), count, before is None, last),
        "exp_parts",
        where,
        args,
        specs,
        (
            jax.ShapeDtypeStruct((rows, spots), BF),
            jax.ShapeDtypeStruct((rows, spots), BF),
            jax.ShapeDtypeStruct((8, spots), F32),
        ),
        (by_tile(rows, tile), by_tile(rows, tile), by_tile(8, tile)),
        (spots // tile,),
        [pltpu.VMEM((8, tile), F32)],
        limit=limit_of(rows),
    )


def turn_kernel(where, pick_ref, x_ref, *out_refs):
    high, low = split(x_ref[...])
    pick = pick_ref[...]
    value = dot(pick, high, NT) + dot(pick, low, NT)
    start = 0
    for out_ref in out_refs:
        out_ref[...] = value[start : start + out_ref.shape[0]]
        start += out_ref.shape[0]


def heights(genes):
    return [(b - a) * genes // XCUT[-1] for a, b in zip(XCUT, XCUT[1:])]


def turn(where, pick, x, tile):
    spots, genes = x.shape
    return call(
        turn_kernel,
        "turn",
        where,
        [pick, off_chip(x)],
        [fixed((genes, genes)), pl.BlockSpec((tile, genes), lambda i, ix: (i, 0))],
        tuple(jax.ShapeDtypeStruct((height, spots), F32) for height in heights(genes)),
        tuple(by_tile(height, tile) for height in heights(genes)),
        (spots // tile,),
    )


def of_batch(refs, batch, width):
    start, stop, at, pieces = batch * width, (batch + 1) * width, 0, []
    for ref in refs[:XS]:
        height = ref.shape[0]
        low, high = max(start, at), min(stop, at + height)
        if low < high:
            pieces.append(ref[low - at : high - at, :])
        at += height
    return pieces[0] if len(pieces) == 1 else jnp.concatenate(pieces, axis=0)


def load_left(refs, high, low):
    at = 0
    for ref in refs:
        wide = ref.shape[1]
        high[:, at : at + wide], low[:, at : at + wide] = split(ref[...])
        at += wide


def product(high, low, e_high, e_low):
    right = jnp.concatenate([ref[...] for ref in e_high], axis=0)
    value = dot(high[...], right) + dot(low[...], right)
    return value + dot(high[...], jnp.concatenate([ref[...] for ref in e_low], axis=0))


def pred_kernel(blocks, count, first, last, stats, where, *refs):
    s_refs, refs = refs[:blocks], refs[blocks:]
    h_refs, l_refs = refs[:count], refs[count : 2 * count]
    refs = refs[2 * count :]
    if not first:
        acc_ref, refs = refs[0], refs[1:]
    if last:
        zinfo_ref, refs = refs[0], refs[1:]
    if stats:
        x_refs, (out_ref, info_ref, high, low, sums) = refs[:XS], refs[XS:]
    else:
        out_ref, high, low = refs
    step = pl.program_id(0)
    genes, tile = out_ref.shape
    width = genes // NB

    @pl.when(step == 0)
    def _():
        load_left(s_refs, high, low)
        if stats:
            sums[...] = jnp.zeros_like(sums)
            info_ref[...] = jnp.zeros_like(info_ref)

    value = product(high, low, h_refs, l_refs)
    if not first:
        value = value + acc_ref[...]
    if last:
        value = value * zinfo_ref[0:1, :]
    out_ref[...] = value
    if not stats:
        return
    rows = [[], [], []]
    for batch in range(NB):
        at = slice(batch * width, (batch + 1) * width)
        pred, x = value[at], of_batch(x_refs, batch, width)
        for number, term in enumerate((pred * x, pred * pred, x * x)):
            rows[number].append(jnp.sum(term, axis=0, keepdims=True))
            lanes = term[:, :128]
            for group in range(1, tile // 128):
                lanes = lanes + term[:, group * 128 : group * 128 + 128]
            sums[number, at] += lanes
    info_ref[0 : 3 * NB, pl.ds(pl.multiple_of(step * tile, 128), tile)] = jnp.concatenate(
        rows[0] + rows[1] + rows[2], axis=0
    )

    @pl.when(step == pl.num_programs(0) - 1)
    def _():
        for number in range(3):
            info_ref[12:13, number * genes : (number + 1) * genes] = jnp.sum(
                sums[number].T, axis=0, keepdims=True
            )


def pred_part(where, blocks, terms, acc, zinfo, x, tile, name):
    spots = terms[0][0].shape[1]
    genes, deep = blocks[0].shape
    first, last, stats = acc is None, zinfo is not None, x is not None
    kept = stats or not first
    specs = [fixed((genes, deep)) for _ in blocks]
    specs += [by_tile(rows, tile, place) for _, _, rows, place in terms] * 2
    args = [*blocks, *(term[0] for term in terms), *(term[1] for term in terms)]
    alias = {}
    if not first:
        specs.append(by_tile(genes, tile))
        args.append(acc)
    if last:
        specs.append(by_tile(8, tile))
        args.append(zinfo)
    shapes = pltpu.HBM((genes, spots), F32) if kept else jax.ShapeDtypeStruct((genes, spots), F32)
    outs = by_tile(genes, tile)
    scratch = [pltpu.VMEM((genes, deep * len(blocks)), BF)] * 2
    if stats:
        specs += [by_tile(height, tile) for height in heights(genes)]
        args += x
        shapes = (shapes, jax.ShapeDtypeStruct((16, spots), F32))
        outs = (outs, fixed_out((16, spots)))
        scratch.append(pltpu.VMEM((3, genes, 128), F32))
    return call(
        functools.partial(pred_kernel, len(blocks), len(terms), first, last, stats),
        name,
        where,
        args,
        specs,
        shapes,
        outs,
        (spots // tile,),
        scratch,
        alias,
        limit_of(deep * len(blocks)),
    )


def fixed_out(shape):
    return pl.BlockSpec(shape, lambda i, ix: (0,) * len(shape))


def emit_kernel(where, pred_ref, pick_ref, out_ref):
    high, low = split(pred_ref[...].T)
    pick = pick_ref[...]
    out_ref[...] = dot(high, pick) + dot(low, pick)


def emit(where, pred, pick, tile):
    genes, spots = pred.shape
    return call(
        emit_kernel,
        "emit",
        where,
        [off_chip(pred), pick],
        [by_tile(genes, tile), fixed((genes, genes))],
        jax.ShapeDtypeStruct((spots, genes), F32),
        pl.BlockSpec((tile, genes), lambda i, ix: (i, 0)),
        (spots // tile,),
        limit=VMEM_LIMIT,
    )


def cosine(inner, left, right):
    left = left + EPS
    inv = lax.rsqrt(left) * lax.rsqrt(right + EPS)
    cos = inner * inv
    return cos, inv, cos / left


def pack_kernel(mine_ref, theirs_ref, core_ref, z_ref, out_ref, spot_ref):
    genes = out_ref.shape[1] // 2
    totals = (mine_ref[...] + theirs_ref[...]) + core_ref[...]
    spot_ref[...] = totals
    cos, _, _ = cosine(totals[0:NB], totals[NB : 2 * NB], totals[2 * NB : 3 * NB])
    out_ref[...] = jnp.zeros_like(out_ref)
    spots = z_ref.shape[1]
    for number in range(3):
        at = slice(number * genes, (number + 1) * genes)
        out_ref[number : number + 1, 0:genes] = mine_ref[12:13, at]
        out_ref[number : number + 1, genes : 2 * genes] = theirs_ref[12:13, at]
        out_ref[3 + number : 4 + number, 0:128] = z_ref[2 + number : 3 + number, spots - 128 :]
    out_ref[6:7, 0:128] = jnp.broadcast_to(
        jnp.sum(jnp.sum(cos, axis=0, keepdims=True), axis=1, keepdims=True), (1, 128)
    )


def pack(mine, theirs, core, zinfo, genes):
    return pl.pallas_call(
        pack_kernel,
        out_shape=(
            jax.ShapeDtypeStruct((8, 2 * genes), F32),
            jax.ShapeDtypeStruct(mine.shape, F32),
        ),
        compiler_params=pltpu.CompilerParams(vmem_limit_bytes=VMEM_LIMIT),
        cost_estimate=CHEAP,
        name="pack",
    )(mine, theirs, core, zinfo)


def rows_kernel(count, chosen, where, *refs):
    s_refs, (high_ref, low_ref, buffer, sem) = refs[:count], refs[count:]
    rows = high_ref.shape[0] // 2
    pieces = rows // KC
    for slot in range(2 * pieces):
        which = where[1 - slot // pieces]
        piece = slot % pieces
        if chosen is not None:
            for hit, ref in zip(chosen(where, which * pieces + piece), s_refs):

                @pl.when(hit)
                def _(ref=ref):
                    pltpu.make_async_copy(ref, buffer.at[slot], sem.at[slot]).start()

        else:
            at = pl.ds(pl.multiple_of(which * rows + piece * KC, KC), KC)
            pltpu.make_async_copy(s_refs[0].at[:, at], buffer.at[slot], sem.at[slot]).start()
    for slot in range(2 * pieces):
        pltpu.make_async_copy(s_refs[0].at[:, 0:KC], buffer.at[slot], sem.at[slot]).wait()
        at = slice(slot * KC, slot * KC + KC)
        high_ref[at, :], low_ref[at, :] = split(buffer[slot].T)


def rows_left(where, blocks, rows, chosen):
    genes = blocks[0].shape[0]
    shape = jax.ShapeDtypeStruct((2 * rows, genes), BF)
    slots = 2 * rows // KC
    return call(
        functools.partial(rows_kernel, len(blocks), chosen),
        "rows_left",
        where,
        list(blocks),
        [pl.BlockSpec(memory_space=pl.ANY)] * len(blocks),
        (shape, shape),
        (fixed_out((2 * rows, genes)), fixed_out((2 * rows, genes))),
        (1,),
        [pltpu.VMEM((slots, genes, KC), F32), pltpu.SemaphoreType.DMA((slots,))],
        limit=VMEM_LIMIT,
    )


def back_dots(high_refs, low_refs, bhigh, blow, genes):
    value = None
    for part in range(2):
        at = slice(part * genes, (part + 1) * genes)
        one = dot(high_refs[part][...], bhigh[at]) + dot(low_refs[part][...], bhigh[at])
        one = one + dot(high_refs[part][...], blow[at])
        value = one if value is None else value + one
    return value


def back_sum_kernel(blocks, count, first, sizes, where, *refs):
    batch_scale, gene_scale = sizes
    s_refs, h_refs, l_refs = refs[:blocks], refs[blocks : blocks + count], refs[blocks + count : blocks + 2 * count]
    refs = refs[blocks + 2 * count :]
    if not first:
        acc_ref, refs = refs[0], refs[1:]
    z_ref, own_ref, x_refs, refs = refs[0], refs[1], refs[2 : 2 + 2 * XS], refs[2 + 2 * XS :]
    high_refs, low_refs = refs[0:2], refs[2:4]
    totals_ref, more_ref, spot_ref, out_ref, bhigh, blow, sum_ref, coef, other_ref, high, low = refs[4:]
    pred_refs = (own_ref, other_ref)
    genes, tile = own_ref.shape
    rows = high_refs[0].shape[0]
    width = genes // NB

    @pl.when(pl.program_id(0) == 0)
    def _():
        load_left(s_refs, high, low)
        totals = totals_ref[...] + more_ref[...]
        gene_cos, inv_gene, over_gene = cosine(totals[0:1], totals[1:2], totals[2:3])
        coef[0] = jnp.broadcast_to(-gene_scale * inv_gene, (128, 2 * genes)).T
        coef[1] = jnp.broadcast_to(gene_scale * over_gene, (128, 2 * genes)).T
        cos = jnp.broadcast_to(jnp.sum(gene_cos, axis=1, keepdims=True), (1, 128))
        sum_ref[...] = jnp.concatenate([totals[3:7, 0:128], cos, jnp.zeros((3, 128), F32)], axis=0)

    other = product(high, low, h_refs, l_refs)
    if not first:
        other = other + acc_ref[...]
    other_ref[...] = other * z_ref[0:1, :]
    spot = spot_ref[...]
    _, inv_spot, over_spot = cosine(spot[0:NB], spot[NB : 2 * NB], spot[2 * NB : 3 * NB])
    column = jnp.zeros((1, tile), F32)
    for part in range(2):
        for batch in range(NB):
            at = slice(batch * width, (batch + 1) * width)
            here = slice(part * genes + batch * width, part * genes + (batch + 1) * width)
            x_by = jnp.concatenate([coef[0, here]] * (tile // 128), axis=1) - (
                batch_scale * inv_spot[batch : batch + 1]
            )
            p_by = jnp.concatenate([coef[1, here]] * (tile // 128), axis=1) + (
                batch_scale * over_spot[batch : batch + 1]
            )
            pred = pred_refs[part][at, :]
            grad = of_batch(x_refs[part * XS :], batch, width) * x_by + pred * p_by
            bhigh[here], blow[here] = split(grad)
            column = column + jnp.sum(pred * grad, axis=0, keepdims=True)
    out_ref[0:rows] = back_dots(high_refs, low_refs, bhigh, blow, genes)
    out_ref[rows : rows + 1] = column
    out_ref[rows + 1 : rows + 2] = jnp.concatenate([sum_ref[4:5]] * (tile // 128), axis=1)
    out_ref[rows + 2 : rows + 8] = jnp.zeros((6, tile), F32)


def back_sum(where, blocks, terms, acc, zinfo, own, xs, lefts, totals, more, spot, consts, rows, tile):
    genes, spots = own.shape
    deep = blocks[0].shape[1]
    left = pl.BlockSpec((rows, genes), lambda i, ix: (0, 0), pipeline_mode=pl.Buffered(1))
    specs = [fixed((genes, deep)) for _ in blocks]
    specs += [by_tile(height, tile, place) for _, _, height, place in terms] * 2
    args = [*blocks, *(term[0] for term in terms), *(term[1] for term in terms)]
    if acc is not None:
        specs.append(by_tile(genes, tile))
        args.append(off_chip(acc))
    specs += [by_tile(8, tile), by_tile(genes, tile)] + [by_tile(height, tile) for height in heights(genes)] * 2
    specs += [left] * 4 + [fixed((8, 2 * genes))] * 2 + [by_tile(16, tile)]
    args += [zinfo, off_chip(own), *xs, lefts[0][0], lefts[1][0], lefts[0][1], lefts[1][1], totals, more, spot]
    return call(
        functools.partial(back_sum_kernel, len(blocks), len(terms), acc is None, consts[:2]),
        "back_sum",
        where,
        args,
        specs,
        (
            jax.ShapeDtypeStruct((rows + 8, spots), F32),
            jax.ShapeDtypeStruct((2 * genes, spots), BF),
            jax.ShapeDtypeStruct((2 * genes, spots), BF),
            jax.ShapeDtypeStruct((8, 128), F32),
        ),
        (by_tile(rows + 8, tile), by_tile(2 * genes, tile), by_tile(2 * genes, tile), fixed_out((8, 128))),
        (spots // tile,),
        [
            pltpu.VMEM((2, 2 * genes, 128), F32),
            pltpu.VMEM((genes, tile), F32),
            pltpu.VMEM((genes, deep * len(blocks)), BF),
            pltpu.VMEM((genes, deep * len(blocks)), BF),
        ],
        limit=limit_of(deep * len(blocks)),
    )


def back_own_kernel(scale, where, *refs):
    high_refs, low_refs = refs[0:2], refs[2:4]
    bhigh, blow, sum_ref, z_ref, dens_ref, sent_ref, w_ref, out_ref = refs[4:]
    rows, genes = high_refs[0].shape
    value = back_dots(high_refs, low_refs, bhigh, blow, genes)
    raw = z_ref[1:2, :]
    dens, mass = sum_ref[0:1, 0:1], sum_ref[1:2, 0:1]
    grad_raw = scale * (1.0 / mass - dens_ref[...] / (dens * raw))
    out_ref[...] = value + w_ref[...] * grad_raw - (sent_ref[0:1, :] + raw * grad_raw)


def back_own(where, highs, lefts, sums, zinfo, density, sent, weights, scale, rows, tile):
    twice, spots = highs[0].shape
    left = pl.BlockSpec((rows, twice // 2), lambda i, ix: (1, 0), pipeline_mode=pl.Buffered(1))
    specs = [left] * 4 + [by_tile(twice, tile)] * 2
    specs += [fixed((8, 128)), by_tile(8, tile), by_tile(1, tile), by_tile(8, tile, rows // 8)]
    specs.append(pl.BlockSpec((rows, 1), lambda i, ix: (ix[0], 0)))
    args = [lefts[0][0], lefts[1][0], lefts[0][1], lefts[1][1], *highs]
    args += [sums, zinfo, density, off_chip(sent), weights]
    return call(
        functools.partial(back_own_kernel, scale),
        "back_own",
        where,
        args,
        specs,
        jax.ShapeDtypeStruct((rows, spots), F32),
        by_tile(rows, tile),
        (spots // tile,),
        limit=VMEM_LIMIT,
    )


def back_end_kernel(loss_scale, where, mine_ref, got_ref, logit_ref, z_ref, sum_ref, out_ref, loss_ref):
    gene_loss, spot_loss, cents, spots_all = loss_scale
    rows = out_ref.shape[0]
    value = mine_ref[...] + got_ref[0:rows, :] - got_ref[rows : rows + 1, :]
    out_ref[...] = jnp.exp(logit_ref[...]) * z_ref[0:1, :] * value

    @pl.when(pl.program_id(0) == 0)
    def _():
        dens, mass, log_sum, cos = (sum_ref[k : k + 1] for k in range(4))
        gene = (sum_ref[4:5] + got_ref[rows + 1 : rows + 2, 0:128]) * gene_loss
        kl = log_sum / dens + jnp.log(mass * (cents / spots_all)) - jnp.log(dens * (1.0 / spots_all))
        for number, term in enumerate((gene, cos * spot_loss, kl)):
            loss_ref[number] = term[0, 0]


def back_end(where, mine, got, logits, zinfo, sums, loss_scale, rows, tile):
    spots = mine.shape[1]
    return call(
        functools.partial(back_end_kernel, loss_scale),
        "back_end",
        where,
        [mine, got, off_chip(logits), zinfo, sums],
        [
            by_tile(rows, tile),
            by_tile(rows + 8, tile),
            pl.BlockSpec((rows, tile), lambda i, ix: (ix[0], i)),
            by_tile(8, tile),
            fixed((8, 128)),
        ],
        (jax.ShapeDtypeStruct((rows, spots), F32), jax.ShapeDtypeStruct((3,), F32)),
        (by_tile(rows, tile), pl.BlockSpec(memory_space=pltpu.SMEM)),
        (spots // tile,),
        limit=VMEM_LIMIT,
    )


def swap(value, axis, bit):
    return lax.ppermute(value, axis, [(i, i ^ bit) for i in range(lax.axis_size(axis))])


def after(value, *others):
    return lax.optimization_barrier((value, *others))[0]


def tie(*values):
    return lax.optimization_barrier(values)


def local(logits, centroid_expr, spatial, cluster_cells, density, gene_order):
    n_spot = lax.axis_size("spot")
    n_gene = lax.axis_size("gene")
    me = lax.axis_index("spot")
    col = lax.axis_index("gene")
    cents, spots = logits.shape
    genes = spatial.shape[1]
    genes_all = genes * n_gene
    spots_all = spots * n_spot
    rows = cents // n_gene
    scale = float(spots_all * cents)
    consts = (
        scale / (NB * spots_all),
        scale / genes_all,
        scale,
        (-1.0 / genes_all, -1.0 / (NB * spots_all), float(cents), float(spots_all)),
    )
    ring = n_spot == 8 and cents // n_spot == KC
    where = jnp.stack([col, col ^ 1, me]).astype(jnp.int32)
    tile = 512

    order = (gene_order - col * genes).reshape(genes, 1)
    pick = order == lax.broadcasted_iota(jnp.int32, (genes, genes), 1)
    mine = lax.dot_general(
        pick.astype(F32), centroid_expr, NT, precision=lax.Precision.HIGH, preferred_element_type=F32
    )
    pick = pick.astype(BF)
    theirs = swap(mine, "gene", 2)
    weights = cluster_cells.astype(F32)
    weights = (weights / jnp.sum(weights)).reshape(cents, 1)
    dens_row = density.reshape(1, spots)
    fwd = lambda name, blocks, terms, acc, scale_by, x: pred_part(
        where, blocks, terms, acc, scale_by, x, tile, name
    )
    if ring:
        hop = lambda block, bit: swap(block, "spot", bit)
        send = lambda one, *others: swap(after(one, *others), "gene", 2)
        keys = lambda *order: [functools.partial(lambda k, ix: ix[2] ^ k, k) for k in order]
        o1, o2, oy = [hop(mine, bit) for bit in (2, 4, 1)]
        x_own = list(turn(where, pick, spatial, 2 * tile))
        x_own[0], oy = tie(x_own[0], oy)
        x0 = send(x_own[0])
        logits, *x_own = tie(logits, *x_own)
        *e_one, z_one = exp_parts(where, keys(0, 1, 2, 4), KC, logits, weights, dens_row, None, False, 2 * tile)
        theirs, o1, oy, o2, z_one, *x_own = tie(theirs, o1, oy, o2, z_one, *x_own)
        o2y, o3 = hop(o2, 1), hop(o2, 2)
        acc = fwd("own_early", [mine, oy, o1, o2], [(*e_one, 4 * KC, 0)], None, None, None)
        acc, o2y, o3, oy, theirs, z_one, logits = tie(acc, o2y, o3, oy, theirs, z_one, logits)
        o3y, o1y, ty = hop(o2y, 2), hop(o1, 1), hop(theirs, 1)
        *e_two, zinfo = exp_parts(where, keys(3, 5, 6, 7), KC, logits, weights, dens_row, z_one, True, 2 * tile)
        theirs, zinfo, held = tie(theirs, zinfo, x_own[1])
        t1, t2, x1 = hop(theirs, 2), hop(theirs, 4), send(held)
        acc, o3y, o1y, zinfo = tie(acc, o3y, o1y, zinfo)
        pred_own, info = fwd("own_late", [o1y, o2y, o3, o3y], [(*e_two, 4 * KC, 0)], acc, zinfo, x_own)
        own = [mine, oy, o1, o1y, o2, o2y, o3, o3y]
        own_pick = lambda ix, block: [(block ^ ix[2]) == key for key in range(n_spot)]
    else:
        x_own = turn(where, pick, spatial, 2 * tile)
        x_got = [swap(one, "gene", 2) for one in x_own]
        *e_all, zinfo = exp_parts(where, [lambda ix: 0], cents, logits, weights, dens_row, None, True, tile)
        own = [lax.all_gather(mine, "spot", axis=1, tiled=True)]
        other = [lax.all_gather(theirs, "spot", axis=1, tiled=True)]
        whole = [(*e_all, cents, 0)]
        pred_own, info = fwd("own_late", own, whole, None, zinfo, x_own)
        own_pick = None

    info_x = swap(info, "gene", 2)
    predicted = emit(where, pred_own, pick, 2 * tile)
    if ring:
        predicted, info_x, x1, ty, t1, t2, theirs, x0, held = tie(
            predicted, info_x, x1, ty, t1, t2, theirs, x0, x_own[2]
        )
        t2y, t3, x2, t1y = hop(t2, 1), hop(t2, 2), send(held), hop(t1, 1)
        x_got = [x0, x1, x2]
    totals, spot = pack(info, info_x, swap(info + info_x, "gene", 1), zinfo, genes)
    if ring:
        got = swap(totals, "spot", 2)
        theirs, totals = tie(theirs, totals)
        acc_other = fwd("other_mid", [theirs, ty, t1, t2], [(*e_one, 4 * KC, 0)], None, None, None)
        acc_other, got, t2y, t3 = tie(acc_other, got, t2y, t3)
        totals = totals + got
        got = swap(totals, "spot", 1)
        t3y = hop(t2y, 2)
        acc_other, totals = tie(acc_other, totals)
        acc_other = fwd("other_more", [t2y, t3], [(*e_two, KC, 1), (*e_two, KC, 2)], acc_other, None, None)
        acc_other, got, mine = tie(acc_other, got, mine)
        totals = totals + got
        more = swap(totals, "spot", 4)
        own[0] = mine
        left_own = rows_left(where, own, rows, own_pick)
        t1y, t3y, left_own = tie(t1y, t3y, left_own)
        other = [theirs, ty, t1, t1y, t2, t2y, t3, t3y]
        last = ([t1y, t3y], [(*e_two, KC, 0), (*e_two, KC, 3)], acc_other)
    else:
        totals = lax.psum(totals, "spot")
        more = jnp.zeros_like(totals)
        left_own = rows_left(where, own, rows, own_pick)
        last = (other, whole, None)
    left_other = rows_left(where, other, rows, own_pick)
    if ring:
        left_other, more = tie(left_other, more)

    lefts = (left_own, left_other)
    sent, *highs, sums = back_sum(
        where, *last, zinfo, pred_own, (*x_own, *x_got), lefts, totals, more, spot, consts, rows, tile
    )
    got = swap(sent, "gene", 1)
    rest = back_own(where, highs, lefts, sums, zinfo, dens_row, sent, weights, consts[2], rows, tile)
    rest, got = tie(rest, got)
    grad, loss = back_end(where, rest, got, logits, zinfo, sums, consts[3], rows, 2 * tile)
    return loss, predicted, grad


def solution(mesh):
    return jax.shard_map(
        local,
        mesh=mesh,
        in_specs=(P(None, "spot"), P("spot", "gene"), P("spot", "gene"), P(), P("spot"), P("gene")),
        out_specs=(P(), P("spot", "gene"), P("gene", "spot")),
        check_vma=False,
    )
```
